256 devices in a mesh: region: 8 (over z), tile: 32 (over y, x, core).
Axes of the slice: x: 4, y: 4, z: 8, core: 2. Of those that a mesh axis runs over, the one named last changes fastest.
Arguments:
- offsets: float32 [2, 1048576], P(None, ('region', 'tile')), may hold values from 0 to 1
- design: float32 [2, 1048576], P(None, ('region', 'tile')), may hold values from -4 to 4
- target: float32 [1048576], P(('region', 'tile')), may hold values from -6 to 6
- beta_second: float32 [1048576], P(('region', 'tile')), may hold values from -3 to 3
- counts: int32 [4096], P(('region', 'tile')), may hold values from 1 to 256, as said below
- kernel_width: int32 [2, 4096], P(None, ('region', 'tile')), may hold values from 2 to 8
- reach: int32 [2, 4096, 9], P(None, ('region', 'tile')), may hold values 0 or 1
- assignment: int32 [8, 512], P('region', 'tile'), may hold values from 0 to 511, each once within a row
Outputs:
- betas: float32 [2, 1048576], P(None, ('region', 'tile'))
- hats: float32 [2, 1048576], P(None, ('region', 'tile'))
- residual: float32 [1048576], P(('region', 'tile'))
The draws below stay inside these ranges and needn't reach their ends.
Inputs may be any that keep to these rules, and one draw needn't show every extreme that they name: `counts`: some tile holds 256 live records in every draw.
All inputs are finite; a program needn't handle non-finite values. No bound on the sum of `reach` on one device may be relied on, other than what follows from the above.
Results may differ from the reference program's by a relative error of at most 0.0003.
Values sent between devices are 32-bit elements; how exact they have to be, the bound alone decides.
A program may use at most 64 MiB of HBM per device.

```python
import jax
import jax.numpy as jnp
from jax import lax

TILE = 256
TX = 4
NREG = 8
TPR = 512
TY = 128
NTILES = 4096
RECORDS = 1048576


def draw_counts(key, part):
    subkeys = jax.random.split(key, 3)
    upper_draw = jax.random.randint(subkeys[0], (NTILES,), 0, TILE)
    lower_draw = jax.random.randint(subkeys[1], (NTILES,), 0, TILE)
    filled = 1 + upper_draw * lower_draw // TILE
    chosen = jax.random.randint(subkeys[2], (), 0, NTILES)
    return filled.at[chosen].set(TILE).astype(jnp.int32)


def place_ends(drawn, stream_key, least, largest):
    place = [jax.random.randint(jax.random.fold_in(stream_key, axis), (), 0, length) for axis, length in enumerate(drawn.shape)]
    longest = drawn.shape.index(max(drawn.shape))
    beside = place[:longest] + [(place[longest] + 1) % drawn.shape[longest]] + place[longest + 1:]
    return drawn.at[tuple(place)].set(least).at[tuple(beside)].set(largest)


def level_of(rng, dims, pieces, smallest, top_value):
    gain = 1.0
    for axis_at, shards_of in pieces:
        steps = jax.random.uniform(jax.random.fold_in(jax.random.fold_in(rng, 6), axis_at), (shards_of,), jnp.float32, smallest / len(pieces), top_value / len(pieces))
        gain = gain * jnp.repeat(jnp.exp(steps), dims[axis_at] // shards_of).reshape((-1,) + (1,) * (len(dims) - 1 - axis_at))
    return gain


def gaussian(rng, extent, deviation, bound, pieces=(), held_as=jnp.bfloat16):
    values = deviation * jax.random.normal(rng, extent, jnp.float32)
    if pieces:
        values = values * level_of(rng, extent, pieces, -0.22, 0.18)
    return jnp.clip(values, -bound, bound).astype(held_as)


def setup_inputs(seed: int = 0) -> dict:
    arg_keys = jax.random.split(jax.random.key(seed), 9)
    return {
        "offsets": jnp.clip(1.0 * jax.random.uniform(arg_keys[0], (2, RECORDS), jnp.float32) ** level_of(arg_keys[0], (2, RECORDS), ((1, 256),), -0.2, 0.2), 0.0, 1.0),
        "design": gaussian(arg_keys[1], (2, RECORDS), 1.0, 4.0, ((1, 256),), jnp.float32),
        "target": gaussian(arg_keys[2], (RECORDS,), 1.0, 6.0, ((0, 256),), jnp.float32),
        "beta_second": gaussian(arg_keys[3], (RECORDS,), 0.5, 3.0, ((0, 256),), jnp.float32),
        "counts": draw_counts(jax.random.fold_in(arg_keys[8], 71), 0),
        "kernel_width": place_ends(jax.random.randint(arg_keys[5], (2, NTILES), 2, 9), jax.random.fold_in(arg_keys[5], 1), 2, 8).astype(jnp.int32),
        "reach": place_ends((jax.random.randint(arg_keys[6], (2, NTILES, 9), 0, 4) < 3).astype(jnp.int32), jax.random.fold_in(arg_keys[6], 1), 0, 1),
        "assignment": jax.vmap(lambda own: jax.random.permutation(own, TPR))(jax.random.split(arg_keys[7], NREG)).reshape((NREG, TPR)).astype(jnp.int32),
    }


def pick_rows(values, order):
    return values[order]


def extend(grid):
    blank = jnp.zeros_like(grid[:1, :1])
    lower = jnp.concatenate([blank, grid[:-1, TX - 1:]], axis=0)
    upper = jnp.concatenate([grid[1:, :1], blank], axis=0)
    wider = jnp.concatenate([lower, grid, upper], axis=1)
    return jnp.pad(wider, ((0, 0), (0, 0), (1, 1), (0, 0)))


def reference(offsets, design, target, beta_second, counts, kernel_width, reach, assignment):
    layout_shape = (NREG, TPR, TILE)
    column = assignment // TY
    across = assignment % TY
    region_ids = jnp.arange(NREG, dtype=jnp.int32)[:, None]
    places = offsets.reshape(2, NREG, TPR, TILE)
    east = (region_ids * TX + column).astype(jnp.float32)[:, :, None] + places[0]
    north = across.astype(jnp.float32)[:, :, None] + places[1]
    present = (jnp.arange(TILE, dtype=jnp.int32)[None, None, :] < counts.reshape(NREG, TPR)[:, :, None]).astype(jnp.float32)
    cov_one = design[0].reshape(layout_shape)
    cov_two = design[1].reshape(layout_shape)
    observed = target.reshape(layout_shape)
    prior_beta = beta_second.reshape(layout_shape)
    inverse = jnp.argsort(assignment, axis=1).astype(jnp.int32)
    flat_cells = assignment.reshape(-1)

    def layout(values):
        return extend(jax.vmap(pick_rows)(values, inverse).reshape(NREG, TX, TY, TILE))

    base = [layout(east), layout(north), layout(present)]

    def smooth_all(covariate, partial_value, widths, near_mask):
        table = jnp.stack(base + [layout(covariate), layout(partial_value)])
        anchor = jnp.int32(0)

        def per_tile(item):
            number, own_east, own_north, own_cov, own_live, width, mask_row = item
            region_of = number // TPR
            cell = flat_cells[number]
            block = lax.dynamic_slice(table, (anchor, region_of, cell // TY, cell % TY, anchor), (5, 1, 3, 3, TILE)).reshape(5, 9 * TILE)
            centre = jnp.arange(9) == 4
            valid = ((mask_row > 0) | centre).astype(jnp.float32)
            weight_mask = block[2] * jnp.repeat(valid, TILE)
            squared = (own_east[:, None] - block[0][None, :]) ** 2 + (own_north[:, None] - block[1][None, :]) ** 2
            inverse_width = 32.0 / (width.astype(jnp.float32) ** 2)
            kernel = jnp.exp(-squared * inverse_width) * weight_mask[None, :]
            totals = 1.0 + jnp.dot(kernel, block[3] * block[3], precision=lax.Precision.HIGHEST)
            weighted = jnp.dot(kernel, block[3] * block[4], precision=lax.Precision.HIGHEST)
            return own_live * weighted / totals, own_live * own_cov * own_cov / totals

        items = (jnp.arange(NTILES, dtype=jnp.int32), east.reshape(NTILES, TILE), north.reshape(NTILES, TILE),
                 covariate.reshape(NTILES, TILE), present.reshape(NTILES, TILE), widths, near_mask)
        return lax.map(per_tile, items)

    beta_one, hat_one = smooth_all(cov_one, observed - cov_two * prior_beta, kernel_width[0], reach[0])
    beta_one_grid = beta_one.reshape(layout_shape)
    beta_two, hat_two = smooth_all(cov_two, observed - cov_one * beta_one_grid, kernel_width[1], reach[1])
    residual = present * (observed - cov_one * beta_one_grid - cov_two * beta_two.reshape(layout_shape))
    betas = jnp.stack([beta_one.reshape(-1), beta_two.reshape(-1)])
    hats = jnp.stack([hat_one.reshape(-1), hat_two.reshape(-1)])
    return betas, hats, residual.reshape(-1)
```

```python
import functools
import math

import jax
import jax.numpy as jnp
from jax import lax
from jax.experimental import pallas as pl
from jax.experimental.pallas import tpu as pltpu
from jax.sharding import PartitionSpec as P

TX = 4
LANES = 128
PER = 16
NPIECE = 13
KDIM = 32
NREGION = 8
NTILE = 32
F32 = jnp.float32
BF16 = jnp.bfloat16


def split3(x):
    hi = x.astype(BF16).astype(F32)
    rest = x - hi
    mid = rest.astype(BF16).astype(F32)
    low = (rest - mid).astype(BF16).astype(F32)
    return hi, mid, low


def wide_split(x):
    hi, mid, low = split3(x)
    return jnp.concatenate([hi.astype(BF16), mid.astype(BF16), low.astype(BF16)], axis=1)


def join3(x):
    return x[:, :LANES] + x[:, LANES : 2 * LANES] + x[:, 2 * LANES :]


def remote(src, dst, send, recv, region, tile):
    return pltpu.make_async_remote_copy(
        src_ref=src,
        dst_ref=dst,
        send_sem=send,
        recv_sem=recv,
        device_id=(region, tile),
        device_id_type=pl.DeviceIdType.MESH,
    )


def signal(sem, region, tile):
    pl.semaphore_signal(sem, inc=1, device_id=(region, tile), device_id_type=pl.DeviceIdType.MESH)


def each(low, high, step):
    def turn(index, carry):
        step(index)
        return carry

    lax.fori_loop(low, high, turn, 0)


def gather_kernel(
    offs, design, target, prior, meta, data_out, meta_out, cells_out,
    stage, rbuf, msg, recv, send1, recv1, send2, recv2,
):
    region = lax.axis_index("region")
    tile = lax.axis_index("tile")
    group = tile // 16
    piece = lax.rem(tile, 16)
    up = lax.rem(region + 1, NREGION)
    down = lax.rem(region + NREGION - 1, NREGION)

    barrier = pltpu.get_barrier_semaphore()
    each(1, NTILE, lambda o: signal(barrier, region, lax.rem(tile + o, NTILE)))
    each(0, 16, lambda i: signal(barrier, up, group * 16 + i))
    each(0, 16, lambda i: signal(barrier, down, group * 16 + i))

    lane = lax.broadcasted_iota(jnp.int32, (PER, LANES), 1)
    count = meta[0:PER, 0:1]
    for h in range(2):
        present = ((lane + LANES * h).astype(F32) < count).astype(F32)
        east = offs[pl.ds(2 * h, PER, stride=4), :]
        north = offs[pl.ds(2 * h + 1, PER, stride=4), :]
        cov_one = design[pl.ds(2 * h, PER, stride=4), :]
        cov_two = design[pl.ds(2 * h + 1, PER, stride=4), :]
        seen = target[pl.ds(h, PER, stride=2), :]
        before = prior[pl.ds(h, PER, stride=2), :]
        values = (
            east, north, cov_one * present, seen - cov_two * before, cov_two * present, seen,
        )
        for f, value in enumerate(values):
            stage[2 * f + h, 0:PER, :] = value
    stage[12, 0:PER, :] = meta[0:PER, :]
    row_lane = lax.broadcasted_iota(jnp.int32, (8, LANES), 1)
    cell_row = jnp.where(row_lane // PER == lax.rem(tile, 8), meta[PER : PER + 8, :], 0.0)
    for p in range(NPIECE):
        stage[p, PER : PER + 8, :] = cell_row

    pl.semaphore_wait(barrier, NTILE - 1 + 32)

    def to_middle(o):
        other = lax.rem(tile + o, NTILE)
        held = jnp.minimum(lax.rem(other, 16), NPIECE - 1)
        return remote(
            stage.at[held, pl.ds(0, PER + 1)], rbuf.at[tile, pl.ds(0, PER + 1)],
            send1.at[o], recv1.at[tile], region, other,
        )

    each(1, NTILE, lambda o: to_middle(o).start())
    rbuf[tile] = stage[jnp.minimum(piece, NPIECE - 1)]

    def from_source(o):
        other = lax.rem(tile + o, NTILE)
        return remote(
            stage.at[0, pl.ds(0, PER + 1)], rbuf.at[other, pl.ds(0, PER + 1)],
            send1.at[o], recv1.at[other], region, other,
        )

    each(1, NTILE, lambda o: from_source(o).wait_recv())

    cell_rows = [
        jnp.sum(rbuf[8 * b : 8 * b + 8, PER, :], axis=0, keepdims=True) for b in range(4)
    ]
    for b in range(4):
        cells_out[b : b + 1, :] = cell_rows[b]
    cells_out[4:8, :] = jnp.zeros((4, LANES), F32)

    @pl.when(piece < NPIECE)
    def _():
        spread = wide_split(rbuf[:, 0:PER, :].reshape(NTILE * PER, LANES))
        number = lax.broadcasted_iota(jnp.int32, (640, LANES), 0)
        owner = lax.shift_right_logical(number * 205, 13)
        q = number - owner * 40
        first = (group * 16 + owner) * 16
        side = jnp.where(q < 32, q - 24, q - 32)
        base = jnp.where(q < 24, q - 4, (side - 1) * 4 + jnp.where(q < 32, 3, 0))
        open_up = jnp.where(region < NREGION - 1, 1, 0)
        open_down = jnp.where(region > 0, 1, 0)
        beside = jnp.where(side < 6, jnp.where(q < 32, open_up, open_down), 0)
        allowed = jnp.where(q < 24, 1, beside)
        cell = first + base
        wanted = jnp.where(allowed > 0, cell, -1).astype(F32)
        hot = jnp.concatenate(
            [jnp.where(wanted == cell_rows[b], 1.0, 0.0).astype(BF16) for b in range(4)], axis=1
        )
        moved = join3(jnp.dot(hot, spread, preferred_element_type=F32))
        msg[...] = moved.reshape(16, 40, LANES)

    def own_copy(o):
        i = lax.rem(piece + o, 16)
        return remote(
            msg.at[i, pl.ds(0, 24)], recv.at[piece, pl.ds(0, 24)],
            send2.at[0, o], recv2.at[0, piece], region, group * 16 + i,
        )

    def up_copy(i):
        return remote(
            msg.at[i, pl.ds(24, 8)], recv.at[piece, pl.ds(24, 8)],
            send2.at[1, i], recv2.at[1, piece], up, group * 16 + i,
        )

    def down_copy(i):
        return remote(
            msg.at[i, pl.ds(32, 8)], recv.at[piece, pl.ds(32, 8)],
            send2.at[2, i], recv2.at[2, piece], down, group * 16 + i,
        )

    @pl.when(piece < NPIECE)
    def _():
        each(1, 16, lambda o: own_copy(o).start())
        each(0, 16, lambda i: up_copy(i).start())
        each(0, 16, lambda i: down_copy(i).start())
        recv[piece, 0:24, :] = msg[piece, 0:24, :]

    def wait_own(p):
        @pl.when(p != piece)
        def _():
            remote(
                msg.at[0, pl.ds(0, 24)], recv.at[p, pl.ds(0, 24)],
                send2.at[0, 0], recv2.at[0, p], region, group * 16 + p,
            ).wait_recv()

    def wait_sides(p):
        remote(
            msg.at[0, pl.ds(24, 8)], recv.at[p, pl.ds(24, 8)],
            send2.at[1, 0], recv2.at[1, p], down, group * 16 + p,
        ).wait_recv()
        remote(
            msg.at[0, pl.ds(32, 8)], recv.at[p, pl.ds(32, 8)],
            send2.at[2, 0], recv2.at[2, p], up, group * 16 + p,
        ).wait_recv()

    each(0, NPIECE, wait_own)
    each(0, NPIECE, wait_sides)
    for p in range(12):
        data_out[p] = recv[p]
    meta_out[...] = recv[12].astype(jnp.int32)

    each(1, NTILE, lambda o: to_middle(o).wait_send())

    @pl.when(piece < NPIECE)
    def _():
        each(1, 16, lambda o: own_copy(o).wait_send())
        each(0, 16, lambda i: up_copy(i).wait_send())
        each(0, 16, lambda i: down_copy(i).wait_send())


def smooth_kernel(which, data, meta, counts, *refs):
    if which == 0:
        beta_out, hat_out, pull_out, left, right, cross, square, pull, turned = refs
    else:
        grid, beta_out, hat_out, left, right, cross, square, pull, turned = refs
    slot = lax.broadcasted_iota(jnp.int32, (40, LANES), 0)
    col = jnp.where(slot < 24, lax.rem(slot, 4) + 1, jnp.where(slot < 32, 0, 5))
    row = jnp.where(slot < 24, slot // 4, jnp.where(slot < 32, slot - 24, slot - 32))
    col = col.astype(F32) - 3.0
    row = row.astype(F32) - 3.0
    width = meta[4:20, 1 + which : 2 + which].astype(F32)
    rate = jnp.broadcast_to((32.0 * math.log2(math.e)) / (width * width), (PER, LANES))
    rates = split3(rate)
    pairs = ((0, 0), (0, 1), (1, 0), (1, 1), (0, 2), (2, 0))
    zero40 = jnp.zeros((40, LANES), F32)
    zero16 = jnp.zeros((PER, LANES), F32)
    for h in range(2):
        x = data[h] + col
        y = data[2 + h] + row
        far = -(x * x + y * y)
        own_x, own_y, own_far = x[4:20], y[4:20], far[4:20]
        lefts = (split3(2.0 * rate * own_x), split3(2.0 * rate * own_y), rates)
        rights = (split3(x), split3(y), split3(far))
        k = 0
        for one, two in zip(lefts, rights):
            for a, b in pairs:
                left[h, pl.ds(k, PER, stride=KDIM), :] = one[a]
                cross[h, pl.ds(k, 40, stride=KDIM), :] = two[b]
                k += 1
        for part in split3(rate * own_far):
            left[h, pl.ds(k, PER, stride=KDIM), :] = part
            cross[h, pl.ds(k, 40, stride=KDIM), :] = zero40 + 1.0
            k += 1
        while k < KDIM:
            left[h, pl.ds(k, PER, stride=KDIM), :] = zero16
            cross[h, pl.ds(k, 40, stride=KDIM), :] = zero40
            k += 1
        cov = data[4 + 4 * which + h]
        square[h] = cov * cov
        if which == 0:
            pull[h] = cov * data[6 + h]
        else:
            pull[h] = grid[h]

    def pack(t):
        for h in range(2):
            right[h, t] = cross[h, pl.ds(pl.multiple_of(t * KDIM, KDIM), KDIM), :].astype(BF16)

    each(0, 40, pack)

    def turn(i):
        for h in range(2):
            rows = left[h, pl.ds(pl.multiple_of(i * KDIM, KDIM), KDIM), :]
            turned[h, i] = jnp.transpose(rows).astype(BF16)

    each(0, PER, turn)

    ones = jnp.ones((8, LANES), F32)
    sums = functools.partial(
        lax.dot_general, dimension_numbers=(((1,), (1,)), ((), ())),
        precision=lax.Precision.HIGHEST, preferred_element_type=F32,
    )
    lane = lax.broadcasted_iota(jnp.int32, (1, LANES), 1)

    def one_tile(i):
        down = i // 4 + 1
        over = lax.rem(i, 4) + 1
        places, keeps = [], []
        for e in range(9):
            c = over + (e // 3 - 1)
            r = down + (e % 3 - 1)
            places.append(jnp.where(c == 0, 24 + r, jnp.where(c == 5, 32 + r, r * 4 + c - 1)))
            if e == 4:
                keeps.append(None)
            else:
                keeps.append(jnp.where(counts[4 + i, 3 + 9 * which + e] > 0, 1.0, 0.0))
        count = counts[4 + i, 0]
        for h in range(2):
            points = turned[h, i]
            weight_sum = jnp.zeros((LANES, LANES), F32)
            pull_sum = jnp.zeros((LANES, LANES), F32)
            for e in range(9):
                t = places[e]
                for g in range(2):
                    weight = jnp.exp2(jnp.dot(points, right[g, t], preferred_element_type=F32))
                    heavy = square[g, pl.ds(t, 1), :]
                    drawn = pull[g, pl.ds(t, 1), :]
                    if keeps[e] is not None:
                        heavy = heavy * keeps[e]
                        drawn = drawn * keeps[e]
                    weight_sum += weight * heavy
                    pull_sum += weight * drawn
            total = 1.0 + sums(ones, weight_sum)[0:1]
            drawn = sums(ones, pull_sum)[0:1]
            live = (lane + LANES * h < count).astype(F32)
            beta = live * drawn / total
            beta_out[h, pl.ds(i, 1), :] = beta
            hat_out[h, pl.ds(i, 1), :] = live * square[h, pl.ds(4 + i, 1), :] / total
            if which == 0:
                seen = data[10 + h, pl.ds(4 + i, 1), :]
                cov_one = data[4 + h, pl.ds(4 + i, 1), :]
                cov_two = data[8 + h, pl.ds(4 + i, 1), :]
                pull_out[h, pl.ds(i, 1), :] = cov_two * (seen - cov_one * beta)

    each(0, PER, one_tile)


def halo_kernel(own, grid_out, recv, send, land):
    region = lax.axis_index("region")
    tile = lax.axis_index("tile")
    steps = [(a, b) for a in (-1, 0, 1) for b in (-1, 0, 1) if (a, b) != (0, 0)]

    def place(a, b):
        return lax.rem(region + a + NREGION, NREGION), lax.rem(tile + b + NTILE, NTILE)

    barrier = pltpu.get_barrier_semaphore()
    for a, b in steps:
        signal(barrier, *place(a, b))
    pl.semaphore_wait(barrier, 8)
    copies = []
    for k, (a, b) in enumerate(steps):
        copies.append(remote(own, recv.at[7 - k], send.at[k], land.at[7 - k], *place(a, b)))
    for copy in copies:
        copy.start()
    for copy in copies:
        copy.wait_recv()
    fits = {-1: region > 0, 0: None, 1: region < NREGION - 1}
    fits_row = {-1: tile > 0, 0: None, 1: tile < NTILE - 1}
    at = {step: k for k, step in enumerate(steps)}

    def take(h, a, b, low, high):
        rows = recv[at[(a, b)], h, low:high, :]
        for fit in (fits[a], fits_row[b]):
            if fit is not None:
                rows = jnp.where(fit, rows, 0.0)
        return rows

    for h in range(2):
        grid_out[h, 4:20, :] = own[h]
        grid_out[h, 0:4, :] = take(h, 0, -1, 12, 16)
        grid_out[h, 20:24, :] = take(h, 0, 1, 0, 4)
        for a, edge, first in ((-1, 3, 24), (1, 0, 32)):
            grid_out[h, first : first + 1, :] = take(h, a, -1, 12 + edge, 13 + edge)
            for r in range(4):
                grid_out[h, first + 1 + r : first + 2 + r, :] = take(h, a, 0, 4 * r + edge, 4 * r + edge + 1)
            grid_out[h, first + 5 : first + 6, :] = take(h, a, 1, edge, edge + 1)
            grid_out[h, first + 6 : first + 8, :] = jnp.zeros((2, LANES), F32)
    for copy in copies:
        copy.wait_send()


def return_kernel(
    beta_one, hat_one, beta_two, hat_two, cells, design, target, meta, betas, hats, residual,
    stage, rbuf, msg, recv, send1, recv1, send2, recv2,
):
    region = lax.axis_index("region")
    tile = lax.axis_index("tile")
    group = tile // 8
    piece = lax.rem(tile, 8)
    barrier = pltpu.get_barrier_semaphore()
    each(1, NTILE, lambda o: signal(barrier, region, lax.rem(tile + o, NTILE)))
    for f, ref in enumerate((beta_one, hat_one, beta_two, hat_two)):
        for h in range(2):
            stage[2 * f + h] = ref[h]
    pl.semaphore_wait(barrier, NTILE - 1)

    def to_middle(o):
        other = lax.rem(tile + o, NTILE)
        return remote(
            stage.at[lax.rem(other, 8)], rbuf.at[tile], send1.at[o], recv1.at[tile], region, other
        )

    each(1, NTILE, lambda o: to_middle(o).start())
    rbuf[tile] = stage[piece]

    row = cells[pl.ds(group, 1), :]
    column = jnp.transpose(jnp.broadcast_to(row, (LANES, LANES)))
    lane = lax.broadcasted_iota(jnp.int32, (LANES, LANES), 1)
    hot = jnp.concatenate(
        [
            jnp.where((lane + LANES * b).astype(F32) == column, 1.0, 0.0).astype(BF16)
            for b in range(4)
        ],
        axis=1,
    )

    def from_source(o):
        other = lax.rem(tile + o, NTILE)
        return remote(stage.at[0], rbuf.at[other], send1.at[o], recv1.at[other], region, other)

    each(1, NTILE, lambda o: from_source(o).wait_recv())
    spread = wide_split(rbuf[...].reshape(NTILE * PER, LANES))
    msg[...] = join3(jnp.dot(hot, spread, preferred_element_type=F32)).reshape(8, PER, LANES)

    def home_copy(o):
        i = lax.rem(piece + o, 8)
        return remote(
            msg.at[i], recv.at[piece], send2.at[o], recv2.at[piece], region, group * 8 + i
        )

    each(1, 8, lambda o: home_copy(o).start())
    recv[piece] = msg[piece]

    def from_middle(o):
        p = lax.rem(piece + o, 8)
        return remote(msg.at[0], recv.at[p], send2.at[o], recv2.at[p], region, group * 8 + p)

    each(1, 8, lambda o: from_middle(o).wait_recv())
    wide = lax.broadcasted_iota(jnp.int32, (PER, LANES), 1)
    count = meta[0:PER, 0:1]
    for h in range(2):
        present = ((wide + LANES * h).astype(F32) < count).astype(F32)
        one, two = recv[h], recv[4 + h]
        cov_one = design[pl.ds(2 * h, PER, stride=4), :]
        cov_two = design[pl.ds(2 * h + 1, PER, stride=4), :]
        seen = target[pl.ds(h, PER, stride=2), :]
        betas[pl.ds(2 * h, PER, stride=4), :] = one
        betas[pl.ds(2 * h + 1, PER, stride=4), :] = two
        hats[pl.ds(2 * h, PER, stride=4), :] = recv[2 + h]
        hats[pl.ds(2 * h + 1, PER, stride=4), :] = recv[6 + h]
        residual[pl.ds(h, PER, stride=2), :] = present * (seen - cov_one * one - cov_two * two)
    each(1, NTILE, lambda o: to_middle(o).wait_send())
    each(1, 8, lambda o: home_copy(o).wait_send())


VM = pl.BlockSpec(memory_space=pltpu.VMEM)
SM = pl.BlockSpec(memory_space=pltpu.SMEM)
DMA = pltpu.SemaphoreType.DMA


def shape(*dims, dtype=F32):
    return jax.ShapeDtypeStruct(dims, dtype)


def smooth(which, data, meta, *extra):
    outs = [shape(2, PER, LANES)] * (3 if which == 0 else 2)
    return pl.pallas_call(
        functools.partial(smooth_kernel, which),
        out_shape=outs,
        in_specs=[VM, VM, SM] + [VM] * len(extra),
        out_specs=[VM] * len(outs),
        scratch_shapes=[
            pltpu.VMEM((2, PER * KDIM, LANES), F32),
            pltpu.VMEM((2, 40, KDIM, LANES), BF16),
            pltpu.VMEM((2, 40 * KDIM, LANES), F32),
            pltpu.VMEM((2, 40, LANES), F32),
            pltpu.VMEM((2, 40, LANES), F32),
            pltpu.VMEM((2, PER, LANES, KDIM), BF16),
        ],
        name="smooth_one" if which == 0 else "smooth_two",
    )(data, meta, meta, *extra)


def body(offsets, design, target, beta_second, counts, kernel_width, reach, assignment):
    def rows(pair):
        return pair.reshape(2, NTILE, LANES).transpose(1, 0, 2).reshape(2 * NTILE, LANES)

    offs, design = rows(offsets), rows(design)
    target = target.reshape(NTILE, LANES)
    prior = beta_second.reshape(NTILE, LANES)
    cell = assignment[0]
    order = (cell % 128) * TX + cell // 128
    notes = jnp.concatenate([counts[:, None], kernel_width.T, reach[0], reach[1]], axis=1)
    meta = jnp.concatenate(
        [
            jnp.pad(notes, ((0, 0), (0, LANES - 21))),
            jnp.broadcast_to(jnp.tile(order, 8)[None], (8, LANES)),
        ],
        axis=0,
    ).astype(F32)
    data, own_meta, cells = pl.pallas_call(
        gather_kernel,
        out_shape=[shape(12, 40, LANES), shape(40, LANES, dtype=jnp.int32), shape(8, LANES)],
        in_specs=[VM] * 5,
        out_specs=[VM] * 3,
        scratch_shapes=[
            pltpu.VMEM((NPIECE, 24, LANES), F32),
            pltpu.VMEM((NTILE, 24, LANES), F32),
            pltpu.VMEM((16, 40, LANES), F32),
            pltpu.VMEM((NPIECE, 40, LANES), F32),
            DMA((NTILE,)),
            DMA((NTILE,)),
            DMA((3, 16)),
            DMA((3, 16)),
        ],
        compiler_params=pltpu.CompilerParams(collective_id=0, has_side_effects=True),
        name="to_owners",
    )(offs, design, target, prior, meta)
    beta_one, hat_one, pull = smooth(0, data, own_meta)
    grid = pl.pallas_call(
        halo_kernel,
        out_shape=shape(2, 40, LANES),
        in_specs=[VM],
        out_specs=VM,
        scratch_shapes=[pltpu.VMEM((8, 2, PER, LANES), F32), DMA((8,)), DMA((8,))],
        compiler_params=pltpu.CompilerParams(collective_id=1, has_side_effects=True),
        name="edges",
    )(pull)
    beta_two, hat_two = smooth(1, data, own_meta, grid)
    betas, hats, residual = pl.pallas_call(
        return_kernel,
        out_shape=[shape(64, LANES), shape(64, LANES), shape(NTILE, LANES)],
        in_specs=[VM] * 8,
        out_specs=[VM] * 3,
        scratch_shapes=[
            pltpu.VMEM((8, PER, LANES), F32),
            pltpu.VMEM((NTILE, PER, LANES), F32),
            pltpu.VMEM((8, PER, LANES), F32),
            pltpu.VMEM((8, PER, LANES), F32),
            DMA((NTILE,)),
            DMA((NTILE,)),
            DMA((8,)),
            DMA((8,)),
        ],
        compiler_params=pltpu.CompilerParams(collective_id=2, has_side_effects=True),
        name="to_slots",
    )(beta_one, hat_one, beta_two, hat_two, cells, design, target, meta)

    def flat(pair):
        return pair.reshape(NTILE, 2, LANES).transpose(1, 0, 2).reshape(2, NTILE * LANES)

    return flat(betas), flat(hats), residual.reshape(-1)


def solution(mesh):
    split = ("region", "tile")
    in_specs = (
        P(None, split), P(None, split), P(split), P(split), P(split), P(None, split),
        P(None, split, None), P("region", "tile"),
    )
    out_specs = (P(None, split), P(None, split), P(split))
    return jax.shard_map(body, mesh=mesh, in_specs=in_specs, out_specs=out_specs, check_vma=False)
```

```python
import functools
import math

import jax
import jax.numpy as jnp
from jax import lax
from jax.experimental import pallas as pl
from jax.experimental.pallas import tpu as pltpu
from jax.sharding import PartitionSpec as P

TX = 4
LANES = 128
PER = 16
NPIECE = 13
CHUNK = 64
NREGION = 8
NTILE = 32
F32 = jnp.float32
BF16 = jnp.bfloat16


def split3(x):
    hi = x.astype(BF16).astype(F32)
    rest = x - hi
    mid = rest.astype(BF16).astype(F32)
    low = (rest - mid).astype(BF16).astype(F32)
    return hi, mid, low


def wide_split(x):
    hi, mid, low = split3(x)
    return jnp.concatenate([hi.astype(BF16), mid.astype(BF16), low.astype(BF16)], axis=1)


def join3(x):
    return x[:, :LANES] + x[:, LANES : 2 * LANES] + x[:, 2 * LANES :]


def remote(src, dst, send, recv, region, tile):
    return pltpu.make_async_remote_copy(
        src_ref=src,
        dst_ref=dst,
        send_sem=send,
        recv_sem=recv,
        device_id=(region, tile),
        device_id_type=pl.DeviceIdType.MESH,
    )


def signal(sem, region, tile):
    pl.semaphore_signal(sem, inc=1, device_id=(region, tile), device_id_type=pl.DeviceIdType.MESH)


def each(low, high, step):
    def turn(index, carry):
        step(index)
        return carry

    lax.fori_loop(low, high, turn, 0)


def walk(tile):
    turned = (tile // 8) * 8 + 6 - lax.rem(tile, 8) + 2 * lax.rem(tile, 2)
    return jnp.where(lax.rem(tile // 8, 2) == 1, turned, tile)


def gather_kernel(
    offsets_in, design_in, target_in, prior_in, counts_in, width_in, reach_in, cells_in,
    data_out, width_out, list_out, cells_out, home_out,
    offs, design, target, prior, counts, widths, reach, cells, notes, rows_of,
    stage, rbuf, msg, recv, load, send1, recv1, send2, recv2,
):
    region = lax.axis_index("region")
    tile = lax.axis_index("tile")
    group = tile // 16
    piece = lax.rem(tile, 16)
    up = lax.rem(region + 1, NREGION)
    down = lax.rem(region + NREGION - 1, NREGION)

    barrier = pltpu.get_barrier_semaphore()
    each(1, NTILE, lambda o: signal(barrier, region, lax.rem(tile + o, NTILE)))
    each(0, 16, lambda i: signal(barrier, up, group * 16 + i))
    each(0, 16, lambda i: signal(barrier, down, group * 16 + i))

    loads = [
        pltpu.make_async_copy(source, place, load.at[k])
        for k, (source, place) in enumerate(
            (
                (counts_in, counts), (width_in, widths), (reach_in, reach), (cells_in, cells),
                (offsets_in, offs), (design_in, design), (target_in, target), (prior_in, prior),
            )
        )
    ]
    for copy in loads:
        copy.start()
    notes[...] = jnp.zeros((32, LANES), F32)
    stage[12] = jnp.zeros((24, LANES), F32)
    rows_of[...] = jnp.zeros((48, LANES), F32)
    for copy in loads[:4]:
        copy.wait()
    notes[0:1, 0:PER] = counts[...].astype(F32)
    notes[1:3, 0:PER] = widths[...].astype(F32)
    for e in range(9):
        for w in range(2):
            at = 3 + 9 * w + e
            notes[at : at + 1, 0:PER] = reach[e, w : w + 1, :].astype(F32)
    turned = jnp.transpose(notes[...])[0:PER]
    stage[12, 0:PER, 0:32] = turned
    cell = cells[...]
    order = (lax.bitwise_and(cell, 127) * TX + lax.shift_right_logical(cell, 7)).astype(F32)
    for k in range(8):
        notes[24:25, PER * k : PER * k + PER] = order
    row_lane = lax.broadcasted_iota(jnp.int32, (8, LANES), 1)
    cell_row = jnp.where(
        lax.shift_right_logical(row_lane, 4) == lax.rem(tile, 8),
        jnp.broadcast_to(notes[24:25, :], (8, LANES)), 0.0,
    )
    for p in range(NPIECE):
        stage[p, PER : PER + 8, :] = cell_row
    for copy in loads[4:]:
        copy.wait()
    lane = lax.broadcasted_iota(jnp.int32, (PER, LANES), 1)
    count = turned[:, 0:1]
    for t in range(PER):
        for h in range(2):
            span = slice(LANES * (2 * t + h), LANES * (2 * t + h + 1))
            for f in range(2):
                stage[2 * f + h, t : t + 1, :] = offs[f : f + 1, span]
                stage[4 + 4 * f + h, t : t + 1, :] = design[f : f + 1, span]
    for h in range(2):
        present = ((lane + LANES * h).astype(F32) < count).astype(F32)
        cov_one = stage[4 + h, 0:PER, :] * present
        cov_two = stage[8 + h, 0:PER, :]
        seen = target[pl.ds(h, PER, stride=2), :]
        before = prior[pl.ds(h, PER, stride=2), :]
        stage[4 + h, 0:PER, :] = cov_one
        stage[6 + h, 0:PER, :] = seen - cov_two * before
        cov_two = cov_two * present
        stage[8 + h, 0:PER, :] = cov_two
        stage[10 + h, 0:PER, :] = seen
        home_out[h] = cov_one
        home_out[2 + h] = cov_two
        home_out[4 + h] = seen * present

    pl.semaphore_wait(barrier, NTILE - 1 + 32)

    def to_middle(o):
        other = lax.rem(tile + o, NTILE)
        held = jnp.minimum(lax.rem(other, 16), NPIECE - 1)
        return remote(
            stage.at[held, pl.ds(0, PER + 1)], rbuf.at[tile, pl.ds(0, PER + 1)],
            send1.at[o], recv1.at[tile], region, other,
        )

    each(1, NTILE, lambda o: to_middle(o).start())
    rbuf[tile] = stage[jnp.minimum(piece, NPIECE - 1)]

    def from_source(o):
        other = lax.rem(tile + o, NTILE)
        return remote(
            stage.at[0, pl.ds(0, PER + 1)], rbuf.at[other, pl.ds(0, PER + 1)],
            send1.at[o], recv1.at[other], region, other,
        )

    each(1, NTILE, lambda o: from_source(o).wait_recv())

    cell_rows = [
        jnp.sum(rbuf[8 * b : 8 * b + 8, PER, :], axis=0, keepdims=True) for b in range(4)
    ]
    for b in range(4):
        cells_out[b : b + 1, :] = cell_rows[b]
    cells_out[4:8, :] = jnp.zeros((4, LANES), F32)

    @pl.when(piece < NPIECE)
    def _():
        spread = wide_split(rbuf[:, 0:PER, :].reshape(NTILE * PER, LANES))
        number = lax.broadcasted_iota(jnp.int32, (640, LANES), 0)
        owner = lax.shift_right_logical(number * 205, 13)
        q = number - owner * 40
        turned_owner = 14 - lax.bitwise_and(owner, 7) + 2 * lax.bitwise_and(owner, 1)
        first = (group * 16 + jnp.where(owner < 8, owner, turned_owner)) * 16
        side = jnp.where(q < 32, q - 24, q - 32)
        base = jnp.where(q < 24, q - 4, (side - 1) * 4 + jnp.where(q < 32, 3, 0))
        open_up = jnp.where(region < NREGION - 1, 1, 0)
        open_down = jnp.where(region > 0, 1, 0)
        beside = jnp.where(side < 6, jnp.where(q < 32, open_up, open_down), 0)
        allowed = jnp.where(q < 24, 1, beside)
        cell = first + base
        wanted = jnp.where(allowed > 0, cell, -1).astype(F32)
        hot = jnp.concatenate(
            [jnp.where(wanted == cell_rows[b], 1.0, 0.0).astype(BF16) for b in range(4)], axis=1
        )
        moved = join3(jnp.dot(hot, spread, preferred_element_type=F32))
        msg[...] = moved.reshape(16, 40, LANES)

    def own_copy(o):
        i = lax.rem(piece + o, 16)
        return remote(
            msg.at[i, pl.ds(0, 24)], recv.at[piece, pl.ds(0, 24)],
            send2.at[0, o], recv2.at[0, piece], region, group * 16 + i,
        )

    def up_copy(i):
        return remote(
            msg.at[i, pl.ds(24, 8)], recv.at[piece, pl.ds(24, 8)],
            send2.at[1, i], recv2.at[1, piece], up, group * 16 + i,
        )

    def down_copy(i):
        return remote(
            msg.at[i, pl.ds(32, 8)], recv.at[piece, pl.ds(32, 8)],
            send2.at[2, i], recv2.at[2, piece], down, group * 16 + i,
        )

    @pl.when(piece < NPIECE)
    def _():
        each(1, 16, lambda o: own_copy(o).start())
        each(0, 16, lambda i: up_copy(i).start())
        each(0, 16, lambda i: down_copy(i).start())
        recv[piece, 0:24, :] = msg[piece, 0:24, :]

    def wait_own(p):
        @pl.when(p != piece)
        def _():
            remote(
                msg.at[0, pl.ds(0, 24)], recv.at[p, pl.ds(0, 24)],
                send2.at[0, 0], recv2.at[0, p], region, group * 16 + p,
            ).wait_recv()

    def wait_sides(p):
        remote(
            msg.at[0, pl.ds(24, 8)], recv.at[p, pl.ds(24, 8)],
            send2.at[1, 0], recv2.at[1, p], down, group * 16 + p,
        ).wait_recv()
        remote(
            msg.at[0, pl.ds(32, 8)], recv.at[p, pl.ds(32, 8)],
            send2.at[2, 0], recv2.at[2, p], up, group * 16 + p,
        ).wait_recv()

    each(0, NPIECE, wait_own)
    each(0, NPIECE, wait_sides)
    for p in range(12):
        data_out[p] = recv[p]
    width_out[...] = recv[12, 4:20, :]
    for r in range(6):
        rows_of[8 * r : 8 * r + 1, :] = recv[12, 24 + r : 25 + r, :]
        rows_of[8 * r + 1 : 8 * r + 5, :] = recv[12, 4 * r : 4 * r + 4, :]
        rows_of[8 * r + 5 : 8 * r + 6, :] = recv[12, 32 + r : 33 + r, :]

    def spread_lane(r, at):
        return jnp.broadcast_to(rows_of[8 * r : 8 * r + 8, at : at + 1], (8, LANES))

    lanes = lax.broadcasted_iota(jnp.int32, (8, LANES), 1)
    lanes_f = lanes.astype(F32)
    over = lax.broadcasted_iota(jnp.int32, (8, LANES), 0)
    filled = [spread_lane(r, 0) for r in range(6)]
    near = [
        [filled[r] if a == 1 else pltpu.roll(filled[r], (1 - a) % 8, 0) for a in range(3)]
        for r in range(6)
    ]
    for w in range(2):
        for r in range(1, 5):
            many = jnp.zeros((8, LANES), F32)
            todo = jnp.zeros((8, LANES), F32)
            for e in range(9):
                beside, beyond = e // 3, r + e % 3 - 1
                there = near[beyond][beside]
                keep = None if e == 4 else spread_lane(r, 3 + 9 * w + e)
                c = over + (beside - 1)
                t = jnp.where(c == 0, 24 + beyond, jnp.where(c == 5, 32 + beyond, beyond * 4 + c - 1))
                at = (8 * t).astype(F32)
                for h in range(2):
                    flag = jnp.where(there > LANES * h, 1.0 if keep is None else keep, 0.0)
                    todo = todo + jnp.where(many == lanes_f, flag * (at + 320.0 * h), 0.0)
                    many = many + flag
            chunks = lax.shift_right_logical(filled[r].astype(jnp.int32) + CHUNK - 1, CHUNK.bit_length() - 1)
            value = jnp.where(lanes == 24, many, todo).astype(jnp.int32)
            value = jnp.where(lanes == 25, chunks, value)
            value = jnp.where(lanes == 26, filled[r].astype(jnp.int32), value)
            list_out[w, 8 * r - 8 : 8 * r, :] = value

    each(1, NTILE, lambda o: to_middle(o).wait_send())

    @pl.when(piece < NPIECE)
    def _():
        each(1, 16, lambda o: own_copy(o).wait_send())
        each(0, 16, lambda i: up_copy(i).wait_send())
        each(0, 16, lambda i: down_copy(i).wait_send())


def smooth_kernel(which, data, widths, lists, *refs):
    if which == 0:
        beta_out, hat_out, pull_out, *scratch = refs
    else:
        grid, beta_out, hat_out, *scratch = refs
    cand, square, fade, rates, fan, weight_sums, pull_sums, tall_of = scratch
    base = 32.0 * math.log2(math.e)
    width = widths[:, 1 + which : 2 + which]
    rate = jnp.broadcast_to(base / (width * width), (PER, LANES))
    rates[...] = -rate
    slot = lax.broadcasted_iota(jnp.int32, (40, LANES), 0)
    col = jnp.where(slot < 24, lax.rem(slot, 4) + 1, jnp.where(slot < 32, 0, 5)).astype(F32)
    row = jnp.where(
        slot < 24, slot // 4, jnp.where(slot < 32, slot - 24, slot - 32)
    ).astype(F32)

    def line(i):
        return lax.shift_right_logical(i, 2) * 8 + lax.bitwise_and(i, 3) + 1

    total = jnp.int32(0)
    for i in range(PER):
        at = 8 * (i // 4) + i % 4 + 1
        total = total + lists[which, at, 24] * lists[which, at, 25]

    columns = []
    for h in range(2):
        x = data[h] - 0.5
        y = data[2 + h] - 0.5
        cov = data[4 + 4 * which + h]
        squared = cov * cov
        square[h] = squared[4:20]
        pull = cov * data[6 + h] if which == 0 else grid[h]
        for k, field in enumerate((x + col, y + row, squared, pull)):
            cand[pl.ds(320 * h + k, 40, stride=8), :] = field
        own_x, own_y = x[4:20], y[4:20]
        fade[h] = jnp.exp2(-rate * (own_x * own_x + own_y * own_y))
        for source in (2.0 * rate * own_x, 2.0 * rate * own_y):
            columns.append(jnp.transpose(jnp.concatenate(split3(source), axis=0)).astype(BF16))
    columns = jnp.concatenate(columns, axis=0)
    which_row = lax.bitwise_and(lax.broadcasted_iota(jnp.int32, (3 * PER, LANES), 0), PER - 1)
    for i in range(PER):
        pick = jnp.where(which_row == i, 1.0, 0.0).astype(BF16)
        fan[i] = jnp.dot(columns, pick, preferred_element_type=F32)

    def item(n, carry):
        i, k, j, old_i, old_k, old_at, keep, power, weight_sum, pull_sum = carry
        weight = jnp.exp2(power)
        heavy = cand[pl.ds(old_at + 2, 1), :]
        drawn = cand[pl.ds(old_at + 3, 1), :]
        weight_sum = weight_sum * keep + weight * heavy
        pull_sum = pull_sum * keep + weight * drawn
        old = pl.ds(pl.multiple_of(old_k * CHUNK, CHUNK), CHUNK)
        weight_sums[old_i, old, :] = weight_sum
        pull_sums[old_i, old, :] = pull_sum

        here = line(i)
        at = lists[which, here, j]
        x = cand[pl.ds(at, 1), :] - (lax.bitwise_and(i, 3) + 1).astype(F32)
        y = cand[pl.ds(at + 1, 1), :] - (lax.shift_right_logical(i, 2) + 1).astype(F32)
        far = (x * x + y * y) * rates[pl.ds(i, 1), :]
        first = lax.shift_right_logical(k, 1) * 256 + lax.bitwise_and(k, 1) * CHUNK
        u = fan[i, pl.ds(pl.multiple_of(first, CHUNK), CHUNK), :]
        v = fan[i, pl.ds(pl.multiple_of(first + LANES, CHUNK), CHUNK), :]
        power = u * x + (v * y + far)
        keep = jnp.where(j == 0, 0.0, 1.0)
        last = j + 1 == lists[which, here, 24]
        end = last & (k + 1 == lists[which, here, 25])
        next_j = jnp.where(last, 0, j + 1)
        next_k = jnp.where(end, 0, jnp.where(last, k + 1, k))
        next_i = jnp.minimum(jnp.where(end, i + 1, i), PER - 1)
        return next_i, next_k, next_j, i, k, at, keep, power, weight_sum, pull_sum

    zero = fan[0, 0:CHUNK, :] * 0.0
    start = jnp.int32(0)
    lax.fori_loop(
        0, total + 1, item,
        (start, start, start, start, start, start, jnp.float32(0), zero, zero, zero),
    )

    ones = jnp.ones((8, LANES), BF16)
    lane = lax.broadcasted_iota(jnp.int32, (1, LANES), 1)

    def row_sum(values):
        high = values.astype(BF16)
        low = (values - high.astype(F32)).astype(BF16)
        both = jnp.concatenate([high, low], axis=0)
        sums = lax.dot_general(ones, both, (((1,), (1,)), ((), ())), preferred_element_type=F32)
        return sums[0:1, :LANES] + sums[0:1, LANES:]

    def finish(i, h):
        half = pl.ds(LANES * h, LANES)
        factor = fade[h, pl.ds(i, 1), :]
        total = 1.0 + factor * row_sum(weight_sums[i, half, :])
        drawn = factor * row_sum(pull_sums[i, half, :])
        live = lane + LANES * h < lists[which, line(i) if h else 8 * (i // 4) + i % 4 + 1, 26]
        beta = jnp.where(live, drawn / total, 0.0)
        beta_out[h, pl.ds(i, 1), :] = beta
        hat_out[h, pl.ds(i, 1), :] = jnp.where(live, square[h, pl.ds(i, 1), :] / total, 0.0)
        if which == 0:
            seen = data[10 + h, pl.ds(4 + i, 1), :]
            cov_one = data[4 + h, pl.ds(4 + i, 1), :]
            cov_two = data[8 + h, pl.ds(4 + i, 1), :]
            pull_out[h, pl.ds(i, 1), :] = cov_two * (seen - cov_one * beta)

    beta_out[1] = jnp.zeros((PER, LANES), F32)
    hat_out[1] = jnp.zeros((PER, LANES), F32)
    if which == 0:
        pull_out[1] = jnp.zeros((PER, LANES), F32)
    tall = jnp.int32(0)
    for i in range(PER):
        finish(i, 0)
        tall_of[tall] = i
        tall = tall + jnp.where(lists[which, 8 * (i // 4) + i % 4 + 1, 26] > LANES, 1, 0)

    def finish_some(g):
        for k in range(4):
            finish(tall_of[jnp.minimum(g * 4 + k, tall - 1)], 1)

    each(0, lax.shift_right_logical(tall + 3, 2), finish_some)


def halo_kernel(own, grid_out, recv, send, land):
    region = lax.axis_index("region")
    tile = lax.axis_index("tile")
    steps = [(a, b) for a in (-1, 0, 1) for b in (-1, 0, 1) if (a, b) != (0, 0)]

    owner = walk(tile)

    def place(a, b):
        return lax.rem(region + a + NREGION, NREGION), walk(lax.rem(owner + b + NTILE, NTILE))

    barrier = pltpu.get_barrier_semaphore()
    for a, b in steps:
        signal(barrier, *place(a, b))
    pl.semaphore_wait(barrier, 8)
    copies = []
    for k, (a, b) in enumerate(steps):
        copies.append(remote(own, recv.at[7 - k], send.at[k], land.at[7 - k], *place(a, b)))
    for copy in copies:
        copy.start()
    for copy in copies:
        copy.wait_recv()
    fits = {-1: region > 0, 0: None, 1: region < NREGION - 1}
    fits_row = {-1: owner > 0, 0: None, 1: owner < NTILE - 1}
    at = {step: k for k, step in enumerate(steps)}

    def take(h, a, b, low, high):
        rows = recv[at[(a, b)], h, low:high, :]
        for fit in (fits[a], fits_row[b]):
            if fit is not None:
                rows = jnp.where(fit, rows, 0.0)
        return rows

    for h in range(2):
        grid_out[h, 4:20, :] = own[h]
        grid_out[h, 0:4, :] = take(h, 0, -1, 12, 16)
        grid_out[h, 20:24, :] = take(h, 0, 1, 0, 4)
        for a, edge, first in ((-1, 3, 24), (1, 0, 32)):
            grid_out[h, first : first + 1, :] = take(h, a, -1, 12 + edge, 13 + edge)
            for r in range(4):
                grid_out[h, first + 1 + r : first + 2 + r, :] = take(h, a, 0, 4 * r + edge, 4 * r + edge + 1)
            grid_out[h, first + 5 : first + 6, :] = take(h, a, 1, edge, edge + 1)
            grid_out[h, first + 6 : first + 8, :] = jnp.zeros((2, LANES), F32)
    for copy in copies:
        copy.wait_send()


def return_kernel(
    beta_one, hat_one, beta_two, hat_two, cells, home, betas, hats, residual,
    stage, rbuf, msg, recv, send1, recv1, send2, recv2,
):
    region = lax.axis_index("region")
    tile = lax.axis_index("tile")
    group = tile // 8
    piece = lax.rem(tile, 8)
    barrier = pltpu.get_barrier_semaphore()
    each(1, NTILE, lambda o: signal(barrier, region, lax.rem(tile + o, NTILE)))
    for f, ref in enumerate((beta_one, hat_one, beta_two, hat_two)):
        for h in range(2):
            stage[2 * f + h] = ref[h]
    pl.semaphore_wait(barrier, NTILE - 1)

    def to_middle(o):
        other = lax.rem(tile + o, NTILE)
        return remote(
            stage.at[lax.rem(other, 8)], rbuf.at[tile], send1.at[o], recv1.at[tile], region, other
        )

    each(1, NTILE, lambda o: to_middle(o).start())
    rbuf[tile] = stage[piece]

    row = cells[pl.ds(group, 1), :]
    column = jnp.transpose(jnp.broadcast_to(row, (LANES, LANES)))
    lane = lax.broadcasted_iota(jnp.int32, (LANES, LANES), 1)
    hots = []
    for b in range(4):
        of = lax.shift_right_logical(lane, 4)
        if b % 2 == 1:
            of = 6 - of + 2 * lax.bitwise_and(of, 1)
        here = LANES * b + of * PER + lax.bitwise_and(lane, PER - 1)
        hots.append(jnp.where(here.astype(F32) == column, 1.0, 0.0).astype(BF16))
    hot = jnp.concatenate(hots, axis=1)

    def from_source(o):
        other = lax.rem(tile + o, NTILE)
        return remote(stage.at[0], rbuf.at[other], send1.at[o], recv1.at[other], region, other)

    each(1, NTILE, lambda o: from_source(o).wait_recv())
    spread = wide_split(rbuf[...].reshape(NTILE * PER, LANES))
    msg[...] = join3(jnp.dot(hot, spread, preferred_element_type=F32)).reshape(8, PER, LANES)

    def home_copy(o):
        i = lax.rem(piece + o, 8)
        return remote(
            msg.at[i], recv.at[piece], send2.at[o], recv2.at[piece], region, group * 8 + i
        )

    each(1, 8, lambda o: home_copy(o).start())
    recv[piece] = msg[piece]

    def from_middle(o):
        p = lax.rem(piece + o, 8)
        return remote(msg.at[0], recv.at[p], send2.at[o], recv2.at[p], region, group * 8 + p)

    each(1, 8, lambda o: from_middle(o).wait_recv())
    for h in range(2):
        left = home[4 + h] - home[h] * recv[h] - home[2 + h] * recv[4 + h]
        residual[pl.ds(h, PER, stride=2), :] = left
        for t in range(PER):
            span = slice(LANES * (2 * t + h), LANES * (2 * t + h + 1))
            for f in range(2):
                betas[f : f + 1, span] = recv[4 * f + h, t : t + 1, :]
                hats[f : f + 1, span] = recv[2 + 4 * f + h, t : t + 1, :]
    each(1, NTILE, lambda o: to_middle(o).wait_send())
    each(1, 8, lambda o: home_copy(o).wait_send())


def store_kernel(betas, hats, residual, betas_out, hats_out, residual_out, done):
    pairs = ((betas, betas_out), (hats, hats_out), (residual, residual_out))
    copies = [pltpu.make_async_copy(a, b, done.at[k]) for k, (a, b) in enumerate(pairs)]
    for copy in copies:
        copy.start()
    for copy in copies:
        copy.wait()


VM = pl.BlockSpec(memory_space=pltpu.VMEM)
SM = pl.BlockSpec(memory_space=pltpu.SMEM)
HB = pl.BlockSpec(memory_space=pltpu.HBM)
DMA = pltpu.SemaphoreType.DMA


def shape(*dims, dtype=F32):
    return jax.ShapeDtypeStruct(dims, dtype)


def smooth(which, data, widths, lists, *extra):
    outs = [shape(2, PER, LANES)] * (3 if which == 0 else 2)
    return pl.pallas_call(
        functools.partial(smooth_kernel, which),
        out_shape=outs,
        in_specs=[VM, VM, SM] + [VM] * len(extra),
        out_specs=[VM] * len(outs),
        scratch_shapes=[
            pltpu.VMEM((640, LANES), F32),
            pltpu.VMEM((2, PER, LANES), F32),
            pltpu.VMEM((2, PER, LANES), F32),
            pltpu.VMEM((PER, LANES), F32),
            pltpu.VMEM((PER, 4 * LANES, LANES), F32),
            pltpu.VMEM((PER, 2 * LANES, LANES), F32),
            pltpu.VMEM((PER, 2 * LANES, LANES), F32),
            pltpu.SMEM((32,), jnp.int32),
        ],
        compiler_params=pltpu.CompilerParams(vmem_limit_bytes=16 << 20),
        name="smooth_one" if which == 0 else "smooth_two",
    )(data, widths, lists, *extra)


def body(offsets, design, target, beta_second, counts, kernel_width, reach, assignment):
    data, widths, lists, cells, home = pl.pallas_call(
        gather_kernel,
        out_shape=[
            shape(12, 40, LANES), shape(PER, LANES), shape(2, 32, LANES, dtype=jnp.int32),
            shape(8, LANES), shape(6, PER, LANES),
        ],
        in_specs=[HB] * 8,
        out_specs=[VM] * 5,
        scratch_shapes=[
            pltpu.VMEM((2, NTILE * LANES), F32),
            pltpu.VMEM((2, NTILE * LANES), F32),
            pltpu.VMEM((NTILE, LANES), F32),
            pltpu.VMEM((NTILE, LANES), F32),
            pltpu.VMEM((1, PER), jnp.int32),
            pltpu.VMEM((2, PER), jnp.int32),
            pltpu.VMEM((9, 2, PER), jnp.int32),
            pltpu.VMEM((1, PER), jnp.int32),
            pltpu.VMEM((32, LANES), F32),
            pltpu.VMEM((48, LANES), F32),
            pltpu.VMEM((NPIECE, 24, LANES), F32),
            pltpu.VMEM((NTILE, 24, LANES), F32),
            pltpu.VMEM((16, 40, LANES), F32),
            pltpu.VMEM((NPIECE, 40, LANES), F32),
            DMA((8,)),
            DMA((NTILE,)),
            DMA((NTILE,)),
            DMA((3, 16)),
            DMA((3, 16)),
        ],
        compiler_params=pltpu.CompilerParams(collective_id=0, has_side_effects=True, vmem_limit_bytes=8 << 20),
        name="to_owners",
    )(
        *(
            pltpu.with_memory_space_constraint(value, pltpu.HBM)
            for value in (
                offsets, design, target.reshape(NTILE, LANES), beta_second.reshape(NTILE, LANES),
                counts.reshape(1, PER), kernel_width, reach.transpose(2, 0, 1), assignment,
            )
        )
    )
    beta_one, hat_one, pull = smooth(0, data, widths, lists)
    grid = pl.pallas_call(
        halo_kernel,
        out_shape=shape(2, 40, LANES),
        in_specs=[VM],
        out_specs=VM,
        scratch_shapes=[pltpu.VMEM((8, 2, PER, LANES), F32), DMA((8,)), DMA((8,))],
        compiler_params=pltpu.CompilerParams(collective_id=1, has_side_effects=True, vmem_limit_bytes=8 << 20),
        name="edges",
    )(pull)
    beta_two, hat_two = smooth(1, data, widths, lists, grid)
    betas, hats, residual = pl.pallas_call(
        return_kernel,
        out_shape=[shape(2, NTILE * LANES), shape(2, NTILE * LANES), shape(NTILE, LANES)],
        in_specs=[VM] * 6,
        out_specs=[VM] * 3,
        scratch_shapes=[
            pltpu.VMEM((8, PER, LANES), F32),
            pltpu.VMEM((NTILE, PER, LANES), F32),
            pltpu.VMEM((8, PER, LANES), F32),
            pltpu.VMEM((8, PER, LANES), F32),
            DMA((NTILE,)),
            DMA((NTILE,)),
            DMA((8,)),
            DMA((8,)),
        ],
        compiler_params=pltpu.CompilerParams(collective_id=2, has_side_effects=True, vmem_limit_bytes=8 << 20),
        name="to_slots",
    )(beta_one, hat_one, beta_two, hat_two, cells, home)
    betas, hats, residual = pl.pallas_call(
        store_kernel,
        out_shape=[shape(2, NTILE * LANES), shape(2, NTILE * LANES), shape(NTILE, LANES)],
        in_specs=[VM] * 3,
        out_specs=[HB] * 3,
        scratch_shapes=[DMA((3,))],
        compiler_params=pltpu.CompilerParams(vmem_limit_bytes=8 << 20),
        name="store",
    )(betas, hats, residual)
    return betas, hats, residual.reshape(-1)


def solution(mesh):
    split = ("region", "tile")
    in_specs = (
        P(None, split), P(None, split), P(split), P(split), P(split), P(None, split),
        P(None, split, None), P("region", "tile"),
    )
    out_specs = (P(None, split), P(None, split), P(split))
    return jax.shard_map(body, mesh=mesh, in_specs=in_specs, out_specs=out_specs, check_vma=False)
```

```python
import functools
import math

import jax
import jax.numpy as jnp
from jax import lax
from jax.experimental import pallas as pl
from jax.experimental.pallas import tpu as pltpu
from jax.sharding import PartitionSpec as P

TX = 4
LANES = 128
PER = 16
NPIECE = 13
CHUNK = 64
NREGION = 8
NTILE = 32
F32 = jnp.float32
BF16 = jnp.bfloat16


def split3(x):
    hi = x.astype(BF16).astype(F32)
    rest = x - hi
    mid = rest.astype(BF16).astype(F32)
    low = (rest - mid).astype(BF16).astype(F32)
    return hi, mid, low


def wide_split(x):
    hi, mid, low = split3(x)
    return jnp.concatenate([hi.astype(BF16), mid.astype(BF16), low.astype(BF16)], axis=1)


def join3(x):
    return x[:, :LANES] + x[:, LANES : 2 * LANES] + x[:, 2 * LANES :]


def remote(src, dst, send, recv, region, tile):
    return pltpu.make_async_remote_copy(
        src_ref=src,
        dst_ref=dst,
        send_sem=send,
        recv_sem=recv,
        device_id=(region, tile),
        device_id_type=pl.DeviceIdType.MESH,
    )


def signal(sem, region, tile):
    pl.semaphore_signal(sem, inc=1, device_id=(region, tile), device_id_type=pl.DeviceIdType.MESH)


def each(low, high, step):
    def turn(index, carry):
        step(index)
        return carry

    lax.fori_loop(low, high, turn, 0)


def walk(tile):
    turned = (tile // 8) * 8 + 6 - lax.rem(tile, 8) + 2 * lax.rem(tile, 2)
    return jnp.where(lax.rem(tile // 8, 2) == 1, turned, tile)


def gather_kernel(
    offsets_in, design_in, target_in, prior_in, counts_in, width_in, reach_in, cells_in,
    data_out, width_out, list_out, cells_out, home_out,
    offs, design, target, prior, counts, widths, reach, cells, notes, rows_of,
    wanted, stage, rbuf, msg, recv, load, send1, recv1, send2, recv2,
):
    region = lax.axis_index("region")
    tile = lax.axis_index("tile")
    group = tile // 16
    piece = lax.rem(tile, 16)
    up = lax.rem(region + 1, NREGION)
    down = lax.rem(region + NREGION - 1, NREGION)

    barrier = pltpu.get_barrier_semaphore()
    each(1, NTILE, lambda o: signal(barrier, region, lax.rem(tile + o, NTILE)))
    each(0, 16, lambda i: signal(barrier, up, group * 16 + i))
    each(0, 16, lambda i: signal(barrier, down, group * 16 + i))

    loads = [
        pltpu.make_async_copy(source, place, load.at[k])
        for k, (source, place) in enumerate(
            (
                (counts_in, counts), (width_in, widths), (reach_in, reach), (cells_in, cells),
                (offsets_in, offs), (design_in, design), (target_in, target), (prior_in, prior),
            )
        )
    ]
    for copy in loads:
        copy.start()
    notes[...] = jnp.zeros((32, LANES), F32)
    stage[12] = jnp.zeros((24, LANES), F32)
    rows_of[...] = jnp.zeros((48, LANES), F32)
    for copy in loads[:4]:
        copy.wait()
    notes[0:1, 0:PER] = counts[...].astype(F32)
    notes[1:3, 0:PER] = widths[...].astype(F32)
    for e in range(9):
        for w in range(2):
            at = 3 + 9 * w + e
            notes[at : at + 1, 0:PER] = reach[e, w : w + 1, :].astype(F32)
    turned = jnp.transpose(notes[...])[0:PER]
    stage[12, 0:PER, 0:32] = turned
    cell = cells[...]
    order = (lax.bitwise_and(cell, 127) * TX + lax.shift_right_logical(cell, 7)).astype(F32)
    for k in range(8):
        notes[24:25, PER * k : PER * k + PER] = order
    row_lane = lax.broadcasted_iota(jnp.int32, (8, LANES), 1)
    cell_row = jnp.where(
        lax.shift_right_logical(row_lane, 4) == lax.rem(tile, 8),
        jnp.broadcast_to(notes[24:25, :], (8, LANES)), 0.0,
    )
    for p in range(NPIECE):
        stage[p, PER : PER + 8, :] = cell_row
    for copy in loads[4:]:
        copy.wait()
    lane = lax.broadcasted_iota(jnp.int32, (PER, LANES), 1)
    count = turned[:, 0:1]
    for t in range(PER):
        for h in range(2):
            span = slice(LANES * (2 * t + h), LANES * (2 * t + h + 1))
            for f in range(2):
                stage[2 * f + h, t : t + 1, :] = offs[f : f + 1, span]
                stage[4 + 4 * f + h, t : t + 1, :] = design[f : f + 1, span]
    for h in range(2):
        present = ((lane + LANES * h).astype(F32) < count).astype(F32)
        cov_one = stage[4 + h, 0:PER, :] * present
        cov_two = stage[8 + h, 0:PER, :]
        seen = target[pl.ds(h, PER, stride=2), :]
        before = prior[pl.ds(h, PER, stride=2), :]
        stage[4 + h, 0:PER, :] = cov_one
        stage[6 + h, 0:PER, :] = seen - cov_two * before
        cov_two = cov_two * present
        stage[8 + h, 0:PER, :] = cov_two
        stage[10 + h, 0:PER, :] = seen
        home_out[h] = cov_one
        home_out[2 + h] = cov_two
        home_out[4 + h] = seen * present

    pl.semaphore_wait(barrier, NTILE - 1 + 32)

    def to_middle(o):
        other = lax.rem(tile + o, NTILE)
        held = jnp.minimum(lax.rem(other, 16), NPIECE - 1)
        return remote(
            stage.at[held, pl.ds(0, PER + 1)], rbuf.at[tile, pl.ds(0, PER + 1)],
            send1.at[o], recv1.at[tile], region, other,
        )

    each(1, NTILE, lambda o: to_middle(o).start())
    rbuf[tile] = stage[jnp.minimum(piece, NPIECE - 1)]

    number = lax.broadcasted_iota(jnp.int32, (640, LANES), 0)
    owner = lax.shift_right_logical(number * 205, 13)
    q = number - owner * 40
    turned_owner = 14 - lax.bitwise_and(owner, 7) + 2 * lax.bitwise_and(owner, 1)
    first = (group * 16 + jnp.where(owner < 8, owner, turned_owner)) * 16
    side = jnp.where(q < 32, q - 24, q - 32)
    base = jnp.where(q < 24, q - 4, (side - 1) * 4 + jnp.where(q < 32, 3, 0))
    open_up = jnp.where(region < NREGION - 1, 1, 0)
    open_down = jnp.where(region > 0, 1, 0)
    beside = jnp.where(side < 6, jnp.where(q < 32, open_up, open_down), 0)
    allowed = jnp.where(q < 24, 1, beside)
    cell = first + base
    wanted[...] = jnp.where(allowed > 0, cell, -1).astype(F32)

    def from_source(o):
        other = lax.rem(tile + o, NTILE)
        return remote(
            stage.at[0, pl.ds(0, PER + 1)], rbuf.at[other, pl.ds(0, PER + 1)],
            send1.at[o], recv1.at[other], region, other,
        )

    each(1, NTILE, lambda o: from_source(o).wait_recv())

    cell_rows = [
        jnp.sum(rbuf[8 * b : 8 * b + 8, PER, :], axis=0, keepdims=True) for b in range(4)
    ]
    for b in range(4):
        cells_out[b : b + 1, :] = cell_rows[b]
    cells_out[4:8, :] = jnp.zeros((4, LANES), F32)

    @pl.when(piece < NPIECE)
    def _():
        spread = wide_split(rbuf[:, 0:PER, :].reshape(NTILE * PER, LANES))
        hot = jnp.concatenate(
            [jnp.where(wanted[...] == cell_rows[b], 1.0, 0.0).astype(BF16) for b in range(4)], axis=1
        )
        moved = join3(jnp.dot(hot, spread, preferred_element_type=F32))
        msg[...] = moved.reshape(16, 40, LANES)

    def own_copy(o):
        i = lax.rem(piece + o, 16)
        return remote(
            msg.at[i, pl.ds(0, 24)], recv.at[piece, pl.ds(0, 24)],
            send2.at[0, o], recv2.at[0, piece], region, group * 16 + i,
        )

    def up_copy(i):
        return remote(
            msg.at[i, pl.ds(24, 8)], recv.at[piece, pl.ds(24, 8)],
            send2.at[1, i], recv2.at[1, piece], up, group * 16 + i,
        )

    def down_copy(i):
        return remote(
            msg.at[i, pl.ds(32, 8)], recv.at[piece, pl.ds(32, 8)],
            send2.at[2, i], recv2.at[2, piece], down, group * 16 + i,
        )

    @pl.when(piece < NPIECE)
    def _():
        each(1, 16, lambda o: own_copy(o).start())
        each(0, 16, lambda i: up_copy(i).start())
        each(0, 16, lambda i: down_copy(i).start())
        recv[piece, 0:24, :] = msg[piece, 0:24, :]

    def wait_own(p):
        @pl.when(p != piece)
        def _():
            remote(
                msg.at[0, pl.ds(0, 24)], recv.at[p, pl.ds(0, 24)],
                send2.at[0, 0], recv2.at[0, p], region, group * 16 + p,
            ).wait_recv()

    def wait_sides(p):
        remote(
            msg.at[0, pl.ds(24, 8)], recv.at[p, pl.ds(24, 8)],
            send2.at[1, 0], recv2.at[1, p], down, group * 16 + p,
        ).wait_recv()
        remote(
            msg.at[0, pl.ds(32, 8)], recv.at[p, pl.ds(32, 8)],
            send2.at[2, 0], recv2.at[2, p], up, group * 16 + p,
        ).wait_recv()

    each(0, NPIECE, wait_own)
    each(0, NPIECE, wait_sides)
    for p in range(12):
        data_out[p] = recv[p]
    width_out[...] = recv[12, 4:20, :]
    for r in range(6):
        rows_of[8 * r : 8 * r + 1, :] = recv[12, 24 + r : 25 + r, :]
        rows_of[8 * r + 1 : 8 * r + 5, :] = recv[12, 4 * r : 4 * r + 4, :]
        rows_of[8 * r + 5 : 8 * r + 6, :] = recv[12, 32 + r : 33 + r, :]

    def spread_lane(r, at):
        return jnp.broadcast_to(rows_of[8 * r : 8 * r + 8, at : at + 1], (8, LANES))

    lanes = lax.broadcasted_iota(jnp.int32, (8, LANES), 1)
    lanes_f = lanes.astype(F32)
    over = lax.broadcasted_iota(jnp.int32, (8, LANES), 0)
    filled = [spread_lane(r, 0) for r in range(6)]
    near = [
        [filled[r] if a == 1 else pltpu.roll(filled[r], (1 - a) % 8, 0) for a in range(3)]
        for r in range(6)
    ]
    for w in range(2):
        for r in range(1, 5):
            many = jnp.zeros((8, LANES), F32)
            todo = jnp.zeros((8, LANES), F32)
            for e in range(9):
                beside, beyond = e // 3, r + e % 3 - 1
                there = near[beyond][beside]
                keep = None if e == 4 else spread_lane(r, 3 + 9 * w + e)
                c = over + (beside - 1)
                t = jnp.where(c == 0, 24 + beyond, jnp.where(c == 5, 32 + beyond, beyond * 4 + c - 1))
                at = (8 * t).astype(F32)
                for h in range(2):
                    flag = jnp.where(there > LANES * h, 1.0 if keep is None else keep, 0.0)
                    todo = todo + jnp.where(many == lanes_f, flag * (at + 320.0 * h), 0.0)
                    many = many + flag
            chunks = lax.shift_right_logical(filled[r].astype(jnp.int32) + CHUNK - 1, CHUNK.bit_length() - 1)
            value = jnp.where(lanes_f < many, todo, 240.0).astype(jnp.int32)
            pairs = lax.shift_right_logical(many.astype(jnp.int32) + 1, 1)
            value = jnp.where(lanes == 24, pairs, value)
            value = jnp.where(lanes == 25, chunks, value)
            value = jnp.where(lanes == 26, filled[r].astype(jnp.int32), value)
            list_out[w, 8 * r - 8 : 8 * r, :] = value

    each(1, NTILE, lambda o: to_middle(o).wait_send())

    @pl.when(piece < NPIECE)
    def _():
        each(1, 16, lambda o: own_copy(o).wait_send())
        each(0, 16, lambda i: up_copy(i).wait_send())
        each(0, 16, lambda i: down_copy(i).wait_send())


def rate_of(which, notes):
    width = notes[:, 1 + which : 2 + which]
    return jnp.broadcast_to((32.0 * math.log2(math.e)) / (width * width), (PER, LANES))


def prepare(which, data, notes, cand, fan, rates):
    rate = rate_of(which, notes)
    rates[...] = -rate
    slot = lax.broadcasted_iota(jnp.int32, (40, LANES), 0)
    col = jnp.where(slot < 24, lax.rem(slot, 4) + 1, jnp.where(slot < 32, 0, 5)).astype(F32)
    row = jnp.where(
        slot < 24, slot // 4, jnp.where(slot < 32, slot - 24, slot - 32)
    ).astype(F32)
    columns = []
    for h in range(2):
        x = data[h] - 0.5
        y = data[2 + h] - 0.5
        cov = data[4 + 4 * which + h]
        for k, field in enumerate((x + col, y + row, cov * cov)):
            cand[pl.ds(320 * h + k, 40, stride=8), :] = field
        for source in (2.0 * rate * x[4:20], 2.0 * rate * y[4:20]):
            columns.append(jnp.transpose(jnp.concatenate(split3(source), axis=0)).astype(BF16))
    columns = jnp.concatenate(columns, axis=0)
    which_row = lax.bitwise_and(lax.broadcasted_iota(jnp.int32, (3 * PER, LANES), 0), PER - 1)
    for i in range(PER):
        pick = jnp.where(which_row == i, 1.0, 0.0).astype(BF16)
        fan[i] = jnp.dot(columns, pick, preferred_element_type=F32)


def sums_of(which, cand, pull, fan, rates, lists, weight_sums, pull_sums):
    def line(i):
        return lax.shift_right_logical(i, 2) * 8 + lax.bitwise_and(i, 3) + 1

    total = jnp.int32(0)
    for i in range(PER):
        at = 8 * (i // 4) + i % 4 + 1
        total = total + lists[which, at, 24] * lists[which, at, 25]

    shape3 = (CHUNK // 8, 8, LANES)

    def row(ref, at):
        return jnp.broadcast_to(ref[pl.ds(at, 1), :], (8, LANES))

    def item(n, carry):
        i, k, j, at, pairs, chunks, old_i, old_k, old_at, keep, powers, sums = carry
        sums = [value * keep for value in sums]
        for power, base in zip(powers, old_at):
            weight = jnp.exp2(power)
            sums[0] = sums[0] + weight * row(cand, base + 2)
            sums[1] = sums[1] + weight * row(pull, lax.shift_right_logical(base, 3))
        old = pl.ds(pl.multiple_of(old_k * CHUNK, CHUNK), CHUNK)
        weight_sums[old_i, old, :] = sums[0].reshape(CHUNK, LANES)
        pull_sums[old_i, old, :] = sums[1].reshape(CHUNK, LANES)

        first = lax.shift_right_logical(k, 1) * 256 + lax.bitwise_and(k, 1) * CHUNK
        u = fan[i, pl.ds(pl.multiple_of(first, CHUNK), CHUNK), :].reshape(shape3)
        v = fan[i, pl.ds(pl.multiple_of(first + LANES, CHUNK), CHUNK), :].reshape(shape3)
        scale = row(rates, i)
        shift_x = (lax.bitwise_and(i, 3) + 1).astype(F32)
        shift_y = (lax.shift_right_logical(i, 2) + 1).astype(F32)
        powers = []
        for base in at:
            x = row(cand, base) - shift_x
            y = row(cand, base + 1) - shift_y
            powers.append(u * x + (v * y + (x * x + y * y) * scale))
        keep = jnp.where(j == 0, 0.0, 1.0)
        last = j + 1 == pairs
        end = last & (k + 1 == chunks)
        next_j = jnp.where(last, 0, j + 1)
        next_k = jnp.where(end, 0, jnp.where(last, k + 1, k))
        next_i = jnp.minimum(jnp.where(end, i + 1, i), PER - 1)
        here = line(next_i)
        return (
            next_i, next_k, next_j,
            (lists[which, here, 2 * next_j], lists[which, here, 2 * next_j + 1]),
            lists[which, here, 24], lists[which, here, 25], i, k, at, keep, tuple(powers), tuple(sums),
        )

    zero = (fan[0, 0:CHUNK, :] * 0.0).reshape(shape3)
    start = jnp.int32(0)
    lax.fori_loop(
        0, total + 1, item,
        (
            start, start, start, (lists[which, 1, 0], lists[which, 1, 1]),
            lists[which, 1, 24], lists[which, 1, 25],
            start, start, (start, start), jnp.float32(0), (zero, zero), (zero, zero),
        ),
    )


def first_kernel(data, notes, lists, weight_sums, pull_sums, cand, pull, fan, rates):
    prepare(0, data, notes, cand, fan, rates)
    for h in range(2):
        pull[40 * h : 40 * h + 40, :] = data[4 + h] * data[6 + h]
    sums_of(0, cand, pull, fan, rates, lists, weight_sums, pull_sums)


def second_kernel(cand, pull, fan, rates, lists, weight_sums, pull_sums):
    sums_of(1, cand, pull, fan, rates, lists, weight_sums, pull_sums)


def finish(which, h, data, notes, weight_sums, pull_sums, totals):
    ones = jnp.ones((8, LANES), BF16)
    for k, ref in enumerate((weight_sums, pull_sums)):
        for i in range(PER):
            values = ref[i, LANES * h : LANES * h + LANES, :]
            high = values.astype(BF16)
            low = (values - high.astype(F32)).astype(BF16)
            both = jnp.concatenate([high, low], axis=0)
            sums = lax.dot_general(
                ones, both, (((1,), (1,)), ((), ())), preferred_element_type=F32
            )
            totals[k, i : i + 1, :] = sums[0:1, :LANES] + sums[0:1, LANES:]
    x = data[h, 4:20, :] - 0.5
    y = data[2 + h, 4:20, :] - 0.5
    cov = data[4 + 4 * which + h, 4:20, :]
    fade = jnp.exp2(-rate_of(which, notes) * (x * x + y * y))
    lane = lax.broadcasted_iota(jnp.int32, (PER, LANES), 1)
    live = (lane + LANES * h).astype(F32) < notes[:, 0:1]
    total = 1.0 + fade * totals[0]
    beta = jnp.where(live, fade * totals[1] / total, 0.0)
    return beta, jnp.where(live, cov * cov / total, 0.0)


def halo_kernel(
    weight_sums, pull_sums, data, notes, grid_out, beta_out, hat_out, cand_out, fan_out, rates_out,
    own, totals, recv, send, land,
):
    region = lax.axis_index("region")
    tile = lax.axis_index("tile")
    steps = [(a, b) for a in (-1, 0, 1) for b in (-1, 0, 1) if (a, b) != (0, 0)]

    owner = walk(tile)

    def place(a, b):
        return lax.rem(region + a + NREGION, NREGION), walk(lax.rem(owner + b + NTILE, NTILE))

    barrier = pltpu.get_barrier_semaphore()
    for a, b in steps:
        signal(barrier, *place(a, b))
    for h in range(2):
        beta, hat = finish(0, h, data, notes, weight_sums, pull_sums, totals)
        beta_out[h] = beta
        hat_out[h] = hat
        own[h] = data[8 + h, 4:20, :] * (data[10 + h, 4:20, :] - data[4 + h, 4:20, :] * beta)
    pl.semaphore_wait(barrier, 8)
    copies = []
    for k, (a, b) in enumerate(steps):
        copies.append(remote(own, recv.at[7 - k], send.at[k], land.at[7 - k], *place(a, b)))
    for copy in copies:
        copy.start()
    prepare(1, data, notes, cand_out, fan_out, rates_out)
    for copy in copies:
        copy.wait_recv()
    fits = {-1: region > 0, 0: None, 1: region < NREGION - 1}
    fits_row = {-1: owner > 0, 0: None, 1: owner < NTILE - 1}
    at = {step: k for k, step in enumerate(steps)}

    def take(h, a, b, low, high):
        rows = recv[at[(a, b)], h, low:high, :]
        for fit in (fits[a], fits_row[b]):
            if fit is not None:
                rows = jnp.where(fit, rows, 0.0)
        return rows

    for h in range(2):
        to = 40 * h
        grid_out[to + 4 : to + 20, :] = own[h]
        grid_out[to : to + 4, :] = take(h, 0, -1, 12, 16)
        grid_out[to + 20 : to + 24, :] = take(h, 0, 1, 0, 4)
        for a, edge, first in ((-1, 3, to + 24), (1, 0, to + 32)):
            grid_out[first : first + 1, :] = take(h, a, -1, 12 + edge, 13 + edge)
            for r in range(4):
                grid_out[first + 1 + r : first + 2 + r, :] = take(h, a, 0, 4 * r + edge, 4 * r + edge + 1)
            grid_out[first + 5 : first + 6, :] = take(h, a, 1, edge, edge + 1)
            grid_out[first + 6 : first + 8, :] = jnp.zeros((2, LANES), F32)
    for copy in copies:
        copy.wait_send()


def return_kernel(
    beta_one, hat_one, weight_sums, pull_sums, data, notes, cells, home, betas, hats, residual,
    totals, stage, rbuf, msg, recv, send1, recv1, send2, recv2,
):
    region = lax.axis_index("region")
    tile = lax.axis_index("tile")
    group = tile // 8
    piece = lax.rem(tile, 8)
    barrier = pltpu.get_barrier_semaphore()
    each(1, NTILE, lambda o: signal(barrier, region, lax.rem(tile + o, NTILE)))
    for h in range(2):
        stage[h] = beta_one[h]
        stage[2 + h] = hat_one[h]
        stage[4 + h], stage[6 + h] = finish(1, h, data, notes, weight_sums, pull_sums, totals)
    pl.semaphore_wait(barrier, NTILE - 1)

    def to_middle(o):
        other = lax.rem(tile + o, NTILE)
        return remote(
            stage.at[lax.rem(other, 8)], rbuf.at[tile], send1.at[o], recv1.at[tile], region, other
        )

    each(1, NTILE, lambda o: to_middle(o).start())
    rbuf[tile] = stage[piece]

    row = cells[pl.ds(group, 1), :]
    column = jnp.transpose(jnp.broadcast_to(row, (LANES, LANES)))
    lane = lax.broadcasted_iota(jnp.int32, (LANES, LANES), 1)
    hots = []
    for b in range(4):
        of = lax.shift_right_logical(lane, 4)
        if b % 2 == 1:
            of = 6 - of + 2 * lax.bitwise_and(of, 1)
        here = LANES * b + of * PER + lax.bitwise_and(lane, PER - 1)
        hots.append(jnp.where(here.astype(F32) == column, 1.0, 0.0).astype(BF16))
    hot = jnp.concatenate(hots, axis=1)

    def from_source(o):
        other = lax.rem(tile + o, NTILE)
        return remote(stage.at[0], rbuf.at[other], send1.at[o], recv1.at[other], region, other)

    each(1, NTILE, lambda o: from_source(o).wait_recv())
    spread = wide_split(rbuf[...].reshape(NTILE * PER, LANES))
    msg[...] = join3(jnp.dot(hot, spread, preferred_element_type=F32)).reshape(8, PER, LANES)

    def home_copy(o):
        i = lax.rem(piece + o, 8)
        return remote(
            msg.at[i], recv.at[piece], send2.at[o], recv2.at[piece], region, group * 8 + i
        )

    each(1, 8, lambda o: home_copy(o).start())
    recv[piece] = msg[piece]

    def from_middle(o):
        p = lax.rem(piece + o, 8)
        return remote(msg.at[0], recv.at[p], send2.at[o], recv2.at[p], region, group * 8 + p)

    each(1, 8, lambda o: from_middle(o).wait_recv())
    for h in range(2):
        left = home[4 + h] - home[h] * recv[h] - home[2 + h] * recv[4 + h]
        residual[pl.ds(h, PER, stride=2), :] = left
        for t in range(PER):
            span = slice(LANES * (2 * t + h), LANES * (2 * t + h + 1))
            for f in range(2):
                betas[f : f + 1, span] = recv[4 * f + h, t : t + 1, :]
                hats[f : f + 1, span] = recv[2 + 4 * f + h, t : t + 1, :]
    each(1, NTILE, lambda o: to_middle(o).wait_send())
    each(1, 8, lambda o: home_copy(o).wait_send())


def store_kernel(betas, hats, residual, betas_out, hats_out, residual_out, done):
    pairs = ((betas, betas_out), (hats, hats_out), (residual, residual_out))
    copies = [pltpu.make_async_copy(a, b, done.at[k]) for k, (a, b) in enumerate(pairs)]
    for copy in copies:
        copy.start()
    for copy in copies:
        copy.wait()


VM = pl.BlockSpec(memory_space=pltpu.VMEM)
SM = pl.BlockSpec(memory_space=pltpu.SMEM)
HB = pl.BlockSpec(memory_space=pltpu.HBM)
DMA = pltpu.SemaphoreType.DMA


def shape(*dims, dtype=F32):
    return jax.ShapeDtypeStruct(dims, dtype)


def body(offsets, design, target, beta_second, counts, kernel_width, reach, assignment):
    data, notes, lists, cells, home = pl.pallas_call(
        gather_kernel,
        out_shape=[
            shape(12, 40, LANES), shape(PER, LANES), shape(2, 32, LANES, dtype=jnp.int32),
            shape(8, LANES), shape(6, PER, LANES),
        ],
        in_specs=[HB] * 8,
        out_specs=[VM] * 5,
        scratch_shapes=[
            pltpu.VMEM((2, NTILE * LANES), F32),
            pltpu.VMEM((2, NTILE * LANES), F32),
            pltpu.VMEM((NTILE, LANES), F32),
            pltpu.VMEM((NTILE, LANES), F32),
            pltpu.VMEM((1, PER), jnp.int32),
            pltpu.VMEM((2, PER), jnp.int32),
            pltpu.VMEM((9, 2, PER), jnp.int32),
            pltpu.VMEM((1, PER), jnp.int32),
            pltpu.VMEM((32, LANES), F32),
            pltpu.VMEM((48, LANES), F32),
            pltpu.VMEM((640, LANES), F32),
            pltpu.VMEM((NPIECE, 24, LANES), F32),
            pltpu.VMEM((NTILE, 24, LANES), F32),
            pltpu.VMEM((16, 40, LANES), F32),
            pltpu.VMEM((NPIECE, 40, LANES), F32),
            DMA((8,)),
            DMA((NTILE,)),
            DMA((NTILE,)),
            DMA((3, 16)),
            DMA((3, 16)),
        ],
        compiler_params=pltpu.CompilerParams(collective_id=0, has_side_effects=True, vmem_limit_bytes=8 << 20),
        name="to_owners",
    )(
        *(
            pltpu.with_memory_space_constraint(value, pltpu.HBM)
            for value in (
                offsets, design, target.reshape(NTILE, LANES), beta_second.reshape(NTILE, LANES),
                counts.reshape(1, PER), kernel_width, reach.transpose(2, 0, 1), assignment,
            )
        )
    )
    sums = [shape(PER, 2 * LANES, LANES)] * 2
    tables = [(640, LANES), (80, LANES), (PER, 4 * LANES, LANES), (PER, LANES)]
    weight_sums, pull_sums = pl.pallas_call(
        first_kernel,
        out_shape=sums,
        in_specs=[VM, VM, SM],
        out_specs=[VM] * 2,
        scratch_shapes=[pltpu.VMEM(dims, F32) for dims in tables],
        compiler_params=pltpu.CompilerParams(vmem_limit_bytes=16 << 20),
        name="smooth_one",
    )(data, notes, lists)
    grid, beta_one, hat_one, cand, fan, rates = pl.pallas_call(
        halo_kernel,
        out_shape=[
            shape(80, LANES), shape(2, PER, LANES), shape(2, PER, LANES), shape(640, LANES),
            shape(PER, 4 * LANES, LANES), shape(PER, LANES),
        ],
        in_specs=[VM] * 4,
        out_specs=[VM] * 6,
        scratch_shapes=[
            pltpu.VMEM((2, PER, LANES), F32),
            pltpu.VMEM((2, PER, LANES), F32),
            pltpu.VMEM((8, 2, PER, LANES), F32),
            DMA((8,)),
            DMA((8,)),
        ],
        compiler_params=pltpu.CompilerParams(
            collective_id=1, has_side_effects=True, vmem_limit_bytes=16 << 20
        ),
        name="edges",
    )(weight_sums, pull_sums, data, notes)
    weight_sums, pull_sums = pl.pallas_call(
        second_kernel,
        out_shape=sums,
        in_specs=[VM] * 4 + [SM],
        out_specs=[VM] * 2,
        compiler_params=pltpu.CompilerParams(vmem_limit_bytes=16 << 20),
        name="smooth_two",
    )(cand, grid, fan, rates, lists)
    betas, hats, residual = pl.pallas_call(
        return_kernel,
        out_shape=[shape(2, NTILE * LANES), shape(2, NTILE * LANES), shape(NTILE, LANES)],
        in_specs=[VM] * 8,
        out_specs=[VM] * 3,
        scratch_shapes=[
            pltpu.VMEM((2, PER, LANES), F32),
            pltpu.VMEM((8, PER, LANES), F32),
            pltpu.VMEM((NTILE, PER, LANES), F32),
            pltpu.VMEM((8, PER, LANES), F32),
            pltpu.VMEM((8, PER, LANES), F32),
            DMA((NTILE,)),
            DMA((NTILE,)),
            DMA((8,)),
            DMA((8,)),
        ],
        compiler_params=pltpu.CompilerParams(collective_id=2, has_side_effects=True, vmem_limit_bytes=8 << 20),
        name="to_slots",
    )(beta_one, hat_one, weight_sums, pull_sums, data, notes, cells, home)
    betas, hats, residual = pl.pallas_call(
        store_kernel,
        out_shape=[shape(2, NTILE * LANES), shape(2, NTILE * LANES), shape(NTILE, LANES)],
        in_specs=[VM] * 3,
        out_specs=[HB] * 3,
        scratch_shapes=[DMA((3,))],
        compiler_params=pltpu.CompilerParams(vmem_limit_bytes=8 << 20),
        name="store",
    )(betas, hats, residual)
    return betas, hats, residual.reshape(-1)


def solution(mesh):
    split = ("region", "tile")
    in_specs = (
        P(None, split), P(None, split), P(split), P(split), P(split), P(None, split),
        P(None, split, None), P("region", "tile"),
    )
    out_specs = (P(None, split), P(None, split), P(split))
    return jax.shard_map(body, mesh=mesh, in_specs=in_specs, out_specs=out_specs, check_vma=False)
```

```python
import functools
import math

import jax
import jax.numpy as jnp
from jax import lax
from jax.experimental import pallas as pl
from jax.experimental.pallas import tpu as pltpu
from jax.sharding import PartitionSpec as P

TX = 4
LANES = 128
PER = 16
NPIECE = 13
CHUNK = 64
NREGION = 8
NTILE = 32
F32 = jnp.float32
BF16 = jnp.bfloat16


def split3(x):
    hi = x.astype(BF16).astype(F32)
    rest = x - hi
    mid = rest.astype(BF16).astype(F32)
    low = (rest - mid).astype(BF16).astype(F32)
    return hi, mid, low


def wide_split(x):
    hi, mid, low = split3(x)
    return jnp.concatenate([hi.astype(BF16), mid.astype(BF16), low.astype(BF16)], axis=1)


def join3(x):
    return x[:, :LANES] + x[:, LANES : 2 * LANES] + x[:, 2 * LANES :]


def remote(src, dst, send, recv, region, tile):
    return pltpu.make_async_remote_copy(
        src_ref=src,
        dst_ref=dst,
        send_sem=send,
        recv_sem=recv,
        device_id=(region, tile),
        device_id_type=pl.DeviceIdType.MESH,
    )


def signal(sem, region, tile):
    pl.semaphore_signal(sem, inc=1, device_id=(region, tile), device_id_type=pl.DeviceIdType.MESH)


def links(k):
    away = (0, 1, 2, 1)
    return away[k // 2 % 4] + away[k // 8 % 4] + k % 2 / 2


FAR_FIRST = sorted(range(1, NTILE), key=lambda k: -links(k))


def each(low, high, step):
    def turn(index, carry):
        step(index)
        return carry

    lax.fori_loop(low, high, turn, 0)


def walk(tile):
    turned = (tile // 8) * 8 + 6 - lax.rem(tile, 8) + 2 * lax.rem(tile, 2)
    return jnp.where(lax.rem(tile // 8, 2) == 1, turned, tile)


def gather_kernel(
    offsets_in, design_in, target_in, prior_in, counts_in, width_in, reach_in, cells_in,
    data_out, width_out, list_out, cells_out, home_out,
    offs, design, target, prior, counts, widths, reach, cells, notes, rows_of,
    wanted, stage, rbuf, msg, recv, load, send1, recv1, send2, recv2,
):
    region = lax.axis_index("region")
    tile = lax.axis_index("tile")
    group = tile // 16
    piece = lax.rem(tile, 16)
    up = lax.rem(region + 1, NREGION)
    down = lax.rem(region + NREGION - 1, NREGION)

    barrier = pltpu.get_barrier_semaphore()
    for k in range(15, -1, -1):
        signal(barrier, up, jnp.bitwise_xor(tile, k))
        signal(barrier, down, jnp.bitwise_xor(tile, k))
    for k in FAR_FIRST:
        signal(barrier, region, jnp.bitwise_xor(tile, k))

    loads = [
        pltpu.make_async_copy(source, place, load.at[k])
        for k, (source, place) in enumerate(
            (
                (counts_in, counts), (width_in, widths), (reach_in, reach), (cells_in, cells),
                (offsets_in, offs), (design_in, design), (target_in, target), (prior_in, prior),
            )
        )
    ]
    for copy in loads:
        copy.start()
    notes[...] = jnp.zeros((32, LANES), F32)
    stage[12] = jnp.zeros((24, LANES), F32)
    rows_of[...] = jnp.zeros((48, LANES), F32)
    for copy in loads[:4]:
        copy.wait()
    notes[0:1, 0:PER] = counts[...].astype(F32)
    notes[1:3, 0:PER] = widths[...].astype(F32)
    for e in range(9):
        for w in range(2):
            at = 3 + 9 * w + e
            notes[at : at + 1, 0:PER] = reach[e, w : w + 1, :].astype(F32)
    turned = jnp.transpose(notes[...])[0:PER]
    stage[12, 0:PER, 0:32] = turned
    cell = cells[...]
    order = (lax.bitwise_and(cell, 127) * TX + lax.shift_right_logical(cell, 7)).astype(F32)
    for k in range(8):
        notes[24:25, PER * k : PER * k + PER] = order
    row_lane = lax.broadcasted_iota(jnp.int32, (8, LANES), 1)
    cell_row = jnp.where(
        lax.shift_right_logical(row_lane, 4) == lax.rem(tile, 8),
        jnp.broadcast_to(notes[24:25, :], (8, LANES)), 0.0,
    )
    for p in range(NPIECE):
        stage[p, PER : PER + 8, :] = cell_row
    for copy in loads[4:]:
        copy.wait()
    lane = lax.broadcasted_iota(jnp.int32, (PER, LANES), 1)
    count = turned[:, 0:1]
    for t in range(PER):
        for h in range(2):
            span = slice(LANES * (2 * t + h), LANES * (2 * t + h + 1))
            for f in range(2):
                stage[2 * f + h, t : t + 1, :] = offs[f : f + 1, span]
                stage[4 + 4 * f + h, t : t + 1, :] = design[f : f + 1, span]
    for h in range(2):
        present = ((lane + LANES * h).astype(F32) < count).astype(F32)
        cov_one = stage[4 + h, 0:PER, :] * present
        cov_two = stage[8 + h, 0:PER, :]
        seen = target[pl.ds(h, PER, stride=2), :]
        before = prior[pl.ds(h, PER, stride=2), :]
        stage[4 + h, 0:PER, :] = cov_one
        stage[6 + h, 0:PER, :] = seen - cov_two * before
        cov_two = cov_two * present
        stage[8 + h, 0:PER, :] = cov_two
        stage[10 + h, 0:PER, :] = seen
        home_out[h] = cov_one
        home_out[2 + h] = cov_two
        home_out[4 + h] = seen * present

    pl.semaphore_wait(barrier, NTILE - 1 + 32)

    def to_middle(o):
        other = jnp.bitwise_xor(tile, o)
        held = jnp.minimum(lax.rem(other, 16), NPIECE - 1)
        return remote(
            stage.at[held, pl.ds(0, PER + 1)], rbuf.at[tile, pl.ds(0, PER + 1)],
            send1.at[o], recv1.at[tile], region, other,
        )

    for k in FAR_FIRST:
        to_middle(k).start()
    rbuf[tile] = stage[jnp.minimum(piece, NPIECE - 1)]

    number = lax.broadcasted_iota(jnp.int32, (640, LANES), 0)
    owner = lax.shift_right_logical(number * 205, 13)
    q = number - owner * 40
    turned_owner = 14 - lax.bitwise_and(owner, 7) + 2 * lax.bitwise_and(owner, 1)
    first = (group * 16 + jnp.where(owner < 8, owner, turned_owner)) * 16
    side = jnp.where(q < 32, q - 24, q - 32)
    base = jnp.where(q < 24, q - 4, (side - 1) * 4 + jnp.where(q < 32, 3, 0))
    open_up = jnp.where(region < NREGION - 1, 1, 0)
    open_down = jnp.where(region > 0, 1, 0)
    beside = jnp.where(side < 6, jnp.where(q < 32, open_up, open_down), 0)
    allowed = jnp.where(q < 24, 1, beside)
    cell = first + base
    wanted[...] = jnp.where(allowed > 0, cell, -1).astype(F32)

    def from_source(o):
        other = jnp.bitwise_xor(tile, o)
        return remote(
            stage.at[0, pl.ds(0, PER + 1)], rbuf.at[other, pl.ds(0, PER + 1)],
            send1.at[o], recv1.at[other], region, other,
        )

    each(1, NTILE, lambda o: from_source(o).wait_recv())

    cell_rows = [
        jnp.sum(rbuf[8 * b : 8 * b + 8, PER, :], axis=0, keepdims=True) for b in range(4)
    ]
    for b in range(4):
        cells_out[b : b + 1, :] = cell_rows[b]
    cells_out[4:8, :] = jnp.zeros((4, LANES), F32)

    @pl.when(piece < NPIECE)
    def _():
        spread = wide_split(rbuf[:, 0:PER, :].reshape(NTILE * PER, LANES))
        hot = jnp.concatenate(
            [jnp.where(wanted[...] == cell_rows[b], 1.0, 0.0).astype(BF16) for b in range(4)], axis=1
        )
        moved = join3(jnp.dot(hot, spread, preferred_element_type=F32))
        msg[...] = moved.reshape(16, 40, LANES)

    def own_copy(o):
        i = jnp.bitwise_xor(piece, o)
        return remote(
            msg.at[i, pl.ds(0, 24)], recv.at[piece, pl.ds(0, 24)],
            send2.at[0, o], recv2.at[0, piece], region, group * 16 + i,
        )

    def up_copy(i):
        return remote(
            msg.at[i, pl.ds(24, 8)], recv.at[piece, pl.ds(24, 8)],
            send2.at[1, i], recv2.at[1, piece], up, group * 16 + i,
        )

    def down_copy(i):
        return remote(
            msg.at[i, pl.ds(32, 8)], recv.at[piece, pl.ds(32, 8)],
            send2.at[2, i], recv2.at[2, piece], down, group * 16 + i,
        )

    @pl.when(piece < NPIECE)
    def _():
        for k in sorted(range(16), key=lambda k: -links(k)):
            up_copy(jnp.bitwise_xor(piece, k)).start()
            down_copy(jnp.bitwise_xor(piece, k)).start()
        for k in FAR_FIRST:
            if k < 16:
                own_copy(k).start()
        recv[piece, 0:24, :] = msg[piece, 0:24, :]

    def wait_own(p):
        @pl.when(p != piece)
        def _():
            remote(
                msg.at[0, pl.ds(0, 24)], recv.at[p, pl.ds(0, 24)],
                send2.at[0, 0], recv2.at[0, p], region, group * 16 + p,
            ).wait_recv()

    def wait_sides(p):
        remote(
            msg.at[0, pl.ds(24, 8)], recv.at[p, pl.ds(24, 8)],
            send2.at[1, 0], recv2.at[1, p], down, group * 16 + p,
        ).wait_recv()
        remote(
            msg.at[0, pl.ds(32, 8)], recv.at[p, pl.ds(32, 8)],
            send2.at[2, 0], recv2.at[2, p], up, group * 16 + p,
        ).wait_recv()

    each(0, NPIECE, wait_own)
    each(0, NPIECE, wait_sides)
    for p in range(12):
        data_out[p] = recv[p]
    width_out[...] = recv[12, 4:20, :]
    for r in range(6):
        rows_of[8 * r : 8 * r + 1, :] = recv[12, 24 + r : 25 + r, :]
        rows_of[8 * r + 1 : 8 * r + 5, :] = recv[12, 4 * r : 4 * r + 4, :]
        rows_of[8 * r + 5 : 8 * r + 6, :] = recv[12, 32 + r : 33 + r, :]

    def spread_lane(r, at):
        return jnp.broadcast_to(rows_of[8 * r : 8 * r + 8, at : at + 1], (8, LANES))

    lanes = lax.broadcasted_iota(jnp.int32, (8, LANES), 1)
    lanes_f = lanes.astype(F32)
    over = lax.broadcasted_iota(jnp.int32, (8, LANES), 0)
    filled = [spread_lane(r, 0) for r in range(6)]
    near = [
        [filled[r] if a == 1 else pltpu.roll(filled[r], (1 - a) % 8, 0) for a in range(3)]
        for r in range(6)
    ]
    for w in range(2):
        for r in range(1, 5):
            many = jnp.zeros((8, LANES), F32)
            todo = jnp.zeros((8, LANES), F32)
            for e in range(9):
                beside, beyond = e // 3, r + e % 3 - 1
                there = near[beyond][beside]
                keep = None if e == 4 else spread_lane(r, 3 + 9 * w + e)
                c = over + (beside - 1)
                t = jnp.where(c == 0, 24 + beyond, jnp.where(c == 5, 32 + beyond, beyond * 4 + c - 1))
                at = (8 * t).astype(F32)
                for h in range(2):
                    flag = jnp.where(there > LANES * h, 1.0 if keep is None else keep, 0.0)
                    todo = todo + jnp.where(many == lanes_f, flag * (at + 320.0 * h), 0.0)
                    many = many + flag
            chunks = lax.shift_right_logical(filled[r].astype(jnp.int32) + CHUNK - 1, CHUNK.bit_length() - 1)
            value = jnp.where(lanes_f < many, todo, 240.0).astype(jnp.int32)
            pairs = lax.shift_right_logical(many.astype(jnp.int32) + 1, 1)
            value = jnp.where(lanes == 24, pairs, value)
            value = jnp.where(lanes == 25, chunks, value)
            value = jnp.where(lanes == 26, filled[r].astype(jnp.int32), value)
            list_out[w, 8 * r - 8 : 8 * r, :] = value

    each(1, NTILE, lambda o: to_middle(o).wait_send())

    @pl.when(piece < NPIECE)
    def _():
        each(1, 16, lambda o: own_copy(o).wait_send())
        each(0, 16, lambda i: up_copy(i).wait_send())
        each(0, 16, lambda i: down_copy(i).wait_send())


def rate_of(which, notes):
    width = notes[:, 1 + which : 2 + which]
    return jnp.broadcast_to((32.0 * math.log2(math.e)) / (width * width), (PER, LANES))


def prepare(which, data, notes, cand, fan, rates):
    rate = rate_of(which, notes)
    rates[...] = -rate
    slot = lax.broadcasted_iota(jnp.int32, (40, LANES), 0)
    col = jnp.where(slot < 24, lax.rem(slot, 4) + 1, jnp.where(slot < 32, 0, 5)).astype(F32)
    row = jnp.where(
        slot < 24, slot // 4, jnp.where(slot < 32, slot - 24, slot - 32)
    ).astype(F32)
    columns = []
    for h in range(2):
        x = data[h] - 0.5
        y = data[2 + h] - 0.5
        cov = data[4 + 4 * which + h]
        for k, field in enumerate((x + col, y + row, cov * cov)):
            cand[pl.ds(320 * h + k, 40, stride=8), :] = field
        for source in (2.0 * rate * x[4:20], 2.0 * rate * y[4:20]):
            columns.append(jnp.transpose(jnp.concatenate(split3(source), axis=0)).astype(BF16))
    columns = jnp.concatenate(columns, axis=0)
    which_row = lax.bitwise_and(lax.broadcasted_iota(jnp.int32, (3 * PER, LANES), 0), PER - 1)
    for i in range(PER):
        pick = jnp.where(which_row == i, 1.0, 0.0).astype(BF16)
        fan[i] = jnp.dot(columns, pick, preferred_element_type=F32)


def sums_of(which, cand, pull, fan, rates, lists, weight_sums, pull_sums):
    def line(i):
        return lax.shift_right_logical(i, 2) * 8 + lax.bitwise_and(i, 3) + 1

    total = jnp.int32(0)
    for i in range(PER):
        at = 8 * (i // 4) + i % 4 + 1
        total = total + lists[which, at, 24] * lists[which, at, 25]

    shape3 = (CHUNK // 8, 8, LANES)

    def row(ref, at):
        return jnp.broadcast_to(ref[pl.ds(at, 1), :], (8, LANES))

    def item(n, carry):
        i, k, j, at, pairs, chunks, old_i, old_k, old_at, keep, powers, sums = carry
        sums = [value * keep for value in sums]
        for power, base in zip(powers, old_at):
            weight = jnp.exp2(power)
            sums[0] = sums[0] + weight * row(cand, base + 2)
            sums[1] = sums[1] + weight * row(pull, lax.shift_right_logical(base, 3))
        old = pl.ds(pl.multiple_of(old_k * CHUNK, CHUNK), CHUNK)
        weight_sums[old_i, old, :] = sums[0].reshape(CHUNK, LANES)
        pull_sums[old_i, old, :] = sums[1].reshape(CHUNK, LANES)

        first = lax.shift_right_logical(k, 1) * 256 + lax.bitwise_and(k, 1) * CHUNK
        u = fan[i, pl.ds(pl.multiple_of(first, CHUNK), CHUNK), :].reshape(shape3)
        v = fan[i, pl.ds(pl.multiple_of(first + LANES, CHUNK), CHUNK), :].reshape(shape3)
        scale = row(rates, i)
        shift_x = (lax.bitwise_and(i, 3) + 1).astype(F32)
        shift_y = (lax.shift_right_logical(i, 2) + 1).astype(F32)
        powers = []
        for base in at:
            x = row(cand, base) - shift_x
            y = row(cand, base + 1) - shift_y
            powers.append(u * x + (v * y + (x * x + y * y) * scale))
        keep = jnp.where(j == 0, 0.0, 1.0)
        last = j + 1 == pairs
        end = last & (k + 1 == chunks)
        next_j = jnp.where(last, 0, j + 1)
        next_k = jnp.where(end, 0, jnp.where(last, k + 1, k))
        next_i = jnp.minimum(jnp.where(end, i + 1, i), PER - 1)
        here = line(next_i)
        return (
            next_i, next_k, next_j,
            (lists[which, here, 2 * next_j], lists[which, here, 2 * next_j + 1]),
            lists[which, here, 24], lists[which, here, 25], i, k, at, keep, tuple(powers), tuple(sums),
        )

    zero = (fan[0, 0:CHUNK, :] * 0.0).reshape(shape3)
    start = jnp.int32(0)
    lax.fori_loop(
        0, total + 1, item,
        (
            start, start, start, (lists[which, 1, 0], lists[which, 1, 1]),
            lists[which, 1, 24], lists[which, 1, 25],
            start, start, (start, start), jnp.float32(0), (zero, zero), (zero, zero),
        ),
    )


def first_kernel(data, notes, lists, weight_sums, pull_sums, cand, pull, fan, rates):
    prepare(0, data, notes, cand, fan, rates)
    for h in range(2):
        pull[40 * h : 40 * h + 40, :] = data[4 + h] * data[6 + h]
    sums_of(0, cand, pull, fan, rates, lists, weight_sums, pull_sums)


def second_kernel(cand, pull, fan, rates, lists, weight_sums, pull_sums):
    sums_of(1, cand, pull, fan, rates, lists, weight_sums, pull_sums)


def finish(which, h, data, notes, weight_sums, pull_sums, totals):
    ones = jnp.ones((8, LANES), BF16)
    for k, ref in enumerate((weight_sums, pull_sums)):
        for i in range(PER):
            values = ref[i, LANES * h : LANES * h + LANES, :]
            high = values.astype(BF16)
            low = (values - high.astype(F32)).astype(BF16)
            both = jnp.concatenate([high, low], axis=0)
            sums = lax.dot_general(
                ones, both, (((1,), (1,)), ((), ())), preferred_element_type=F32
            )
            totals[k, i : i + 1, :] = sums[0:1, :LANES] + sums[0:1, LANES:]
    x = data[h, 4:20, :] - 0.5
    y = data[2 + h, 4:20, :] - 0.5
    cov = data[4 + 4 * which + h, 4:20, :]
    fade = jnp.exp2(-rate_of(which, notes) * (x * x + y * y))
    lane = lax.broadcasted_iota(jnp.int32, (PER, LANES), 1)
    live = (lane + LANES * h).astype(F32) < notes[:, 0:1]
    total = 1.0 + fade * totals[0]
    beta = jnp.where(live, fade * totals[1] / total, 0.0)
    return beta, jnp.where(live, cov * cov / total, 0.0)


def edge_cells(a, b):
    cols = range(4) if a == 0 else (0 if a == -1 else 3,)
    rows = range(4) if b == 0 else (0 if b == -1 else 3,)
    return [4 * r + c for r in rows for c in cols]


def halo_kernel(
    weight_sums, pull_sums, data, notes, grid_out, beta_out, hat_out, cand_out, fan_out, rates_out,
    own, edge, totals, recv, send, land,
):
    region = lax.axis_index("region")
    tile = lax.axis_index("tile")
    steps = [(a, b) for a in (-1, 0, 1) for b in (-1, 0, 1) if (a, b) != (0, 0)]

    owner = walk(tile)

    def place(a, b):
        return lax.rem(region + a + NREGION, NREGION), walk(lax.rem(owner + b + NTILE, NTILE))

    barrier = pltpu.get_barrier_semaphore()
    for a, b in steps:
        signal(barrier, *place(a, b))
    for h in range(2):
        beta, hat = finish(0, h, data, notes, weight_sums, pull_sums, totals)
        beta_out[h] = beta
        hat_out[h] = hat
        own[h] = data[8 + h, 4:20, :] * (data[10 + h, 4:20, :] - data[4 + h, 4:20, :] * beta)
    edge[...] = jnp.zeros((8, 8, LANES), F32)
    for k, (a, b) in enumerate(steps):
        for h in range(2):
            for n, i in enumerate(edge_cells(a, b)):
                edge[k, 4 * h + n : 4 * h + n + 1, :] = own[h, i : i + 1, :]
    pl.semaphore_wait(barrier, 8)
    copies = []
    for k, (a, b) in enumerate(steps):
        copies.append(remote(edge.at[k], recv.at[7 - k], send.at[k], land.at[7 - k], *place(a, b)))
    for copy in copies:
        copy.start()
    prepare(1, data, notes, cand_out, fan_out, rates_out)
    for copy in copies:
        copy.wait_recv()
    fits = {-1: region > 0, 0: None, 1: region < NREGION - 1}
    fits_row = {-1: owner > 0, 0: None, 1: owner < NTILE - 1}
    for h in range(2):
        to = 40 * h
        grid_out[to + 4 : to + 20, :] = own[h]
        for first in (to + 30, to + 38):
            grid_out[first : first + 2, :] = jnp.zeros((2, LANES), F32)
        for k, (a, b) in enumerate(steps):
            many = len(edge_cells(-a, -b))
            rows = recv[k, 4 * h : 4 * h + many, :]
            for fit in (fits[a], fits_row[b]):
                if fit is not None:
                    rows = jnp.where(fit, rows, 0.0)
            if a == 0:
                first = to + (0 if b == -1 else 20)
            else:
                first = to + (24 if a == -1 else 32) + (0, 1, 5)[b + 1]
            grid_out[first : first + many, :] = rows
    for copy in copies:
        copy.wait_send()


def return_kernel(
    beta_one, hat_one, weight_sums, pull_sums, data, notes, cells, home, betas, hats, residual,
    totals, stage, rbuf, msg, recv, send1, recv1, send2, recv2,
):
    region = lax.axis_index("region")
    tile = lax.axis_index("tile")
    group = tile // 8
    piece = lax.rem(tile, 8)
    barrier = pltpu.get_barrier_semaphore()
    for k in FAR_FIRST:
        signal(barrier, region, jnp.bitwise_xor(tile, k))
    for h in range(2):
        stage[h] = beta_one[h]
        stage[2 + h] = hat_one[h]
        stage[4 + h], stage[6 + h] = finish(1, h, data, notes, weight_sums, pull_sums, totals)
    pl.semaphore_wait(barrier, NTILE - 1)

    def to_middle(o):
        other = jnp.bitwise_xor(tile, o)
        return remote(
            stage.at[lax.rem(other, 8)], rbuf.at[tile], send1.at[o], recv1.at[tile], region, other
        )

    for k in FAR_FIRST:
        to_middle(k).start()
    rbuf[tile] = stage[piece]

    row = cells[pl.ds(group, 1), :]
    column = jnp.transpose(jnp.broadcast_to(row, (LANES, LANES)))
    lane = lax.broadcasted_iota(jnp.int32, (LANES, LANES), 1)
    hots = []
    for b in range(4):
        of = lax.shift_right_logical(lane, 4)
        if b % 2 == 1:
            of = 6 - of + 2 * lax.bitwise_and(of, 1)
        here = LANES * b + of * PER + lax.bitwise_and(lane, PER - 1)
        hots.append(jnp.where(here.astype(F32) == column, 1.0, 0.0).astype(BF16))
    hot = jnp.concatenate(hots, axis=1)

    def from_source(o):
        other = jnp.bitwise_xor(tile, o)
        return remote(stage.at[0], rbuf.at[other], send1.at[o], recv1.at[other], region, other)

    each(1, NTILE, lambda o: from_source(o).wait_recv())
    spread = wide_split(rbuf[...].reshape(NTILE * PER, LANES))
    msg[...] = join3(jnp.dot(hot, spread, preferred_element_type=F32)).reshape(8, PER, LANES)

    def home_copy(o):
        i = jnp.bitwise_xor(piece, o)
        return remote(
            msg.at[i], recv.at[piece], send2.at[o], recv2.at[piece], region, group * 8 + i
        )

    for k in FAR_FIRST:
        if k < 8:
            home_copy(k).start()
    recv[piece] = msg[piece]

    def from_middle(o):
        p = jnp.bitwise_xor(piece, o)
        return remote(msg.at[0], recv.at[p], send2.at[o], recv2.at[p], region, group * 8 + p)

    each(1, 8, lambda o: from_middle(o).wait_recv())
    for h in range(2):
        left = home[4 + h] - home[h] * recv[h] - home[2 + h] * recv[4 + h]
        residual[pl.ds(h, PER, stride=2), :] = left
        for t in range(PER):
            span = slice(LANES * (2 * t + h), LANES * (2 * t + h + 1))
            for f in range(2):
                betas[f : f + 1, span] = recv[4 * f + h, t : t + 1, :]
                hats[f : f + 1, span] = recv[2 + 4 * f + h, t : t + 1, :]
    each(1, NTILE, lambda o: to_middle(o).wait_send())
    each(1, 8, lambda o: home_copy(o).wait_send())


def store_kernel(betas, hats, residual, betas_out, hats_out, residual_out, done):
    pairs = ((betas, betas_out), (hats, hats_out), (residual, residual_out))
    copies = [pltpu.make_async_copy(a, b, done.at[k]) for k, (a, b) in enumerate(pairs)]
    for copy in copies:
        copy.start()
    for copy in copies:
        copy.wait()


VM = pl.BlockSpec(memory_space=pltpu.VMEM)
SM = pl.BlockSpec(memory_space=pltpu.SMEM)
HB = pl.BlockSpec(memory_space=pltpu.HBM)
DMA = pltpu.SemaphoreType.DMA


def shape(*dims, dtype=F32):
    return jax.ShapeDtypeStruct(dims, dtype)


def body(offsets, design, target, beta_second, counts, kernel_width, reach, assignment):
    data, notes, lists, cells, home = pl.pallas_call(
        gather_kernel,
        out_shape=[
            shape(12, 40, LANES), shape(PER, LANES), shape(2, 32, LANES, dtype=jnp.int32),
            shape(8, LANES), shape(6, PER, LANES),
        ],
        in_specs=[HB] * 8,
        out_specs=[VM] * 5,
        scratch_shapes=[
            pltpu.VMEM((2, NTILE * LANES), F32),
            pltpu.VMEM((2, NTILE * LANES), F32),
            pltpu.VMEM((NTILE, LANES), F32),
            pltpu.VMEM((NTILE, LANES), F32),
            pltpu.VMEM((1, PER), jnp.int32),
            pltpu.VMEM((2, PER), jnp.int32),
            pltpu.VMEM((9, 2, PER), jnp.int32),
            pltpu.VMEM((1, PER), jnp.int32),
            pltpu.VMEM((32, LANES), F32),
            pltpu.VMEM((48, LANES), F32),
            pltpu.VMEM((640, LANES), F32),
            pltpu.VMEM((NPIECE, 24, LANES), F32),
            pltpu.VMEM((NTILE, 24, LANES), F32),
            pltpu.VMEM((16, 40, LANES), F32),
            pltpu.VMEM((NPIECE, 40, LANES), F32),
            DMA((8,)),
            DMA((NTILE,)),
            DMA((NTILE,)),
            DMA((3, 16)),
            DMA((3, 16)),
        ],
        compiler_params=pltpu.CompilerParams(collective_id=0, has_side_effects=True, vmem_limit_bytes=8 << 20),
        name="to_owners",
    )(
        *(
            pltpu.with_memory_space_constraint(value, pltpu.HBM)
            for value in (
                offsets, design, target.reshape(NTILE, LANES), beta_second.reshape(NTILE, LANES),
                counts.reshape(1, PER), kernel_width, reach.transpose(2, 0, 1), assignment,
            )
        )
    )
    sums = [shape(PER, 2 * LANES, LANES)] * 2
    tables = [(640, LANES), (80, LANES), (PER, 4 * LANES, LANES), (PER, LANES)]
    weight_sums, pull_sums = pl.pallas_call(
        first_kernel,
        out_shape=sums,
        in_specs=[VM, VM, SM],
        out_specs=[VM] * 2,
        scratch_shapes=[pltpu.VMEM(dims, F32) for dims in tables],
        compiler_params=pltpu.CompilerParams(vmem_limit_bytes=16 << 20),
        name="smooth_one",
    )(data, notes, lists)
    grid, beta_one, hat_one, cand, fan, rates = pl.pallas_call(
        halo_kernel,
        out_shape=[
            shape(80, LANES), shape(2, PER, LANES), shape(2, PER, LANES), shape(640, LANES),
            shape(PER, 4 * LANES, LANES), shape(PER, LANES),
        ],
        in_specs=[VM] * 4,
        out_specs=[VM] * 6,
        scratch_shapes=[
            pltpu.VMEM((2, PER, LANES), F32),
            pltpu.VMEM((8, 8, LANES), F32),
            pltpu.VMEM((2, PER, LANES), F32),
            pltpu.VMEM((8, 8, LANES), F32),
            DMA((8,)),
            DMA((8,)),
        ],
        compiler_params=pltpu.CompilerParams(
            collective_id=1, has_side_effects=True, vmem_limit_bytes=16 << 20
        ),
        name="edges",
    )(weight_sums, pull_sums, data, notes)
    weight_sums, pull_sums = pl.pallas_call(
        second_kernel,
        out_shape=sums,
        in_specs=[VM] * 4 + [SM],
        out_specs=[VM] * 2,
        compiler_params=pltpu.CompilerParams(vmem_limit_bytes=16 << 20),
        name="smooth_two",
    )(cand, grid, fan, rates, lists)
    betas, hats, residual = pl.pallas_call(
        return_kernel,
        out_shape=[shape(2, NTILE * LANES), shape(2, NTILE * LANES), shape(NTILE, LANES)],
        in_specs=[VM] * 8,
        out_specs=[VM] * 3,
        scratch_shapes=[
            pltpu.VMEM((2, PER, LANES), F32),
            pltpu.VMEM((8, PER, LANES), F32),
            pltpu.VMEM((NTILE, PER, LANES), F32),
            pltpu.VMEM((8, PER, LANES), F32),
            pltpu.VMEM((8, PER, LANES), F32),
            DMA((NTILE,)),
            DMA((NTILE,)),
            DMA((8,)),
            DMA((8,)),
        ],
        compiler_params=pltpu.CompilerParams(collective_id=2, has_side_effects=True, vmem_limit_bytes=8 << 20),
        name="to_slots",
    )(beta_one, hat_one, weight_sums, pull_sums, data, notes, cells, home)
    betas, hats, residual = pl.pallas_call(
        store_kernel,
        out_shape=[shape(2, NTILE * LANES), shape(2, NTILE * LANES), shape(NTILE, LANES)],
        in_specs=[VM] * 3,
        out_specs=[HB] * 3,
        scratch_shapes=[DMA((3,))],
        compiler_params=pltpu.CompilerParams(vmem_limit_bytes=8 << 20),
        name="store",
    )(betas, hats, residual)
    return betas, hats, residual.reshape(-1)


def solution(mesh):
    split = ("region", "tile")
    in_specs = (
        P(None, split), P(None, split), P(split), P(split), P(split), P(None, split),
        P(None, split, None), P("region", "tile"),
    )
    out_specs = (P(None, split), P(None, split), P(split))
    return jax.shard_map(body, mesh=mesh, in_specs=in_specs, out_specs=out_specs, check_vma=False)
```

```python
import functools
import math

import jax
import jax.numpy as jnp
from jax import lax
from jax.experimental import pallas as pl
from jax.experimental.pallas import tpu as pltpu
from jax.sharding import PartitionSpec as P

TX = 4
LANES = 128
PER = 16
NPIECE = 13
CHUNK = 64
NREGION = 8
NTILE = 32
F32 = jnp.float32
BF16 = jnp.bfloat16


def split3(x):
    hi = x.astype(BF16).astype(F32)
    rest = x - hi
    mid = rest.astype(BF16).astype(F32)
    low = (rest - mid).astype(BF16).astype(F32)
    return hi, mid, low


def wide_split(x):
    hi, mid, low = split3(x)
    return jnp.concatenate([hi.astype(BF16), mid.astype(BF16), low.astype(BF16)], axis=1)


def join3(x):
    return x[:, :LANES] + x[:, LANES : 2 * LANES] + x[:, 2 * LANES :]


def remote(src, dst, send, recv, region, tile):
    return pltpu.make_async_remote_copy(
        src_ref=src,
        dst_ref=dst,
        send_sem=send,
        recv_sem=recv,
        device_id=(region, tile),
        device_id_type=pl.DeviceIdType.MESH,
    )


def signal(sem, region, tile):
    pl.semaphore_signal(sem, inc=1, device_id=(region, tile), device_id_type=pl.DeviceIdType.MESH)


def links(k):
    away = (0, 1, 2, 1)
    return away[k // 2 % 4] + away[k // 8 % 4] + k % 2 / 2


FAR_FIRST = sorted(range(1, NTILE), key=lambda k: -links(k))


def each(low, high, step):
    def turn(index, carry):
        step(index)
        return carry

    lax.fori_loop(low, high, turn, 0)


def walk(tile):
    turned = (tile // 8) * 8 + 6 - lax.rem(tile, 8) + 2 * lax.rem(tile, 2)
    return jnp.where(lax.rem(tile // 8, 2) == 1, turned, tile)


def gather_kernel(
    offsets_in, design_in, target_in, prior_in, counts_in, width_in, reach_in, cells_in,
    data_out, width_out, list_out, cells_out, home_out,
    offs, design, target, prior, counts, widths, reach, cells, notes, rows_of,
    wanted, stage, rbuf, msg, recv, load, send1, recv1, send2, recv2,
):
    region = lax.axis_index("region")
    tile = lax.axis_index("tile")
    group = tile // 16
    piece = lax.rem(tile, 16)
    up = lax.rem(region + 1, NREGION)
    down = lax.rem(region + NREGION - 1, NREGION)

    barrier = pltpu.get_barrier_semaphore()
    for k in range(15, -1, -1):
        signal(barrier, up, jnp.bitwise_xor(tile, k))
        signal(barrier, down, jnp.bitwise_xor(tile, k))
    for k in FAR_FIRST:
        signal(barrier, region, jnp.bitwise_xor(tile, k))

    loads = [
        pltpu.make_async_copy(source, place, load.at[k])
        for k, (source, place) in enumerate(
            (
                (counts_in, counts), (width_in, widths), (reach_in, reach), (cells_in, cells),
                (offsets_in, offs), (design_in, design), (target_in, target), (prior_in, prior),
            )
        )
    ]
    for copy in loads:
        copy.start()
    notes[...] = jnp.zeros((32, LANES), F32)
    stage[12] = jnp.zeros((24, LANES), F32)
    rows_of[...] = jnp.zeros((48, LANES), F32)
    for copy in loads[:4]:
        copy.wait()
    notes[0:1, 0:PER] = counts[...].astype(F32)
    notes[1:3, 0:PER] = widths[...].astype(F32)
    for e in range(9):
        for w in range(2):
            at = 3 + 9 * w + e
            notes[at : at + 1, 0:PER] = reach[e, w : w + 1, :].astype(F32)
    turned = jnp.transpose(notes[...])[0:PER]
    stage[12, 0:PER, 0:32] = turned
    cell = cells[...]
    order = (lax.bitwise_and(cell, 127) * TX + lax.shift_right_logical(cell, 7)).astype(F32)
    for k in range(8):
        notes[24:25, PER * k : PER * k + PER] = order
    row_lane = lax.broadcasted_iota(jnp.int32, (8, LANES), 1)
    cell_row = jnp.where(
        lax.shift_right_logical(row_lane, 4) == lax.rem(tile, 8),
        jnp.broadcast_to(notes[24:25, :], (8, LANES)), 0.0,
    )
    for p in range(NPIECE):
        stage[p, PER : PER + 8, :] = cell_row
    for copy in loads[4:]:
        copy.wait()
    lane = lax.broadcasted_iota(jnp.int32, (PER, LANES), 1)
    count = turned[:, 0:1]
    for t in range(PER):
        for h in range(2):
            span = slice(LANES * (2 * t + h), LANES * (2 * t + h + 1))
            for f in range(2):
                stage[2 * f + h, t : t + 1, :] = offs[f : f + 1, span]
                stage[4 + 4 * f + h, t : t + 1, :] = design[f : f + 1, span]
    for h in range(2):
        present = ((lane + LANES * h).astype(F32) < count).astype(F32)
        cov_one = stage[4 + h, 0:PER, :] * present
        cov_two = stage[8 + h, 0:PER, :]
        seen = target[pl.ds(h, PER, stride=2), :]
        before = prior[pl.ds(h, PER, stride=2), :]
        stage[4 + h, 0:PER, :] = cov_one
        stage[6 + h, 0:PER, :] = seen - cov_two * before
        cov_two = cov_two * present
        stage[8 + h, 0:PER, :] = cov_two
        stage[10 + h, 0:PER, :] = seen
        home_out[h] = cov_one
        home_out[2 + h] = cov_two
        home_out[4 + h] = seen * present

    pl.semaphore_wait(barrier, NTILE - 1 + 32)

    def to_middle(o):
        other = jnp.bitwise_xor(tile, o)
        held = jnp.minimum(lax.rem(other, 16), NPIECE - 1)
        return remote(
            stage.at[held, pl.ds(0, PER + 1)], rbuf.at[tile, pl.ds(0, PER + 1)],
            send1.at[o], recv1.at[tile], region, other,
        )

    for k in FAR_FIRST:
        to_middle(k).start()
    rbuf[tile] = stage[jnp.minimum(piece, NPIECE - 1)]

    number = lax.broadcasted_iota(jnp.int32, (640, LANES), 0)
    owner = lax.shift_right_logical(number * 205, 13)
    q = number - owner * 40
    turned_owner = 14 - lax.bitwise_and(owner, 7) + 2 * lax.bitwise_and(owner, 1)
    first = (group * 16 + jnp.where(owner < 8, owner, turned_owner)) * 16
    side = jnp.where(q < 32, q - 24, q - 32)
    base = jnp.where(q < 24, q - 4, (side - 1) * 4 + jnp.where(q < 32, 3, 0))
    open_up = jnp.where(region < NREGION - 1, 1, 0)
    open_down = jnp.where(region > 0, 1, 0)
    beside = jnp.where(side < 6, jnp.where(q < 32, open_up, open_down), 0)
    allowed = jnp.where(q < 24, 1, beside)
    cell = first + base
    wanted[...] = jnp.where(allowed > 0, cell, -1).astype(F32)

    def from_source(o):
        other = jnp.bitwise_xor(tile, o)
        return remote(
            stage.at[0, pl.ds(0, PER + 1)], rbuf.at[other, pl.ds(0, PER + 1)],
            send1.at[o], recv1.at[other], region, other,
        )

    each(1, NTILE, lambda o: from_source(o).wait_recv())

    cell_rows = [
        jnp.sum(rbuf[8 * b : 8 * b + 8, PER, :], axis=0, keepdims=True) for b in range(4)
    ]
    for b in range(4):
        cells_out[b : b + 1, :] = cell_rows[b]
    cells_out[4:8, :] = jnp.zeros((4, LANES), F32)

    @pl.when(piece < NPIECE)
    def _():
        spread = wide_split(rbuf[:, 0:PER, :].reshape(NTILE * PER, LANES))
        hot = jnp.concatenate(
            [jnp.where(wanted[...] == cell_rows[b], 1.0, 0.0).astype(BF16) for b in range(4)], axis=1
        )
        moved = join3(jnp.dot(hot, spread, preferred_element_type=F32))
        msg[...] = moved.reshape(16, 40, LANES)

    def own_copy(o):
        i = jnp.bitwise_xor(piece, o)
        return remote(
            msg.at[i, pl.ds(0, 24)], recv.at[piece, pl.ds(0, 24)],
            send2.at[0, o], recv2.at[0, piece], region, group * 16 + i,
        )

    def up_copy(i):
        return remote(
            msg.at[i, pl.ds(24, 8)], recv.at[piece, pl.ds(24, 8)],
            send2.at[1, i], recv2.at[1, piece], up, group * 16 + i,
        )

    def down_copy(i):
        return remote(
            msg.at[i, pl.ds(32, 8)], recv.at[piece, pl.ds(32, 8)],
            send2.at[2, i], recv2.at[2, piece], down, group * 16 + i,
        )

    @pl.when(piece < NPIECE)
    def _():
        for k in sorted(range(16), key=lambda k: -links(k)):
            up_copy(jnp.bitwise_xor(piece, k)).start()
            down_copy(jnp.bitwise_xor(piece, k)).start()
        for k in FAR_FIRST:
            if k < 16:
                own_copy(k).start()
        recv[piece, 0:24, :] = msg[piece, 0:24, :]

    def wait_own(p):
        @pl.when(p != piece)
        def _():
            remote(
                msg.at[0, pl.ds(0, 24)], recv.at[p, pl.ds(0, 24)],
                send2.at[0, 0], recv2.at[0, p], region, group * 16 + p,
            ).wait_recv()

    def wait_sides(p):
        remote(
            msg.at[0, pl.ds(24, 8)], recv.at[p, pl.ds(24, 8)],
            send2.at[1, 0], recv2.at[1, p], down, group * 16 + p,
        ).wait_recv()
        remote(
            msg.at[0, pl.ds(32, 8)], recv.at[p, pl.ds(32, 8)],
            send2.at[2, 0], recv2.at[2, p], up, group * 16 + p,
        ).wait_recv()

    each(0, NPIECE, wait_own)
    each(0, NPIECE, wait_sides)
    for p in range(12):
        data_out[p] = recv[p]
    width_out[...] = recv[12, 4:20, :]
    for r in range(6):
        rows_of[8 * r : 8 * r + 1, :] = recv[12, 24 + r : 25 + r, :]
        rows_of[8 * r + 1 : 8 * r + 5, :] = recv[12, 4 * r : 4 * r + 4, :]
        rows_of[8 * r + 5 : 8 * r + 6, :] = recv[12, 32 + r : 33 + r, :]

    def spread_lane(r, at):
        return jnp.broadcast_to(rows_of[8 * r : 8 * r + 8, at : at + 1], (8, LANES))

    lanes = lax.broadcasted_iota(jnp.int32, (8, LANES), 1)
    lanes_f = lanes.astype(F32)
    over = lax.broadcasted_iota(jnp.int32, (8, LANES), 0)
    filled = [spread_lane(r, 0) for r in range(6)]
    near = [
        [filled[r] if a == 1 else pltpu.roll(filled[r], (1 - a) % 8, 0) for a in range(3)]
        for r in range(6)
    ]
    for w in range(2):
        for r in range(1, 5):
            many = jnp.zeros((8, LANES), F32)
            todo = jnp.zeros((8, LANES), F32)
            for e in range(9):
                beside, beyond = e // 3, r + e % 3 - 1
                there = near[beyond][beside]
                keep = None if e == 4 else spread_lane(r, 3 + 9 * w + e)
                c = over + (beside - 1)
                t = jnp.where(c == 0, 24 + beyond, jnp.where(c == 5, 32 + beyond, beyond * 4 + c - 1))
                at = (8 * t).astype(F32)
                for h in range(2):
                    flag = jnp.where(there > LANES * h, 1.0 if keep is None else keep, 0.0)
                    todo = todo + jnp.where(many == lanes_f, flag * (at + 320.0 * h), 0.0)
                    many = many + flag
            chunks = lax.shift_right_logical(filled[r].astype(jnp.int32) + CHUNK - 1, CHUNK.bit_length() - 1)
            value = jnp.where(lanes_f < many, todo, 240.0).astype(jnp.int32)
            groups = lax.shift_right_logical((many.astype(jnp.int32) + 2) * 11, 5)
            value = jnp.where(lanes == 24, groups, value)
            value = jnp.where(lanes == 25, chunks, value)
            value = jnp.where(lanes == 26, filled[r].astype(jnp.int32), value)
            list_out[w, 8 * r - 8 : 8 * r, :] = value

    each(1, NTILE, lambda o: to_middle(o).wait_send())

    @pl.when(piece < NPIECE)
    def _():
        each(1, 16, lambda o: own_copy(o).wait_send())
        each(0, 16, lambda i: up_copy(i).wait_send())
        each(0, 16, lambda i: down_copy(i).wait_send())


def rate_of(which, notes):
    width = notes[:, 1 + which : 2 + which]
    return jnp.broadcast_to((32.0 * math.log2(math.e)) / (width * width), (PER, LANES))


def prepare(which, data, notes, cand, fan, rates):
    rate = rate_of(which, notes)
    rates[0:PER, :] = -rate
    number = lax.broadcasted_iota(jnp.int32, (PER, LANES), 0)
    rates[PER : 2 * PER, :] = (lax.bitwise_and(number, 3) + 1).astype(F32)
    rates[2 * PER : 3 * PER, :] = (lax.shift_right_logical(number, 2) + 1).astype(F32)
    slot = lax.broadcasted_iota(jnp.int32, (40, LANES), 0)
    col = jnp.where(slot < 24, lax.rem(slot, 4) + 1, jnp.where(slot < 32, 0, 5)).astype(F32)
    row = jnp.where(
        slot < 24, slot // 4, jnp.where(slot < 32, slot - 24, slot - 32)
    ).astype(F32)
    columns = []
    for h in range(2):
        x = data[h] - 0.5
        y = data[2 + h] - 0.5
        cov = data[4 + 4 * which + h]
        for k, field in enumerate((x + col, y + row, cov * cov)):
            cand[pl.ds(320 * h + k, 40, stride=8), :] = field
        along, upward = [
            jnp.transpose(jnp.concatenate(split3(2.0 * rate * source), axis=0)).astype(BF16)
            for source in (x[4:20], y[4:20])
        ]
        for low in range(0, LANES, CHUNK):
            columns += [along[low : low + CHUNK], upward[low : low + CHUNK]]
    columns = jnp.concatenate(columns, axis=0)
    which_row = lax.bitwise_and(lax.broadcasted_iota(jnp.int32, (3 * PER, LANES), 0), PER - 1)
    for i in range(PER):
        pick = jnp.where(which_row == i, 1.0, 0.0).astype(BF16)
        fan[4 * LANES * i : 4 * LANES * (i + 1), :] = jnp.dot(
            columns, pick, preferred_element_type=F32
        )


def sums_of(which, cand, pull, fan, rates, lists, weight_sums, pull_sums):
    def line(i):
        return lax.shift_right_logical(i, 2) * 8 + lax.bitwise_and(i, 3) + 1

    total = jnp.int32(0)
    for i in range(PER):
        at = 8 * (i // 4) + i % 4 + 1
        total = total + lists[which, at, 24] * lists[which, at, 25]

    shape3 = (CHUNK // 8, 8, LANES)
    spare = PER * 2 * LANES

    def row(ref, at):
        return jnp.broadcast_to(ref[pl.ds(at, 1), :], (8, LANES))

    def rows(ref, at):
        return ref[pl.ds(pl.multiple_of(at, CHUNK), CHUNK), :].reshape(shape3)

    for ref in (weight_sums, pull_sums):
        ref[spare : spare + CHUNK, :] = jnp.zeros((CHUNK, LANES), F32)

    def item(n, carry):
        i, k, j, out, at, groups, chunks, old_from, old_out, old_at, fars, powers = carry
        x = [row(cand, base) - row(rates, PER + i) for base in at]
        y = [row(cand, base + 1) - row(rates, 2 * PER + i) for base in at]
        scale = row(rates, i)
        u = rows(fan, 2 * out)
        v = rows(fan, 2 * out + CHUNK)

        weight_sum = rows(weight_sums, old_from)
        pull_sum = rows(pull_sums, old_from)
        for base, far, power in zip(old_at, fars, powers):
            factor = jnp.exp2(far)
            weight = jnp.exp2(power)
            weight_sum = weight_sum + weight * (factor * row(cand, base + 2))
            pull_sum = pull_sum + weight * (factor * row(pull, lax.shift_right_logical(base, 3)))
        place = pl.ds(pl.multiple_of(old_out, CHUNK), CHUNK)
        weight_sums[place, :] = weight_sum.reshape(CHUNK, LANES)
        pull_sums[place, :] = pull_sum.reshape(CHUNK, LANES)

        fars = tuple((x[g] * x[g] + y[g] * y[g]) * scale for g in range(3))
        powers = tuple(u * x[g] + v * y[g] for g in range(3))
        last = j + 1 == groups
        end = last & (k + 1 == chunks)
        next_j = jnp.where(last, 0, j + 1)
        next_k = jnp.where(end, 0, jnp.where(last, k + 1, k))
        next_i = jnp.minimum(jnp.where(end, i + 1, i), PER - 1)
        next_out = next_i * (2 * LANES) + next_k * CHUNK
        here = line(next_i)
        return (
            next_i, next_k, next_j, next_out,
            tuple(lists[which, here, 3 * next_j + g] for g in range(3)),
            lists[which, here, 24], lists[which, here, 25],
            jnp.where(j == 0, spare, out), out, at, fars, powers,
        )

    zero = rows(fan, 0) * 0.0
    none = row(rates, 0) * 0.0
    begin = jnp.int32(0)
    lax.fori_loop(
        0, total + 1, item,
        (
            begin, begin, begin, begin, tuple(lists[which, 1, g] for g in range(3)),
            lists[which, 1, 24], lists[which, 1, 25],
            jnp.int32(spare), begin, (begin,) * 3, (none,) * 3, (zero,) * 3,
        ),
    )


def first_kernel(data, notes, lists, weight_sums, pull_sums, cand, pull, fan, rates):
    prepare(0, data, notes, cand, fan, rates)
    for h in range(2):
        pull[40 * h : 40 * h + 40, :] = data[4 + h] * data[6 + h]
    sums_of(0, cand, pull, fan, rates, lists, weight_sums, pull_sums)


def second_kernel(cand, pull, fan, rates, lists, weight_sums, pull_sums):
    sums_of(1, cand, pull, fan, rates, lists, weight_sums, pull_sums)


def finish(which, h, data, notes, weight_sums, pull_sums, totals):
    ones = jnp.ones((8, LANES), BF16)
    for k, ref in enumerate((weight_sums, pull_sums)):
        for i in range(PER):
            values = ref[LANES * (2 * i + h) : LANES * (2 * i + h + 1), :]
            high = values.astype(BF16)
            low = (values - high.astype(F32)).astype(BF16)
            both = jnp.concatenate([high, low], axis=0)
            sums = lax.dot_general(
                ones, both, (((1,), (1,)), ((), ())), preferred_element_type=F32
            )
            totals[k, i : i + 1, :] = sums[0:1, :LANES] + sums[0:1, LANES:]
    x = data[h, 4:20, :] - 0.5
    y = data[2 + h, 4:20, :] - 0.5
    cov = data[4 + 4 * which + h, 4:20, :]
    fade = jnp.exp2(-rate_of(which, notes) * (x * x + y * y))
    lane = lax.broadcasted_iota(jnp.int32, (PER, LANES), 1)
    live = (lane + LANES * h).astype(F32) < notes[:, 0:1]
    total = 1.0 + fade * totals[0]
    beta = jnp.where(live, fade * totals[1] / total, 0.0)
    return beta, jnp.where(live, cov * cov / total, 0.0)


def edge_cells(a, b):
    cols = range(4) if a == 0 else (0 if a == -1 else 3,)
    rows = range(4) if b == 0 else (0 if b == -1 else 3,)
    return [4 * r + c for r in rows for c in cols]


def halo_kernel(
    weight_sums, pull_sums, data, notes, grid_out, beta_out, hat_out, cand_out, fan_out, rates_out,
    own, edge, totals, recv, send, land,
):
    region = lax.axis_index("region")
    tile = lax.axis_index("tile")
    steps = [(a, b) for a in (-1, 0, 1) for b in (-1, 0, 1) if (a, b) != (0, 0)]

    owner = walk(tile)

    def place(a, b):
        return lax.rem(region + a + NREGION, NREGION), walk(lax.rem(owner + b + NTILE, NTILE))

    barrier = pltpu.get_barrier_semaphore()
    for a, b in steps:
        signal(barrier, *place(a, b))
    for h in range(2):
        beta, hat = finish(0, h, data, notes, weight_sums, pull_sums, totals)
        beta_out[h] = beta
        hat_out[h] = hat
        own[h] = data[8 + h, 4:20, :] * (data[10 + h, 4:20, :] - data[4 + h, 4:20, :] * beta)
    edge[...] = jnp.zeros((8, 8, LANES), F32)
    for k, (a, b) in enumerate(steps):
        for h in range(2):
            for n, i in enumerate(edge_cells(a, b)):
                edge[k, 4 * h + n : 4 * h + n + 1, :] = own[h, i : i + 1, :]
    pl.semaphore_wait(barrier, 8)
    copies = []
    for k, (a, b) in enumerate(steps):
        copies.append(remote(edge.at[k], recv.at[7 - k], send.at[k], land.at[7 - k], *place(a, b)))
    for copy in copies:
        copy.start()
    prepare(1, data, notes, cand_out, fan_out, rates_out)
    for copy in copies:
        copy.wait_recv()
    fits = {-1: region > 0, 0: None, 1: region < NREGION - 1}
    fits_row = {-1: owner > 0, 0: None, 1: owner < NTILE - 1}
    for h in range(2):
        to = 40 * h
        grid_out[to + 4 : to + 20, :] = own[h]
        for first in (to + 30, to + 38):
            grid_out[first : first + 2, :] = jnp.zeros((2, LANES), F32)
        for k, (a, b) in enumerate(steps):
            many = len(edge_cells(-a, -b))
            rows = recv[k, 4 * h : 4 * h + many, :]
            for fit in (fits[a], fits_row[b]):
                if fit is not None:
                    rows = jnp.where(fit, rows, 0.0)
            if a == 0:
                first = to + (0 if b == -1 else 20)
            else:
                first = to + (24 if a == -1 else 32) + (0, 1, 5)[b + 1]
            grid_out[first : first + many, :] = rows
    for copy in copies:
        copy.wait_send()


def return_kernel(
    beta_one, hat_one, weight_sums, pull_sums, data, notes, cells, home, betas, hats, residual,
    totals, stage, rbuf, msg, recv, send1, recv1, send2, recv2,
):
    region = lax.axis_index("region")
    tile = lax.axis_index("tile")
    group = tile // 8
    piece = lax.rem(tile, 8)
    barrier = pltpu.get_barrier_semaphore()
    for k in FAR_FIRST:
        signal(barrier, region, jnp.bitwise_xor(tile, k))
    for h in range(2):
        stage[h] = beta_one[h]
        stage[2 + h] = hat_one[h]
        stage[4 + h], stage[6 + h] = finish(1, h, data, notes, weight_sums, pull_sums, totals)
    pl.semaphore_wait(barrier, NTILE - 1)

    def to_middle(o):
        other = jnp.bitwise_xor(tile, o)
        return remote(
            stage.at[lax.rem(other, 8)], rbuf.at[tile], send1.at[o], recv1.at[tile], region, other
        )

    for k in FAR_FIRST:
        to_middle(k).start()
    rbuf[tile] = stage[piece]

    row = cells[pl.ds(group, 1), :]
    column = jnp.transpose(jnp.broadcast_to(row, (LANES, LANES)))
    lane = lax.broadcasted_iota(jnp.int32, (LANES, LANES), 1)
    hots = []
    for b in range(4):
        of = lax.shift_right_logical(lane, 4)
        if b % 2 == 1:
            of = 6 - of + 2 * lax.bitwise_and(of, 1)
        here = LANES * b + of * PER + lax.bitwise_and(lane, PER - 1)
        hots.append(jnp.where(here.astype(F32) == column, 1.0, 0.0).astype(BF16))
    hot = jnp.concatenate(hots, axis=1)

    def from_source(o):
        other = jnp.bitwise_xor(tile, o)
        return remote(stage.at[0], rbuf.at[other], send1.at[o], recv1.at[other], region, other)

    each(1, NTILE, lambda o: from_source(o).wait_recv())
    spread = wide_split(rbuf[...].reshape(NTILE * PER, LANES))
    msg[...] = join3(jnp.dot(hot, spread, preferred_element_type=F32)).reshape(8, PER, LANES)

    def home_copy(o):
        i = jnp.bitwise_xor(piece, o)
        return remote(
            msg.at[i], recv.at[piece], send2.at[o], recv2.at[piece], region, group * 8 + i
        )

    for k in FAR_FIRST:
        if k < 8:
            home_copy(k).start()
    recv[piece] = msg[piece]

    def from_middle(o):
        p = jnp.bitwise_xor(piece, o)
        return remote(msg.at[0], recv.at[p], send2.at[o], recv2.at[p], region, group * 8 + p)

    each(1, 8, lambda o: from_middle(o).wait_recv())
    for h in range(2):
        left = home[4 + h] - home[h] * recv[h] - home[2 + h] * recv[4 + h]
        residual[pl.ds(h, PER, stride=2), :] = left
        for t in range(PER):
            span = slice(LANES * (2 * t + h), LANES * (2 * t + h + 1))
            for f in range(2):
                betas[f : f + 1, span] = recv[4 * f + h, t : t + 1, :]
                hats[f : f + 1, span] = recv[2 + 4 * f + h, t : t + 1, :]
    each(1, NTILE, lambda o: to_middle(o).wait_send())
    each(1, 8, lambda o: home_copy(o).wait_send())


def store_kernel(betas, hats, residual, betas_out, hats_out, residual_out, done):
    pairs = ((betas, betas_out), (hats, hats_out), (residual, residual_out))
    copies = [pltpu.make_async_copy(a, b, done.at[k]) for k, (a, b) in enumerate(pairs)]
    for copy in copies:
        copy.start()
    for copy in copies:
        copy.wait()


VM = pl.BlockSpec(memory_space=pltpu.VMEM)
SM = pl.BlockSpec(memory_space=pltpu.SMEM)
HB = pl.BlockSpec(memory_space=pltpu.HBM)
DMA = pltpu.SemaphoreType.DMA


def shape(*dims, dtype=F32):
    return jax.ShapeDtypeStruct(dims, dtype)


def body(offsets, design, target, beta_second, counts, kernel_width, reach, assignment):
    data, notes, lists, cells, home = pl.pallas_call(
        gather_kernel,
        out_shape=[
            shape(12, 40, LANES), shape(PER, LANES), shape(2, 32, LANES, dtype=jnp.int32),
            shape(8, LANES), shape(6, PER, LANES),
        ],
        in_specs=[HB] * 8,
        out_specs=[VM] * 5,
        scratch_shapes=[
            pltpu.VMEM((2, NTILE * LANES), F32),
            pltpu.VMEM((2, NTILE * LANES), F32),
            pltpu.VMEM((NTILE, LANES), F32),
            pltpu.VMEM((NTILE, LANES), F32),
            pltpu.VMEM((1, PER), jnp.int32),
            pltpu.VMEM((2, PER), jnp.int32),
            pltpu.VMEM((9, 2, PER), jnp.int32),
            pltpu.VMEM((1, PER), jnp.int32),
            pltpu.VMEM((32, LANES), F32),
            pltpu.VMEM((48, LANES), F32),
            pltpu.VMEM((640, LANES), F32),
            pltpu.VMEM((NPIECE, 24, LANES), F32),
            pltpu.VMEM((NTILE, 24, LANES), F32),
            pltpu.VMEM((16, 40, LANES), F32),
            pltpu.VMEM((NPIECE, 40, LANES), F32),
            DMA((8,)),
            DMA((NTILE,)),
            DMA((NTILE,)),
            DMA((3, 16)),
            DMA((3, 16)),
        ],
        compiler_params=pltpu.CompilerParams(collective_id=0, has_side_effects=True, vmem_limit_bytes=8 << 20),
        name="to_owners",
    )(
        *(
            pltpu.with_memory_space_constraint(value, pltpu.HBM)
            for value in (
                offsets, design, target.reshape(NTILE, LANES), beta_second.reshape(NTILE, LANES),
                counts.reshape(1, PER), kernel_width, reach.transpose(2, 0, 1), assignment,
            )
        )
    )
    sums = [shape((PER + 1) * 2 * LANES, LANES)] * 2
    tables = [(640, LANES), (80, LANES), (PER * 4 * LANES, LANES), (3 * PER, LANES)]
    weight_sums, pull_sums = pl.pallas_call(
        first_kernel,
        out_shape=sums,
        in_specs=[VM, VM, SM],
        out_specs=[VM] * 2,
        scratch_shapes=[pltpu.VMEM(dims, F32) for dims in tables],
        compiler_params=pltpu.CompilerParams(vmem_limit_bytes=16 << 20),
        name="smooth_one",
    )(data, notes, lists)
    grid, beta_one, hat_one, cand, fan, rates = pl.pallas_call(
        halo_kernel,
        out_shape=[
            shape(80, LANES), shape(2, PER, LANES), shape(2, PER, LANES), shape(640, LANES),
            shape(PER * 4 * LANES, LANES), shape(3 * PER, LANES),
        ],
        in_specs=[VM] * 4,
        out_specs=[VM] * 6,
        scratch_shapes=[
            pltpu.VMEM((2, PER, LANES), F32),
            pltpu.VMEM((8, 8, LANES), F32),
            pltpu.VMEM((2, PER, LANES), F32),
            pltpu.VMEM((8, 8, LANES), F32),
            DMA((8,)),
            DMA((8,)),
        ],
        compiler_params=pltpu.CompilerParams(
            collective_id=1, has_side_effects=True, vmem_limit_bytes=16 << 20
        ),
        name="edges",
    )(weight_sums, pull_sums, data, notes)
    weight_sums, pull_sums = pl.pallas_call(
        second_kernel,
        out_shape=sums,
        in_specs=[VM] * 4 + [SM],
        out_specs=[VM] * 2,
        compiler_params=pltpu.CompilerParams(vmem_limit_bytes=16 << 20),
        name="smooth_two",
    )(cand, grid, fan, rates, lists)
    betas, hats, residual = pl.pallas_call(
        return_kernel,
        out_shape=[shape(2, NTILE * LANES), shape(2, NTILE * LANES), shape(NTILE, LANES)],
        in_specs=[VM] * 8,
        out_specs=[VM] * 3,
        scratch_shapes=[
            pltpu.VMEM((2, PER, LANES), F32),
            pltpu.VMEM((8, PER, LANES), F32),
            pltpu.VMEM((NTILE, PER, LANES), F32),
            pltpu.VMEM((8, PER, LANES), F32),
            pltpu.VMEM((8, PER, LANES), F32),
            DMA((NTILE,)),
            DMA((NTILE,)),
            DMA((8,)),
            DMA((8,)),
        ],
        compiler_params=pltpu.CompilerParams(collective_id=2, has_side_effects=True, vmem_limit_bytes=8 << 20),
        name="to_slots",
    )(beta_one, hat_one, weight_sums, pull_sums, data, notes, cells, home)
    betas, hats, residual = pl.pallas_call(
        store_kernel,
        out_shape=[shape(2, NTILE * LANES), shape(2, NTILE * LANES), shape(NTILE, LANES)],
        in_specs=[VM] * 3,
        out_specs=[HB] * 3,
        scratch_shapes=[DMA((3,))],
        compiler_params=pltpu.CompilerParams(vmem_limit_bytes=8 << 20),
        name="store",
    )(betas, hats, residual)
    return betas, hats, residual.reshape(-1)


def solution(mesh):
    split = ("region", "tile")
    in_specs = (
        P(None, split), P(None, split), P(split), P(split), P(split), P(None, split),
        P(None, split, None), P("region", "tile"),
    )
    out_specs = (P(None, split), P(None, split), P(split))
    return jax.shard_map(body, mesh=mesh, in_specs=in_specs, out_specs=out_specs, check_vma=False)
```

```python
import functools
import math

import jax
import jax.numpy as jnp
from jax import lax
from jax.experimental import pallas as pl
from jax.experimental.pallas import tpu as pltpu
from jax.sharding import PartitionSpec as P

TX = 4
LANES = 128
PER = 16
NPIECE = 13
CHUNK = 64
SHARE = (4, 1, 7, 3, 5, 0, 8)
NREGION = 8
NTILE = 32
F32 = jnp.float32
BF16 = jnp.bfloat16


def split3(x):
    hi = x.astype(BF16).astype(F32)
    rest = x - hi
    mid = rest.astype(BF16).astype(F32)
    low = (rest - mid).astype(BF16).astype(F32)
    return hi, mid, low


def wide_split(x):
    hi, mid, low = split3(x)
    return jnp.concatenate([hi.astype(BF16), mid.astype(BF16), low.astype(BF16)], axis=1)


def join3(x):
    return x[:, :LANES] + x[:, LANES : 2 * LANES] + x[:, 2 * LANES :]


def remote(src, dst, send, recv, region, tile):
    return pltpu.make_async_remote_copy(
        src_ref=src,
        dst_ref=dst,
        send_sem=send,
        recv_sem=recv,
        device_id=(region, tile),
        device_id_type=pl.DeviceIdType.MESH,
    )


def signal(sem, region, tile):
    pl.semaphore_signal(sem, inc=1, device_id=(region, tile), device_id_type=pl.DeviceIdType.MESH)


def links(k):
    away = (0, 1, 2, 1)
    return away[k // 2 % 4] + away[k // 8 % 4] + k % 2 / 2


FAR_FIRST = sorted(range(1, NTILE), key=lambda k: -links(k))


def each(low, high, step):
    def turn(index, carry):
        step(index)
        return carry

    lax.fori_loop(low, high, turn, 0)


def walk(tile):
    turned = (tile // 8) * 8 + 6 - lax.rem(tile, 8) + 2 * lax.rem(tile, 2)
    return jnp.where(lax.rem(tile // 8, 2) == 1, turned, tile)


def gather_kernel(
    offsets_in, design_in, target_in, prior_in, counts_in, width_in, reach_in, cells_in,
    data_out, width_out, list_out, cells_out, home_out,
    offs, design, target, prior, counts, widths, reach, cells, notes, rows_of,
    wanted, stage, rbuf, msg, recv, load, send1, recv1, send2, recv2,
):
    region = lax.axis_index("region")
    tile = lax.axis_index("tile")
    group = tile // 16
    piece = lax.rem(tile, 16)
    up = lax.rem(region + 1, NREGION)
    down = lax.rem(region + NREGION - 1, NREGION)

    barrier = pltpu.get_barrier_semaphore()
    for k in range(15, -1, -1):
        signal(barrier, up, jnp.bitwise_xor(tile, k))
        signal(barrier, down, jnp.bitwise_xor(tile, k))
    for k in FAR_FIRST:
        signal(barrier, region, jnp.bitwise_xor(tile, k))

    loads = [
        pltpu.make_async_copy(source, place, load.at[k])
        for k, (source, place) in enumerate(
            (
                (counts_in, counts), (width_in, widths), (reach_in, reach), (cells_in, cells),
                (offsets_in, offs), (design_in, design), (target_in, target), (prior_in, prior),
            )
        )
    ]
    for copy in loads:
        copy.start()
    notes[...] = jnp.zeros((32, LANES), F32)
    stage[12] = jnp.zeros((24, LANES), F32)
    rows_of[...] = jnp.zeros((48, LANES), F32)
    for copy in loads[:4]:
        copy.wait()
    notes[0:1, 0:PER] = counts[...].astype(F32)
    notes[1:3, 0:PER] = widths[...].astype(F32)
    for e in range(9):
        for w in range(2):
            at = 3 + 9 * w + e
            notes[at : at + 1, 0:PER] = reach[e, w : w + 1, :].astype(F32)
    turned = jnp.transpose(notes[...])[0:PER]
    stage[12, 0:PER, 0:32] = turned
    cell = cells[...]
    order = (lax.bitwise_and(cell, 127) * TX + lax.shift_right_logical(cell, 7)).astype(F32)
    for k in range(8):
        notes[24:25, PER * k : PER * k + PER] = order
    row_lane = lax.broadcasted_iota(jnp.int32, (8, LANES), 1)
    cell_row = jnp.where(
        lax.shift_right_logical(row_lane, 4) == lax.rem(tile, 8),
        jnp.broadcast_to(notes[24:25, :], (8, LANES)), 0.0,
    )
    for p in range(NPIECE):
        stage[p, PER : PER + 8, :] = cell_row
    for copy in loads[4:]:
        copy.wait()
    lane = lax.broadcasted_iota(jnp.int32, (PER, LANES), 1)
    count = turned[:, 0:1]
    for t in range(PER):
        for h in range(2):
            span = slice(LANES * (2 * t + h), LANES * (2 * t + h + 1))
            for f in range(2):
                stage[2 * f + h, t : t + 1, :] = offs[f : f + 1, span]
                stage[4 + 4 * f + h, t : t + 1, :] = design[f : f + 1, span]
    for h in range(2):
        present = ((lane + LANES * h).astype(F32) < count).astype(F32)
        cov_one = stage[4 + h, 0:PER, :] * present
        cov_two = stage[8 + h, 0:PER, :]
        seen = target[pl.ds(h, PER, stride=2), :]
        before = prior[pl.ds(h, PER, stride=2), :]
        stage[4 + h, 0:PER, :] = cov_one
        stage[6 + h, 0:PER, :] = seen - cov_two * before
        cov_two = cov_two * present
        stage[8 + h, 0:PER, :] = cov_two
        stage[10 + h, 0:PER, :] = seen
        home_out[h] = cov_one
        home_out[2 + h] = cov_two
        home_out[4 + h] = seen * present

    pl.semaphore_wait(barrier, NTILE - 1 + 32)

    def to_middle(o):
        other = jnp.bitwise_xor(tile, o)
        held = jnp.minimum(lax.rem(other, 16), NPIECE - 1)
        return remote(
            stage.at[held, pl.ds(0, PER + 1)], rbuf.at[tile, pl.ds(0, PER + 1)],
            send1.at[o], recv1.at[tile], region, other,
        )

    for k in FAR_FIRST:
        to_middle(k).start()
    rbuf[tile] = stage[jnp.minimum(piece, NPIECE - 1)]

    number = lax.broadcasted_iota(jnp.int32, (640, LANES), 0)
    owner = lax.shift_right_logical(number * 205, 13)
    q = number - owner * 40
    turned_owner = 14 - lax.bitwise_and(owner, 7) + 2 * lax.bitwise_and(owner, 1)
    first = (group * 16 + jnp.where(owner < 8, owner, turned_owner)) * 16
    side = jnp.where(q < 32, q - 24, q - 32)
    base = jnp.where(q < 24, q - 4, (side - 1) * 4 + jnp.where(q < 32, 3, 0))
    open_up = jnp.where(region < NREGION - 1, 1, 0)
    open_down = jnp.where(region > 0, 1, 0)
    beside = jnp.where(side < 6, jnp.where(q < 32, open_up, open_down), 0)
    allowed = jnp.where(q < 24, 1, beside)
    cell = first + base
    wanted[...] = jnp.where(allowed > 0, cell, -1).astype(F32)

    def from_source(o):
        other = jnp.bitwise_xor(tile, o)
        return remote(
            stage.at[0, pl.ds(0, PER + 1)], rbuf.at[other, pl.ds(0, PER + 1)],
            send1.at[o], recv1.at[other], region, other,
        )

    each(1, NTILE, lambda o: from_source(o).wait_recv())

    cell_rows = [
        jnp.sum(rbuf[8 * b : 8 * b + 8, PER, :], axis=0, keepdims=True) for b in range(4)
    ]
    for b in range(4):
        cells_out[b : b + 1, :] = cell_rows[b]
    cells_out[4:8, :] = jnp.zeros((4, LANES), F32)

    @pl.when(piece < NPIECE)
    def _():
        spread = wide_split(rbuf[:, 0:PER, :].reshape(NTILE * PER, LANES))
        hot = jnp.concatenate(
            [jnp.where(wanted[...] == cell_rows[b], 1.0, 0.0).astype(BF16) for b in range(4)], axis=1
        )
        moved = join3(jnp.dot(hot, spread, preferred_element_type=F32))
        msg[...] = moved.reshape(16, 40, LANES)

    def own_copy(o):
        i = jnp.bitwise_xor(piece, o)
        return remote(
            msg.at[i, pl.ds(0, 24)], recv.at[piece, pl.ds(0, 24)],
            send2.at[0, o], recv2.at[0, piece], region, group * 16 + i,
        )

    def up_copy(i):
        return remote(
            msg.at[i, pl.ds(24, 8)], recv.at[piece, pl.ds(24, 8)],
            send2.at[1, i], recv2.at[1, piece], up, group * 16 + i,
        )

    def down_copy(i):
        return remote(
            msg.at[i, pl.ds(32, 8)], recv.at[piece, pl.ds(32, 8)],
            send2.at[2, i], recv2.at[2, piece], down, group * 16 + i,
        )

    @pl.when(piece < NPIECE)
    def _():
        for k in sorted(range(16), key=lambda k: -links(k)):
            up_copy(jnp.bitwise_xor(piece, k)).start()
            down_copy(jnp.bitwise_xor(piece, k)).start()
        for k in FAR_FIRST:
            if k < 16:
                own_copy(k).start()
        recv[piece, 0:24, :] = msg[piece, 0:24, :]

    def wait_own(p):
        @pl.when(p != piece)
        def _():
            remote(
                msg.at[0, pl.ds(0, 24)], recv.at[p, pl.ds(0, 24)],
                send2.at[0, 0], recv2.at[0, p], region, group * 16 + p,
            ).wait_recv()

    def wait_sides(p):
        remote(
            msg.at[0, pl.ds(24, 8)], recv.at[p, pl.ds(24, 8)],
            send2.at[1, 0], recv2.at[1, p], down, group * 16 + p,
        ).wait_recv()
        remote(
            msg.at[0, pl.ds(32, 8)], recv.at[p, pl.ds(32, 8)],
            send2.at[2, 0], recv2.at[2, p], up, group * 16 + p,
        ).wait_recv()

    each(0, NPIECE, wait_own)
    each(0, NPIECE, wait_sides)
    for p in range(12):
        data_out[p] = recv[p]
    width_out[...] = recv[12, 4:20, :]
    for r in range(6):
        rows_of[8 * r : 8 * r + 1, :] = recv[12, 24 + r : 25 + r, :]
        rows_of[8 * r + 1 : 8 * r + 5, :] = recv[12, 4 * r : 4 * r + 4, :]
        rows_of[8 * r + 5 : 8 * r + 6, :] = recv[12, 32 + r : 33 + r, :]

    def spread_lane(r, at):
        return jnp.broadcast_to(rows_of[8 * r : 8 * r + 8, at : at + 1], (8, LANES))

    lanes = lax.broadcasted_iota(jnp.int32, (8, LANES), 1)
    spots = lax.bitwise_and(lanes, 31)
    spots_f = spots.astype(F32)
    over = lax.broadcasted_iota(jnp.int32, (8, LANES), 0)
    filled = [spread_lane(r, 0) for r in range(6)]
    near = [
        [filled[r] if a == 1 else pltpu.roll(filled[r], (1 - a) % 8, 0) for a in range(3)]
        for r in range(6)
    ]
    for w, skipped, number in ((0, (), 0), (1, (), 1), (1, SHARE, 2)):
        for r in range(1, 5):
            many = jnp.zeros((8, LANES), F32)
            todo = jnp.zeros((8, LANES), F32)
            for e in range(9):
                beside, beyond = e // 3, r + e % 3 - 1
                there = near[beyond][beside]
                keep = None if e == 4 else spread_lane(r, 3 + 9 * w + e)
                c = over + (beside - 1)
                t = jnp.where(c == 0, 24 + beyond, jnp.where(c == 5, 32 + beyond, beyond * 4 + c - 1))
                at = (8 * t).astype(F32)
                for h in range(1 if e in skipped else 0, 2):
                    flag = jnp.where(there > LANES * h, 1.0 if keep is None else keep, 0.0)
                    todo = todo + jnp.where(many == spots_f, flag * (at + 320.0 * h), 0.0)
                    many = many + flag
            chunks = lax.shift_right_logical(filled[r].astype(jnp.int32) + CHUNK - 1, CHUNK.bit_length() - 1)
            value = jnp.where(spots_f < many, todo, 240.0).astype(jnp.int32)
            groups = lax.shift_right_logical((many.astype(jnp.int32) + 2) * 11, 5)
            groups = jnp.maximum(groups, 1)
            value = jnp.where(spots == 24, groups, value)
            value = jnp.where(spots == 25, chunks, value)
            value = jnp.where(spots == 26, filled[r].astype(jnp.int32), value)
            band = value if r == 1 else jnp.where(lax.shift_right_logical(lanes, 5) == r - 1, value, band)
        list_out[number] = band

    each(1, NTILE, lambda o: to_middle(o).wait_send())

    @pl.when(piece < NPIECE)
    def _():
        each(1, 16, lambda o: own_copy(o).wait_send())
        each(0, 16, lambda i: up_copy(i).wait_send())
        each(0, 16, lambda i: down_copy(i).wait_send())


def rate_of(which, notes):
    width = notes[:, 1 + which : 2 + which]
    return jnp.broadcast_to((32.0 * math.log2(math.e)) / (width * width), (PER, LANES))


def prepare(which, data, notes, cand, fan, rates):
    rate = rate_of(which, notes)
    rates[0:PER, :] = -rate
    number = lax.broadcasted_iota(jnp.int32, (PER, LANES), 0)
    rates[PER : 2 * PER, :] = (lax.bitwise_and(number, 3) + 1).astype(F32)
    rates[2 * PER : 3 * PER, :] = (lax.shift_right_logical(number, 2) + 1).astype(F32)
    slot = lax.broadcasted_iota(jnp.int32, (40, LANES), 0)
    col = jnp.where(slot < 24, lax.rem(slot, 4) + 1, jnp.where(slot < 32, 0, 5)).astype(F32)
    row = jnp.where(
        slot < 24, slot // 4, jnp.where(slot < 32, slot - 24, slot - 32)
    ).astype(F32)
    columns = []
    for h in range(2):
        x = data[h] - 0.5
        y = data[2 + h] - 0.5
        cov = data[4 + 4 * which + h]
        for k, field in enumerate((x + col, y + row, cov * cov)):
            cand[pl.ds(320 * h + k, 40, stride=8), :] = field
        along, upward = [
            jnp.transpose(jnp.concatenate(split3(2.0 * rate * source), axis=0)).astype(BF16)
            for source in (x[4:20], y[4:20])
        ]
        for low in range(0, LANES, CHUNK):
            columns += [along[low : low + CHUNK], upward[low : low + CHUNK]]
    columns = jnp.concatenate(columns, axis=0)
    which_row = lax.bitwise_and(lax.broadcasted_iota(jnp.int32, (3 * PER, LANES), 0), PER - 1)
    for i in range(PER):
        pick = jnp.where(which_row == i, 1.0, 0.0).astype(BF16)
        fan[4 * LANES * i : 4 * LANES * (i + 1), :] = jnp.dot(
            columns, pick, preferred_element_type=F32
        )


def sums_of(which, cand, pull, fan, rates, lists, weight_sums, pull_sums):
    def listed(kind, i, at):
        band = lax.shift_right_logical(i, 2) * 32
        return lists[kind, lax.bitwise_and(i, 3) + 1, band + at]

    total = jnp.int32(0)
    for i in range(PER):
        r, at = i % 4 + 1, 32 * (i // 4) + 24
        if which == 0:
            total = total + lists[0, r, at] * lists[0, r, at + 1]
        else:
            total = total + lists[2, r, at] + lists[1, r, at] * (lists[1, r, at + 1] - 1)

    shape3 = (CHUNK // 8, 8, LANES)
    spare = PER * 2 * LANES

    def row(ref, at):
        return jnp.broadcast_to(ref[pl.ds(at, 1), :], (8, LANES))

    def rows(ref, at):
        return ref[pl.ds(pl.multiple_of(at, CHUNK), CHUNK), :].reshape(shape3)

    for ref in (weight_sums, pull_sums):
        ref[spare : spare + CHUNK, :] = jnp.zeros((CHUNK, LANES), F32)

    def item(n, carry):
        i, k, j, out, at, groups, chunks, old_from, old_out, old_at, fars, powers = carry
        x = [row(cand, base) - row(rates, PER + i) for base in at]
        y = [row(cand, base + 1) - row(rates, 2 * PER + i) for base in at]
        scale = row(rates, i)
        u = rows(fan, 2 * out)
        v = rows(fan, 2 * out + CHUNK)

        weight_sum = rows(weight_sums, old_from)
        pull_sum = rows(pull_sums, old_from)
        for base, far, power in zip(old_at, fars, powers):
            factor = jnp.exp2(far)
            weight = jnp.exp2(power)
            weight_sum = weight_sum + weight * (factor * row(cand, base + 2))
            pull_sum = pull_sum + weight * (factor * row(pull, lax.shift_right_logical(base, 3)))
        place = pl.ds(pl.multiple_of(old_out, CHUNK), CHUNK)
        weight_sums[place, :] = weight_sum.reshape(CHUNK, LANES)
        pull_sums[place, :] = pull_sum.reshape(CHUNK, LANES)

        fars = tuple((x[g] * x[g] + y[g] * y[g]) * scale for g in range(3))
        powers = tuple(u * x[g] + v * y[g] for g in range(3))
        last = j + 1 == groups
        end = last & (k + 1 == chunks)
        next_j = jnp.where(last, 0, j + 1)
        next_k = jnp.where(end, 0, jnp.where(last, k + 1, k))
        next_i = jnp.minimum(jnp.where(end, i + 1, i), PER - 1)
        next_out = next_i * (2 * LANES) + next_k * CHUNK
        kind = 0 if which == 0 else jnp.where(next_k == 0, 2, 1)
        return (
            next_i, next_k, next_j, next_out,
            tuple(listed(kind, next_i, 3 * next_j + g) for g in range(3)),
            listed(kind, next_i, 24), listed(kind, next_i, 25),
            jnp.where(j == 0, spare, out), out, at, fars, powers,
        )

    zero = rows(fan, 0) * 0.0
    none = row(rates, 0) * 0.0
    begin = jnp.int32(0)
    kind = 2 * which
    lax.fori_loop(
        0, total + 1, item,
        (
            begin, begin, begin, begin, tuple(lists[kind, 1, g] for g in range(3)),
            lists[kind, 1, 24], lists[kind, 1, 25],
            jnp.int32(spare), begin, (begin,) * 3, (none,) * 3, (zero,) * 3,
        ),
    )


def first_kernel(data, notes, lists, weight_sums, pull_sums, cand, pull, fan, rates):
    prepare(0, data, notes, cand, fan, rates)
    for h in range(2):
        pull[40 * h : 40 * h + 40, :] = data[4 + h] * data[6 + h]
    sums_of(0, cand, pull, fan, rates, lists, weight_sums, pull_sums)


def second_kernel(cand, pull, fan, rates, lists, weight_sums, pull_sums):
    sums_of(1, cand, pull, fan, rates, lists, weight_sums, pull_sums)


def finish(which, h, data, notes, weight_sums, pull_sums, totals, more=None):
    ones = jnp.ones((8, LANES), BF16)
    for k, ref in enumerate((weight_sums, pull_sums)):
        for i in range(PER):
            at = LANES * (2 * i + h)
            values = ref[at : at + LANES, :]
            if more is not None and h == 0:
                added = values[:CHUNK] + more[k, CHUNK * i : CHUNK * (i + 1), :]
                values = jnp.concatenate([added, values[CHUNK:]], axis=0)
            high = values.astype(BF16)
            low = (values - high.astype(F32)).astype(BF16)
            both = jnp.concatenate([high, low], axis=0)
            sums = lax.dot_general(
                ones, both, (((1,), (1,)), ((), ())), preferred_element_type=F32
            )
            totals[k, i : i + 1, :] = sums[0:1, :LANES] + sums[0:1, LANES:]
    x = data[h, 4:20, :] - 0.5
    y = data[2 + h, 4:20, :] - 0.5
    cov = data[4 + 4 * which + h, 4:20, :]
    fade = jnp.exp2(-rate_of(which, notes) * (x * x + y * y))
    lane = lax.broadcasted_iota(jnp.int32, (PER, LANES), 1)
    live = (lane + LANES * h).astype(F32) < notes[:, 0:1]
    total = 1.0 + fade * totals[0]
    beta = jnp.where(live, fade * totals[1] / total, 0.0)
    return beta, jnp.where(live, cov * cov / total, 0.0)


def edge_cells(a, b):
    cols = range(4) if a == 0 else (0 if a == -1 else 3,)
    rows = range(4) if b == 0 else (0 if b == -1 else 3,)
    return [4 * r + c for r in rows for c in cols]


def share(cand, pull, fan, rates, notes, keeps, more):
    shape3 = (CHUNK // 8, 8, LANES)

    def row(ref, at):
        return jnp.broadcast_to(ref[pl.ds(at, 1), :], (8, LANES))

    def rows(ref, at):
        return ref[pl.ds(pl.multiple_of(at, CHUNK), CHUNK), :].reshape(shape3)

    for e in SHARE:
        kept = jnp.ones((PER, LANES), F32)
        if e != 4:
            kept = jnp.broadcast_to(notes[:, 12 + e : 13 + e], (PER, LANES))
        keeps[PER * e : PER * (e + 1), :] = kept

    def band(r):
        for c in range(4):
            i = 4 * r + c
            u = rows(fan, 4 * LANES * i)
            v = rows(fan, 4 * LANES * i + CHUNK)
            scale = row(rates, i)
            north = row(rates, 2 * PER + i)
            weight_sum = jnp.zeros(shape3, F32)
            pull_sum = jnp.zeros(shape3, F32)
            for e in SHARE:
                col, line = c + e // 3, r + e % 3
                t = 24 + line if col == 0 else 32 + line if col == 5 else 4 * line + col - 1
                x = row(cand, 8 * t) - (c + 1.0)
                y = row(cand, 8 * t + 1) - north
                factor = jnp.exp2((x * x + y * y) * scale) * row(keeps, PER * e + i)
                weight = jnp.exp2(u * x + v * y)
                weight_sum = weight_sum + weight * (factor * row(cand, 8 * t + 2))
                pull_sum = pull_sum + weight * (factor * row(pull, t))
            place = pl.ds(pl.multiple_of(CHUNK * i, CHUNK), CHUNK)
            more[0, place, :] = weight_sum.reshape(CHUNK, LANES)
            more[1, place, :] = pull_sum.reshape(CHUNK, LANES)

    each(0, 4, band)


def halo_kernel(
    weight_sums, pull_sums, data, notes, grid_out, beta_out, hat_out, cand_out, fan_out, rates_out,
    own, edge, totals, recv, send, land,
):
    region = lax.axis_index("region")
    tile = lax.axis_index("tile")
    steps = [(a, b) for a in (-1, 0, 1) for b in (-1, 0, 1) if (a, b) != (0, 0)]

    owner = walk(tile)

    def place(a, b):
        return lax.rem(region + a + NREGION, NREGION), walk(lax.rem(owner + b + NTILE, NTILE))

    barrier = pltpu.get_barrier_semaphore()
    for a, b in steps:
        signal(barrier, *place(a, b))
    for h in range(2):
        beta, hat = finish(0, h, data, notes, weight_sums, pull_sums, totals)
        beta_out[h] = beta
        hat_out[h] = hat
        own[h] = data[8 + h, 4:20, :] * (data[10 + h, 4:20, :] - data[4 + h, 4:20, :] * beta)
    edge[...] = jnp.zeros((8, 8, LANES), F32)
    for k, (a, b) in enumerate(steps):
        for h in range(2):
            for n, i in enumerate(edge_cells(a, b)):
                edge[k, 4 * h + n : 4 * h + n + 1, :] = own[h, i : i + 1, :]
    pl.semaphore_wait(barrier, 8)
    copies = []
    for k, (a, b) in enumerate(steps):
        copies.append(remote(edge.at[k], recv.at[7 - k], send.at[k], land.at[7 - k], *place(a, b)))
    for copy in copies:
        copy.start()
    prepare(1, data, notes, cand_out, fan_out, rates_out)
    for copy in copies:
        copy.wait_recv()
    fits = {-1: region > 0, 0: None, 1: region < NREGION - 1}
    fits_row = {-1: owner > 0, 0: None, 1: owner < NTILE - 1}
    for h in range(2):
        to = 40 * h
        grid_out[to + 4 : to + 20, :] = own[h]
        for first in (to + 30, to + 38):
            grid_out[first : first + 2, :] = jnp.zeros((2, LANES), F32)
        for k, (a, b) in enumerate(steps):
            many = len(edge_cells(-a, -b))
            rows = recv[k, 4 * h : 4 * h + many, :]
            for fit in (fits[a], fits_row[b]):
                if fit is not None:
                    rows = jnp.where(fit, rows, 0.0)
            if a == 0:
                first = to + (0 if b == -1 else 20)
            else:
                first = to + (24 if a == -1 else 32) + (0, 1, 5)[b + 1]
            grid_out[first : first + many, :] = rows
    for copy in copies:
        copy.wait_send()


def return_kernel(
    beta_one, hat_one, weight_sums, pull_sums, data, notes, cells, home, cand, pull, fan, rates,
    betas, hats, residual, keeps, more, totals, stage, rbuf, msg, recv, send1, recv1, send2, recv2,
):
    region = lax.axis_index("region")
    tile = lax.axis_index("tile")
    group = tile // 8
    piece = lax.rem(tile, 8)
    barrier = pltpu.get_barrier_semaphore()
    for k in FAR_FIRST:
        signal(barrier, region, jnp.bitwise_xor(tile, k))
    share(cand, pull, fan, rates, notes, keeps, more)
    for h in range(2):
        stage[h] = beta_one[h]
        stage[2 + h] = hat_one[h]
        stage[4 + h], stage[6 + h] = finish(
            1, h, data, notes, weight_sums, pull_sums, totals, more
        )
    pl.semaphore_wait(barrier, NTILE - 1)

    def to_middle(o):
        other = jnp.bitwise_xor(tile, o)
        return remote(
            stage.at[lax.rem(other, 8)], rbuf.at[tile], send1.at[o], recv1.at[tile], region, other
        )

    for k in FAR_FIRST:
        to_middle(k).start()
    rbuf[tile] = stage[piece]

    row = cells[pl.ds(group, 1), :]
    column = jnp.transpose(jnp.broadcast_to(row, (LANES, LANES)))
    lane = lax.broadcasted_iota(jnp.int32, (LANES, LANES), 1)
    hots = []
    for b in range(4):
        of = lax.shift_right_logical(lane, 4)
        if b % 2 == 1:
            of = 6 - of + 2 * lax.bitwise_and(of, 1)
        here = LANES * b + of * PER + lax.bitwise_and(lane, PER - 1)
        hots.append(jnp.where(here.astype(F32) == column, 1.0, 0.0).astype(BF16))
    hot = jnp.concatenate(hots, axis=1)

    def from_source(o):
        other = jnp.bitwise_xor(tile, o)
        return remote(stage.at[0], rbuf.at[other], send1.at[o], recv1.at[other], region, other)

    each(1, NTILE, lambda o: from_source(o).wait_recv())
    spread = wide_split(rbuf[...].reshape(NTILE * PER, LANES))
    msg[...] = join3(jnp.dot(hot, spread, preferred_element_type=F32)).reshape(8, PER, LANES)

    def home_copy(o):
        i = jnp.bitwise_xor(piece, o)
        return remote(
            msg.at[i], recv.at[piece], send2.at[o], recv2.at[piece], region, group * 8 + i
        )

    for k in FAR_FIRST:
        if k < 8:
            home_copy(k).start()
    recv[piece] = msg[piece]

    def from_middle(o):
        p = jnp.bitwise_xor(piece, o)
        return remote(msg.at[0], recv.at[p], send2.at[o], recv2.at[p], region, group * 8 + p)

    each(1, 8, lambda o: from_middle(o).wait_recv())
    for h in range(2):
        left = home[4 + h] - home[h] * recv[h] - home[2 + h] * recv[4 + h]
        residual[pl.ds(h, PER, stride=2), :] = left
        for t in range(PER):
            span = slice(LANES * (2 * t + h), LANES * (2 * t + h + 1))
            for f in range(2):
                betas[f : f + 1, span] = recv[4 * f + h, t : t + 1, :]
                hats[f : f + 1, span] = recv[2 + 4 * f + h, t : t + 1, :]
    each(1, NTILE, lambda o: to_middle(o).wait_send())
    each(1, 8, lambda o: home_copy(o).wait_send())


def store_kernel(betas, hats, residual, betas_out, hats_out, residual_out, done):
    pairs = ((betas, betas_out), (hats, hats_out), (residual, residual_out))
    copies = [pltpu.make_async_copy(a, b, done.at[k]) for k, (a, b) in enumerate(pairs)]
    for copy in copies:
        copy.start()
    for copy in copies:
        copy.wait()


VM = pl.BlockSpec(memory_space=pltpu.VMEM)
SM = pl.BlockSpec(memory_space=pltpu.SMEM)
HB = pl.BlockSpec(memory_space=pltpu.HBM)
DMA = pltpu.SemaphoreType.DMA


def shape(*dims, dtype=F32):
    return jax.ShapeDtypeStruct(dims, dtype)


def body(offsets, design, target, beta_second, counts, kernel_width, reach, assignment):
    data, notes, lists, cells, home = pl.pallas_call(
        gather_kernel,
        out_shape=[
            shape(12, 40, LANES), shape(PER, LANES), shape(3, 8, LANES, dtype=jnp.int32),
            shape(8, LANES), shape(6, PER, LANES),
        ],
        in_specs=[HB] * 8,
        out_specs=[VM] * 5,
        scratch_shapes=[
            pltpu.VMEM((2, NTILE * LANES), F32),
            pltpu.VMEM((2, NTILE * LANES), F32),
            pltpu.VMEM((NTILE, LANES), F32),
            pltpu.VMEM((NTILE, LANES), F32),
            pltpu.VMEM((1, PER), jnp.int32),
            pltpu.VMEM((2, PER), jnp.int32),
            pltpu.VMEM((9, 2, PER), jnp.int32),
            pltpu.VMEM((1, PER), jnp.int32),
            pltpu.VMEM((32, LANES), F32),
            pltpu.VMEM((48, LANES), F32),
            pltpu.VMEM((640, LANES), F32),
            pltpu.VMEM((NPIECE, 24, LANES), F32),
            pltpu.VMEM((NTILE, 24, LANES), F32),
            pltpu.VMEM((16, 40, LANES), F32),
            pltpu.VMEM((NPIECE, 40, LANES), F32),
            DMA((8,)),
            DMA((NTILE,)),
            DMA((NTILE,)),
            DMA((3, 16)),
            DMA((3, 16)),
        ],
        compiler_params=pltpu.CompilerParams(collective_id=0, has_side_effects=True, vmem_limit_bytes=8 << 20),
        name="to_owners",
    )(
        *(
            pltpu.with_memory_space_constraint(value, pltpu.HBM)
            for value in (
                offsets, design, target.reshape(NTILE, LANES), beta_second.reshape(NTILE, LANES),
                counts.reshape(1, PER), kernel_width, reach.transpose(2, 0, 1), assignment,
            )
        )
    )
    sums = [shape((PER + 1) * 2 * LANES, LANES)] * 2
    tables = [(640, LANES), (80, LANES), (PER * 4 * LANES, LANES), (3 * PER, LANES)]
    weight_sums, pull_sums = pl.pallas_call(
        first_kernel,
        out_shape=sums,
        in_specs=[VM, VM, SM],
        out_specs=[VM] * 2,
        scratch_shapes=[pltpu.VMEM(dims, F32) for dims in tables],
        compiler_params=pltpu.CompilerParams(vmem_limit_bytes=16 << 20),
        name="smooth_one",
    )(data, notes, lists)
    grid, beta_one, hat_one, cand, fan, rates = pl.pallas_call(
        halo_kernel,
        out_shape=[
            shape(80, LANES), shape(2, PER, LANES), shape(2, PER, LANES), shape(640, LANES),
            shape(PER * 4 * LANES, LANES), shape(3 * PER, LANES),
        ],
        in_specs=[VM] * 4,
        out_specs=[VM] * 6,
        scratch_shapes=[
            pltpu.VMEM((2, PER, LANES), F32),
            pltpu.VMEM((8, 8, LANES), F32),
            pltpu.VMEM((2, PER, LANES), F32),
            pltpu.VMEM((8, 8, LANES), F32),
            DMA((8,)),
            DMA((8,)),
        ],
        compiler_params=pltpu.CompilerParams(
            collective_id=1, has_side_effects=True, vmem_limit_bytes=16 << 20
        ),
        name="edges",
    )(weight_sums, pull_sums, data, notes)
    weight_sums, pull_sums = pl.pallas_call(
        second_kernel,
        out_shape=sums,
        in_specs=[VM] * 4 + [SM],
        out_specs=[VM] * 2,
        compiler_params=pltpu.CompilerParams(vmem_limit_bytes=16 << 20),
        name="smooth_two",
    )(cand, grid, fan, rates, lists)
    betas, hats, residual = pl.pallas_call(
        return_kernel,
        out_shape=[shape(2, NTILE * LANES), shape(2, NTILE * LANES), shape(NTILE, LANES)],
        in_specs=[VM] * 12,
        out_specs=[VM] * 3,
        scratch_shapes=[
            pltpu.VMEM((9 * PER, LANES), F32),
            pltpu.VMEM((2, PER * CHUNK, LANES), F32),
            pltpu.VMEM((2, PER, LANES), F32),
            pltpu.VMEM((8, PER, LANES), F32),
            pltpu.VMEM((NTILE, PER, LANES), F32),
            pltpu.VMEM((8, PER, LANES), F32),
            pltpu.VMEM((8, PER, LANES), F32),
            DMA((NTILE,)),
            DMA((NTILE,)),
            DMA((8,)),
            DMA((8,)),
        ],
        compiler_params=pltpu.CompilerParams(collective_id=2, has_side_effects=True, vmem_limit_bytes=16 << 20),
        name="to_slots",
    )(beta_one, hat_one, weight_sums, pull_sums, data, notes, cells, home, cand, grid, fan, rates)
    betas, hats, residual = pl.pallas_call(
        store_kernel,
        out_shape=[shape(2, NTILE * LANES), shape(2, NTILE * LANES), shape(NTILE, LANES)],
        in_specs=[VM] * 3,
        out_specs=[HB] * 3,
        scratch_shapes=[DMA((3,))],
        compiler_params=pltpu.CompilerParams(vmem_limit_bytes=8 << 20),
        name="store",
    )(betas, hats, residual)
    return betas, hats, residual.reshape(-1)


def solution(mesh):
    split = ("region", "tile")
    in_specs = (
        P(None, split), P(None, split), P(split), P(split), P(split), P(None, split),
        P(None, split, None), P("region", "tile"),
    )
    out_specs = (P(None, split), P(None, split), P(split))
    return jax.shard_map(body, mesh=mesh, in_specs=in_specs, out_specs=out_specs, check_vma=False)
```

```python
import functools
import math

import jax
import jax.numpy as jnp
from jax import lax
from jax.experimental import pallas as pl
from jax.experimental.pallas import tpu as pltpu
from jax.sharding import PartitionSpec as P

TX = 4
LANES = 128
PER = 16
NPIECE = 13
CHUNK = 64
SHARE = (4, 1, 7, 3, 5, 0, 8)
NREGION = 8
NTILE = 32
F32 = jnp.float32
BF16 = jnp.bfloat16


def split3(x):
    hi = x.astype(BF16).astype(F32)
    rest = x - hi
    mid = rest.astype(BF16).astype(F32)
    low = (rest - mid).astype(BF16).astype(F32)
    return hi, mid, low


def wide_split(x):
    hi, mid, low = split3(x)
    return jnp.concatenate([hi.astype(BF16), mid.astype(BF16), low.astype(BF16)], axis=1)


def join3(x):
    return x[:, :LANES] + x[:, LANES : 2 * LANES] + x[:, 2 * LANES :]


def remote(src, dst, send, recv, region, tile):
    return pltpu.make_async_remote_copy(
        src_ref=src,
        dst_ref=dst,
        send_sem=send,
        recv_sem=recv,
        device_id=(region, tile),
        device_id_type=pl.DeviceIdType.MESH,
    )


def signal(sem, region, tile):
    pl.semaphore_signal(sem, inc=1, device_id=(region, tile), device_id_type=pl.DeviceIdType.MESH)


def links(k):
    away = (0, 1, 2, 1)
    return away[k // 2 % 4] + away[k // 8 % 4] + k % 2 / 2


FAR_FIRST = sorted(range(1, NTILE), key=lambda k: -links(k))


def each(low, high, step):
    def turn(index, carry):
        step(index)
        return carry

    lax.fori_loop(low, high, turn, 0)


def walk(tile):
    turned = (tile // 8) * 8 + 6 - lax.rem(tile, 8) + 2 * lax.rem(tile, 2)
    return jnp.where(lax.rem(tile // 8, 2) == 1, turned, tile)


def gather_kernel(
    offsets_in, design_in, target_in, prior_in, counts_in, width_in, reach_in, cells_in,
    data_out, width_out, list_one, list_two, cells_out, home_out,
    offs, design, target, prior, counts, widths, reach, cells, notes, rows_of,
    wanted, stage, rbuf, msg, recv, load, send1, recv1, send2, recv2,
):
    region = lax.axis_index("region")
    tile = lax.axis_index("tile")
    group = tile // 16
    piece = lax.rem(tile, 16)
    up = lax.rem(region + 1, NREGION)
    down = lax.rem(region + NREGION - 1, NREGION)

    barrier = pltpu.get_barrier_semaphore()
    for k in range(15, -1, -1):
        signal(barrier, up, jnp.bitwise_xor(tile, k))
        signal(barrier, down, jnp.bitwise_xor(tile, k))
    for k in FAR_FIRST:
        signal(barrier, region, jnp.bitwise_xor(tile, k))

    loads = [
        pltpu.make_async_copy(source, place, load.at[k])
        for k, (source, place) in enumerate(
            (
                (counts_in, counts), (width_in, widths), (reach_in, reach), (cells_in, cells),
                (offsets_in, offs), (design_in, design), (target_in, target), (prior_in, prior),
            )
        )
    ]
    for copy in loads:
        copy.start()
    notes[...] = jnp.zeros((32, LANES), F32)
    stage[12] = jnp.zeros((24, LANES), F32)
    rows_of[...] = jnp.zeros((48, LANES), F32)
    for copy in loads[:4]:
        copy.wait()
    notes[0:1, 0:PER] = counts[...].astype(F32)
    notes[1:3, 0:PER] = widths[...].astype(F32)
    for e in range(9):
        for w in range(2):
            at = 3 + 9 * w + e
            notes[at : at + 1, 0:PER] = reach[e, w : w + 1, :].astype(F32)
    turned = jnp.transpose(notes[...])[0:PER]
    stage[12, 0:PER, 0:32] = turned
    cell = cells[...]
    order = (lax.bitwise_and(cell, 127) * TX + lax.shift_right_logical(cell, 7)).astype(F32)
    for k in range(8):
        notes[24:25, PER * k : PER * k + PER] = order
    row_lane = lax.broadcasted_iota(jnp.int32, (8, LANES), 1)
    cell_row = jnp.where(
        lax.shift_right_logical(row_lane, 4) == lax.rem(tile, 8),
        jnp.broadcast_to(notes[24:25, :], (8, LANES)), 0.0,
    )
    for p in range(NPIECE):
        stage[p, PER : PER + 8, :] = cell_row
    for copy in loads[4:]:
        copy.wait()
    lane = lax.broadcasted_iota(jnp.int32, (PER, LANES), 1)
    count = turned[:, 0:1]
    for t in range(PER):
        for h in range(2):
            span = slice(LANES * (2 * t + h), LANES * (2 * t + h + 1))
            for f in range(2):
                stage[2 * f + h, t : t + 1, :] = offs[f : f + 1, span]
                stage[4 + 4 * f + h, t : t + 1, :] = design[f : f + 1, span]
    for h in range(2):
        present = ((lane + LANES * h).astype(F32) < count).astype(F32)
        cov_one = stage[4 + h, 0:PER, :] * present
        cov_two = stage[8 + h, 0:PER, :]
        seen = target[pl.ds(h, PER, stride=2), :]
        before = prior[pl.ds(h, PER, stride=2), :]
        stage[4 + h, 0:PER, :] = cov_one
        stage[6 + h, 0:PER, :] = seen - cov_two * before
        cov_two = cov_two * present
        stage[8 + h, 0:PER, :] = cov_two
        stage[10 + h, 0:PER, :] = seen
        home_out[h] = cov_one
        home_out[2 + h] = cov_two
        home_out[4 + h] = seen * present

    pl.semaphore_wait(barrier, NTILE - 1 + 32)

    def to_middle(o):
        other = jnp.bitwise_xor(tile, o)
        held = jnp.minimum(lax.rem(other, 16), NPIECE - 1)
        return remote(
            stage.at[held, pl.ds(0, PER + 1)], rbuf.at[tile, pl.ds(0, PER + 1)],
            send1.at[o], recv1.at[tile], region, other,
        )

    for k in FAR_FIRST:
        to_middle(k).start()
    rbuf[tile] = stage[jnp.minimum(piece, NPIECE - 1)]

    number = lax.broadcasted_iota(jnp.int32, (640, LANES), 0)
    owner = lax.shift_right_logical(number * 205, 13)
    q = number - owner * 40
    turned_owner = 14 - lax.bitwise_and(owner, 7) + 2 * lax.bitwise_and(owner, 1)
    first = (group * 16 + jnp.where(owner < 8, owner, turned_owner)) * 16
    side = jnp.where(q < 32, q - 24, q - 32)
    base = jnp.where(q < 24, q - 4, (side - 1) * 4 + jnp.where(q < 32, 3, 0))
    open_up = jnp.where(region < NREGION - 1, 1, 0)
    open_down = jnp.where(region > 0, 1, 0)
    beside = jnp.where(side < 6, jnp.where(q < 32, open_up, open_down), 0)
    allowed = jnp.where(q < 24, 1, beside)
    cell = first + base
    wanted[...] = jnp.where(allowed > 0, cell, -1).astype(F32)

    def from_source(o):
        other = jnp.bitwise_xor(tile, o)
        return remote(
            stage.at[0, pl.ds(0, PER + 1)], rbuf.at[other, pl.ds(0, PER + 1)],
            send1.at[o], recv1.at[other], region, other,
        )

    each(1, NTILE, lambda o: from_source(o).wait_recv())

    cell_rows = [
        jnp.sum(rbuf[8 * b : 8 * b + 8, PER, :], axis=0, keepdims=True) for b in range(4)
    ]
    for b in range(4):
        cells_out[b : b + 1, :] = cell_rows[b]
    cells_out[4:8, :] = jnp.zeros((4, LANES), F32)

    @pl.when(piece < NPIECE)
    def _():
        spread = wide_split(rbuf[:, 0:PER, :].reshape(NTILE * PER, LANES))
        hot = jnp.concatenate(
            [jnp.where(wanted[...] == cell_rows[b], 1.0, 0.0).astype(BF16) for b in range(4)], axis=1
        )
        moved = join3(jnp.dot(hot, spread, preferred_element_type=F32))
        msg[...] = moved.reshape(16, 40, LANES)

    def own_copy(o):
        i = jnp.bitwise_xor(piece, o)
        return remote(
            msg.at[i, pl.ds(0, 24)], recv.at[piece, pl.ds(0, 24)],
            send2.at[0, o], recv2.at[0, piece], region, group * 16 + i,
        )

    def up_copy(i):
        return remote(
            msg.at[i, pl.ds(24, 8)], recv.at[piece, pl.ds(24, 8)],
            send2.at[1, i], recv2.at[1, piece], up, group * 16 + i,
        )

    def down_copy(i):
        return remote(
            msg.at[i, pl.ds(32, 8)], recv.at[piece, pl.ds(32, 8)],
            send2.at[2, i], recv2.at[2, piece], down, group * 16 + i,
        )

    @pl.when(piece < NPIECE)
    def _():
        for k in sorted(range(16), key=lambda k: -links(k)):
            up_copy(jnp.bitwise_xor(piece, k)).start()
            down_copy(jnp.bitwise_xor(piece, k)).start()
        for k in FAR_FIRST:
            if k < 16:
                own_copy(k).start()
        recv[piece, 0:24, :] = msg[piece, 0:24, :]

    def wait_own(p):
        @pl.when(p != piece)
        def _():
            remote(
                msg.at[0, pl.ds(0, 24)], recv.at[p, pl.ds(0, 24)],
                send2.at[0, 0], recv2.at[0, p], region, group * 16 + p,
            ).wait_recv()

    def wait_sides(p):
        remote(
            msg.at[0, pl.ds(24, 8)], recv.at[p, pl.ds(24, 8)],
            send2.at[1, 0], recv2.at[1, p], down, group * 16 + p,
        ).wait_recv()
        remote(
            msg.at[0, pl.ds(32, 8)], recv.at[p, pl.ds(32, 8)],
            send2.at[2, 0], recv2.at[2, p], up, group * 16 + p,
        ).wait_recv()

    wait_own(12)
    wait_sides(12)
    width_out[...] = recv[12, 4:20, :]
    for r in range(6):
        rows_of[8 * r : 8 * r + 1, :] = recv[12, 24 + r : 25 + r, :]
        rows_of[8 * r + 1 : 8 * r + 5, :] = recv[12, 4 * r : 4 * r + 4, :]
        rows_of[8 * r + 5 : 8 * r + 6, :] = recv[12, 32 + r : 33 + r, :]

    def spread_lane(r, at):
        return jnp.broadcast_to(rows_of[8 * r : 8 * r + 8, at : at + 1], (8, LANES))

    lanes = lax.broadcasted_iota(jnp.int32, (8, LANES), 1)
    spots = lax.bitwise_and(lanes, 31)
    spots_f = spots.astype(F32)
    over = lax.broadcasted_iota(jnp.int32, (8, LANES), 0)
    filled = [spread_lane(r, 0) for r in range(6)]
    near = [
        [filled[r] if a == 1 else pltpu.roll(filled[r], (1 - a) % 8, 0) for a in range(3)]
        for r in range(6)
    ]
    for w, skipped, place in ((0, (), list_one.at[0]), (1, (), list_two.at[0]), (1, SHARE, list_two.at[1])):
        for r in range(1, 5):
            many = jnp.zeros((8, LANES), F32)
            todo = jnp.zeros((8, LANES), F32)
            for e in range(9):
                beside, beyond = e // 3, r + e % 3 - 1
                there = near[beyond][beside]
                keep = None if e == 4 else spread_lane(r, 3 + 9 * w + e)
                c = over + (beside - 1)
                t = jnp.where(c == 0, 24 + beyond, jnp.where(c == 5, 32 + beyond, beyond * 4 + c - 1))
                at = (8 * t).astype(F32)
                for h in range(1 if e in skipped else 0, 2):
                    flag = jnp.where(there > LANES * h, 1.0 if keep is None else keep, 0.0)
                    todo = todo + jnp.where(many == spots_f, flag * (at + 320.0 * h), 0.0)
                    many = many + flag
            chunks = lax.shift_right_logical(filled[r].astype(jnp.int32) + CHUNK - 1, CHUNK.bit_length() - 1)
            value = jnp.where(spots_f < many, todo, 240.0).astype(jnp.int32)
            groups = lax.shift_right_logical((many.astype(jnp.int32) + 2) * 11, 5)
            groups = jnp.maximum(groups, 1)
            value = jnp.where(spots == 24, groups, value)
            value = jnp.where(spots == 25, chunks, value)
            value = jnp.where(spots == 26, filled[r].astype(jnp.int32), value)
            band = value if r == 1 else jnp.where(lax.shift_right_logical(lanes, 5) == r - 1, value, band)
        place[...] = band
    each(0, NPIECE - 1, wait_own)
    each(0, NPIECE - 1, wait_sides)
    for p in range(12):
        data_out[p] = recv[p]

    each(1, NTILE, lambda o: to_middle(o).wait_send())

    @pl.when(piece < NPIECE)
    def _():
        each(1, 16, lambda o: own_copy(o).wait_send())
        each(0, 16, lambda i: up_copy(i).wait_send())
        each(0, 16, lambda i: down_copy(i).wait_send())


def rate_of(which, notes):
    width = notes[:, 1 + which : 2 + which]
    return jnp.broadcast_to((32.0 * math.log2(math.e)) / (width * width), (PER, LANES))


def prepare(which, data, notes, cand, fan, rates):
    rate = rate_of(which, notes)
    rates[0:PER, :] = -rate
    number = lax.broadcasted_iota(jnp.int32, (PER, LANES), 0)
    rates[PER : 2 * PER, :] = (lax.bitwise_and(number, 3) + 1).astype(F32)
    rates[2 * PER : 3 * PER, :] = (lax.shift_right_logical(number, 2) + 1).astype(F32)
    slot = lax.broadcasted_iota(jnp.int32, (40, LANES), 0)
    col = jnp.where(slot < 24, lax.rem(slot, 4) + 1, jnp.where(slot < 32, 0, 5)).astype(F32)
    row = jnp.where(
        slot < 24, slot // 4, jnp.where(slot < 32, slot - 24, slot - 32)
    ).astype(F32)
    columns = []
    for h in range(2):
        x = data[h] - 0.5
        y = data[2 + h] - 0.5
        cov = data[4 + 4 * which + h]
        for k, field in enumerate((x + col, y + row, cov * cov)):
            cand[pl.ds(320 * h + k, 40, stride=8), :] = field
        along, upward = [
            jnp.transpose(jnp.concatenate(split3(2.0 * rate * source), axis=0)).astype(BF16)
            for source in (x[4:20], y[4:20])
        ]
        for low in range(0, LANES, CHUNK):
            columns += [along[low : low + CHUNK], upward[low : low + CHUNK]]
    columns = jnp.concatenate(columns, axis=0)
    which_row = lax.bitwise_and(lax.broadcasted_iota(jnp.int32, (3 * PER, LANES), 0), PER - 1)
    for i in range(PER):
        pick = jnp.where(which_row == i, 1.0, 0.0).astype(BF16)
        fan[4 * LANES * i : 4 * LANES * (i + 1), :] = jnp.dot(
            columns, pick, preferred_element_type=F32
        )


def sums_of(which, cand, pull, fan, rates, lists, weight_sums, pull_sums):
    def listed(kind, i, at):
        band = lax.shift_right_logical(i, 2) * 32
        return lists[kind, lax.bitwise_and(i, 3) + 1, band + at]

    total = jnp.int32(0)
    for i in range(PER):
        r, at = i % 4 + 1, 32 * (i // 4) + 24
        if which == 0:
            total = total + lists[0, r, at] * lists[0, r, at + 1]
        else:
            total = total + lists[1, r, at] + lists[0, r, at] * (lists[0, r, at + 1] - 1)

    shape3 = (CHUNK // 8, 8, LANES)
    spare = PER * 2 * LANES

    def row(ref, at):
        return jnp.broadcast_to(ref[pl.ds(at, 1), :], (8, LANES))

    def rows(ref, at):
        return ref[pl.ds(pl.multiple_of(at, CHUNK), CHUNK), :].reshape(shape3)

    for ref in (weight_sums, pull_sums):
        ref[spare : spare + CHUNK, :] = jnp.zeros((CHUNK, LANES), F32)

    def item(n, carry):
        i, k, j, out, at, groups, chunks, old_from, old_out, old_at, fars, powers = carry
        x = [row(cand, base) - row(rates, PER + i) for base in at]
        y = [row(cand, base + 1) - row(rates, 2 * PER + i) for base in at]
        scale = row(rates, i)
        u = rows(fan, 2 * out)
        v = rows(fan, 2 * out + CHUNK)

        weight_sum = rows(weight_sums, old_from)
        pull_sum = rows(pull_sums, old_from)
        for base, far, power in zip(old_at, fars, powers):
            factor = jnp.exp2(far)
            weight = jnp.exp2(power)
            weight_sum = weight_sum + weight * (factor * row(cand, base + 2))
            pull_sum = pull_sum + weight * (factor * row(pull, lax.shift_right_logical(base, 3)))
        place = pl.ds(pl.multiple_of(old_out, CHUNK), CHUNK)
        weight_sums[place, :] = weight_sum.reshape(CHUNK, LANES)
        pull_sums[place, :] = pull_sum.reshape(CHUNK, LANES)

        fars = tuple((x[g] * x[g] + y[g] * y[g]) * scale for g in range(3))
        powers = tuple(u * x[g] + v * y[g] for g in range(3))
        last = j + 1 == groups
        end = last & (k + 1 == chunks)
        next_j = jnp.where(last, 0, j + 1)
        next_k = jnp.where(end, 0, jnp.where(last, k + 1, k))
        next_i = jnp.minimum(jnp.where(end, i + 1, i), PER - 1)
        next_out = next_i * (2 * LANES) + next_k * CHUNK
        kind = 0 if which == 0 else jnp.where(next_k == 0, 1, 0)
        return (
            next_i, next_k, next_j, next_out,
            tuple(listed(kind, next_i, 3 * next_j + g) for g in range(3)),
            listed(kind, next_i, 24), listed(kind, next_i, 25),
            jnp.where(j == 0, spare, out), out, at, fars, powers,
        )

    zero = rows(fan, 0) * 0.0
    none = row(rates, 0) * 0.0
    begin = jnp.int32(0)
    kind = which
    lax.fori_loop(
        0, total + 1, item,
        (
            begin, begin, begin, begin, tuple(lists[kind, 1, g] for g in range(3)),
            lists[kind, 1, 24], lists[kind, 1, 25],
            jnp.int32(spare), begin, (begin,) * 3, (none,) * 3, (zero,) * 3,
        ),
    )


def first_kernel(data, notes, lists, weight_sums, pull_sums, cand, pull, fan, rates):
    prepare(0, data, notes, cand, fan, rates)
    for h in range(2):
        pull[40 * h : 40 * h + 40, :] = data[4 + h] * data[6 + h]
    sums_of(0, cand, pull, fan, rates, lists, weight_sums, pull_sums)


def second_kernel(cand, pull, fan, rates, lists, weight_sums, pull_sums):
    sums_of(1, cand, pull, fan, rates, lists, weight_sums, pull_sums)


def finish(which, h, data, notes, weight_sums, pull_sums, totals, more=None):
    ones = jnp.ones((8, LANES), BF16)
    for k, ref in enumerate((weight_sums, pull_sums)):
        for i in range(PER):
            at = LANES * (2 * i + h)
            values = ref[at : at + LANES, :]
            if more is not None and h == 0:
                added = values[:CHUNK] + more[k, CHUNK * i : CHUNK * (i + 1), :]
                values = jnp.concatenate([added, values[CHUNK:]], axis=0)
            high = values.astype(BF16)
            low = (values - high.astype(F32)).astype(BF16)
            both = jnp.concatenate([high, low], axis=0)
            sums = lax.dot_general(
                ones, both, (((1,), (1,)), ((), ())), preferred_element_type=F32
            )
            totals[k, i : i + 1, :] = sums[0:1, :LANES] + sums[0:1, LANES:]
    x = data[h, 4:20, :] - 0.5
    y = data[2 + h, 4:20, :] - 0.5
    cov = data[4 + 4 * which + h, 4:20, :]
    fade = jnp.exp2(-rate_of(which, notes) * (x * x + y * y))
    lane = lax.broadcasted_iota(jnp.int32, (PER, LANES), 1)
    live = (lane + LANES * h).astype(F32) < notes[:, 0:1]
    total = 1.0 + fade * totals[0]
    beta = jnp.where(live, fade * totals[1] / total, 0.0)
    return beta, jnp.where(live, cov * cov / total, 0.0)


def edge_cells(a, b):
    cols = range(4) if a == 0 else (0 if a == -1 else 3,)
    rows = range(4) if b == 0 else (0 if b == -1 else 3,)
    return [4 * r + c for r in rows for c in cols]


def share(cand, pull, fan, rates, notes, keeps, more):
    shape3 = (CHUNK // 8, 8, LANES)

    def row(ref, at):
        return jnp.broadcast_to(ref[pl.ds(at, 1), :], (8, LANES))

    def rows(ref, at):
        return ref[pl.ds(pl.multiple_of(at, CHUNK), CHUNK), :].reshape(shape3)

    for e in SHARE:
        kept = jnp.ones((PER, LANES), F32)
        if e != 4:
            kept = jnp.broadcast_to(notes[:, 12 + e : 13 + e], (PER, LANES))
        keeps[PER * e : PER * (e + 1), :] = kept

    def band(r):
        for c in range(4):
            i = 4 * r + c
            u = rows(fan, 4 * LANES * i)
            v = rows(fan, 4 * LANES * i + CHUNK)
            scale = row(rates, i)
            north = row(rates, 2 * PER + i)
            weight_sum = jnp.zeros(shape3, F32)
            pull_sum = jnp.zeros(shape3, F32)
            for e in SHARE:
                col, line = c + e // 3, r + e % 3
                t = 24 + line if col == 0 else 32 + line if col == 5 else 4 * line + col - 1
                x = row(cand, 8 * t) - (c + 1.0)
                y = row(cand, 8 * t + 1) - north
                factor = jnp.exp2((x * x + y * y) * scale) * row(keeps, PER * e + i)
                weight = jnp.exp2(u * x + v * y)
                weight_sum = weight_sum + weight * (factor * row(cand, 8 * t + 2))
                pull_sum = pull_sum + weight * (factor * row(pull, t))
            place = pl.ds(pl.multiple_of(CHUNK * i, CHUNK), CHUNK)
            more[0, place, :] = weight_sum.reshape(CHUNK, LANES)
            more[1, place, :] = pull_sum.reshape(CHUNK, LANES)

    each(0, 4, band)


def halo_kernel(
    weight_sums, pull_sums, data, notes, grid_out, beta_out, hat_out, cand_out, fan_out, rates_out,
    own, edge, totals, recv, send, land,
):
    region = lax.axis_index("region")
    tile = lax.axis_index("tile")
    steps = [(a, b) for a in (-1, 0, 1) for b in (-1, 0, 1) if (a, b) != (0, 0)]

    owner = walk(tile)

    def place(a, b):
        return lax.rem(region + a + NREGION, NREGION), walk(lax.rem(owner + b + NTILE, NTILE))

    barrier = pltpu.get_barrier_semaphore()
    for a, b in steps:
        signal(barrier, *place(a, b))
    for h in range(2):
        beta, hat = finish(0, h, data, notes, weight_sums, pull_sums, totals)
        beta_out[h] = beta
        hat_out[h] = hat
        own[h] = data[8 + h, 4:20, :] * (data[10 + h, 4:20, :] - data[4 + h, 4:20, :] * beta)
    edge[...] = jnp.zeros((8, 8, LANES), F32)
    for k, (a, b) in enumerate(steps):
        for h in range(2):
            for n, i in enumerate(edge_cells(a, b)):
                edge[k, 4 * h + n : 4 * h + n + 1, :] = own[h, i : i + 1, :]
    pl.semaphore_wait(barrier, 8)
    copies = []
    for k, (a, b) in enumerate(steps):
        copies.append(remote(edge.at[k], recv.at[7 - k], send.at[k], land.at[7 - k], *place(a, b)))
    for copy in copies:
        copy.start()
    prepare(1, data, notes, cand_out, fan_out, rates_out)
    for copy in copies:
        copy.wait_recv()
    fits = {-1: region > 0, 0: None, 1: region < NREGION - 1}
    fits_row = {-1: owner > 0, 0: None, 1: owner < NTILE - 1}
    for h in range(2):
        to = 40 * h
        grid_out[to + 4 : to + 20, :] = own[h]
        for first in (to + 30, to + 38):
            grid_out[first : first + 2, :] = jnp.zeros((2, LANES), F32)
        for k, (a, b) in enumerate(steps):
            many = len(edge_cells(-a, -b))
            rows = recv[k, 4 * h : 4 * h + many, :]
            for fit in (fits[a], fits_row[b]):
                if fit is not None:
                    rows = jnp.where(fit, rows, 0.0)
            if a == 0:
                first = to + (0 if b == -1 else 20)
            else:
                first = to + (24 if a == -1 else 32) + (0, 1, 5)[b + 1]
            grid_out[first : first + many, :] = rows
    for copy in copies:
        copy.wait_send()


def return_kernel(
    beta_one, hat_one, weight_sums, pull_sums, data, notes, cells, home, cand, pull, fan, rates,
    betas, hats, residual, keeps, more, totals, stage, rbuf, msg, recv, send1, recv1, send2, recv2,
):
    region = lax.axis_index("region")
    tile = lax.axis_index("tile")
    group = tile // 8
    piece = lax.rem(tile, 8)
    barrier = pltpu.get_barrier_semaphore()
    for k in FAR_FIRST:
        signal(barrier, region, jnp.bitwise_xor(tile, k))
    share(cand, pull, fan, rates, notes, keeps, more)
    for h in range(2):
        stage[h] = beta_one[h]
        stage[2 + h] = hat_one[h]
        stage[4 + h], stage[6 + h] = finish(
            1, h, data, notes, weight_sums, pull_sums, totals, more
        )
    pl.semaphore_wait(barrier, NTILE - 1)

    def to_middle(o):
        other = jnp.bitwise_xor(tile, o)
        return remote(
            stage.at[lax.rem(other, 8)], rbuf.at[tile], send1.at[o], recv1.at[tile], region, other
        )

    for k in FAR_FIRST:
        to_middle(k).start()
    rbuf[tile] = stage[piece]

    row = cells[pl.ds(group, 1), :]
    column = jnp.transpose(jnp.broadcast_to(row, (LANES, LANES)))
    lane = lax.broadcasted_iota(jnp.int32, (LANES, LANES), 1)
    hots = []
    for b in range(4):
        of = lax.shift_right_logical(lane, 4)
        if b % 2 == 1:
            of = 6 - of + 2 * lax.bitwise_and(of, 1)
        here = LANES * b + of * PER + lax.bitwise_and(lane, PER - 1)
        hots.append(jnp.where(here.astype(F32) == column, 1.0, 0.0).astype(BF16))
    hot = jnp.concatenate(hots, axis=1)

    def from_source(o):
        other = jnp.bitwise_xor(tile, o)
        return remote(stage.at[0], rbuf.at[other], send1.at[o], recv1.at[other], region, other)

    each(1, NTILE, lambda o: from_source(o).wait_recv())
    spread = wide_split(rbuf[...].reshape(NTILE * PER, LANES))
    msg[...] = join3(jnp.dot(hot, spread, preferred_element_type=F32)).reshape(8, PER, LANES)

    def home_copy(o):
        i = jnp.bitwise_xor(piece, o)
        return remote(
            msg.at[i], recv.at[piece], send2.at[o], recv2.at[piece], region, group * 8 + i
        )

    for k in FAR_FIRST:
        if k < 8:
            home_copy(k).start()
    recv[piece] = msg[piece]

    def from_middle(o):
        p = jnp.bitwise_xor(piece, o)
        return remote(msg.at[0], recv.at[p], send2.at[o], recv2.at[p], region, group * 8 + p)

    each(1, 8, lambda o: from_middle(o).wait_recv())
    for h in range(2):
        left = home[4 + h] - home[h] * recv[h] - home[2 + h] * recv[4 + h]
        residual[pl.ds(h, PER, stride=2), :] = left
        for t in range(PER):
            span = slice(LANES * (2 * t + h), LANES * (2 * t + h + 1))
            for f in range(2):
                betas[f : f + 1, span] = recv[4 * f + h, t : t + 1, :]
                hats[f : f + 1, span] = recv[2 + 4 * f + h, t : t + 1, :]
    each(1, NTILE, lambda o: to_middle(o).wait_send())
    each(1, 8, lambda o: home_copy(o).wait_send())


def store_kernel(betas, hats, residual, betas_out, hats_out, residual_out, done):
    pairs = ((betas, betas_out), (hats, hats_out), (residual, residual_out))
    copies = [pltpu.make_async_copy(a, b, done.at[k]) for k, (a, b) in enumerate(pairs)]
    for copy in copies:
        copy.start()
    for copy in copies:
        copy.wait()


VM = pl.BlockSpec(memory_space=pltpu.VMEM)
SM = pl.BlockSpec(memory_space=pltpu.SMEM)
HB = pl.BlockSpec(memory_space=pltpu.HBM)
DMA = pltpu.SemaphoreType.DMA


def shape(*dims, dtype=F32):
    return jax.ShapeDtypeStruct(dims, dtype)


def body(offsets, design, target, beta_second, counts, kernel_width, reach, assignment):
    data, notes, list_one, list_two, cells, home = pl.pallas_call(
        gather_kernel,
        out_shape=[
            shape(12, 40, LANES), shape(PER, LANES), shape(1, 8, LANES, dtype=jnp.int32),
            shape(2, 8, LANES, dtype=jnp.int32), shape(8, LANES), shape(6, PER, LANES),
        ],
        in_specs=[HB] * 8,
        out_specs=[VM] * 6,
        scratch_shapes=[
            pltpu.VMEM((2, NTILE * LANES), F32),
            pltpu.VMEM((2, NTILE * LANES), F32),
            pltpu.VMEM((NTILE, LANES), F32),
            pltpu.VMEM((NTILE, LANES), F32),
            pltpu.VMEM((1, PER), jnp.int32),
            pltpu.VMEM((2, PER), jnp.int32),
            pltpu.VMEM((9, 2, PER), jnp.int32),
            pltpu.VMEM((1, PER), jnp.int32),
            pltpu.VMEM((32, LANES), F32),
            pltpu.VMEM((48, LANES), F32),
            pltpu.VMEM((640, LANES), F32),
            pltpu.VMEM((NPIECE, 24, LANES), F32),
            pltpu.VMEM((NTILE, 24, LANES), F32),
            pltpu.VMEM((16, 40, LANES), F32),
            pltpu.VMEM((NPIECE, 40, LANES), F32),
            DMA((8,)),
            DMA((NTILE,)),
            DMA((NTILE,)),
            DMA((3, 16)),
            DMA((3, 16)),
        ],
        compiler_params=pltpu.CompilerParams(collective_id=0, has_side_effects=True, vmem_limit_bytes=8 << 20),
        name="to_owners",
    )(
        *(
            pltpu.with_memory_space_constraint(value, pltpu.HBM)
            for value in (
                offsets, design, target.reshape(NTILE, LANES), beta_second.reshape(NTILE, LANES),
                counts.reshape(1, PER), kernel_width, reach.transpose(2, 0, 1), assignment,
            )
        )
    )
    sums = [shape((PER + 1) * 2 * LANES, LANES)] * 2
    tables = [(640, LANES), (80, LANES), (PER * 4 * LANES, LANES), (3 * PER, LANES)]
    weight_sums, pull_sums = pl.pallas_call(
        first_kernel,
        out_shape=sums,
        in_specs=[VM, VM, SM],
        out_specs=[VM] * 2,
        scratch_shapes=[pltpu.VMEM(dims, F32) for dims in tables],
        compiler_params=pltpu.CompilerParams(vmem_limit_bytes=16 << 20),
        name="smooth_one",
    )(data, notes, list_one)
    grid, beta_one, hat_one, cand, fan, rates = pl.pallas_call(
        halo_kernel,
        out_shape=[
            shape(80, LANES), shape(2, PER, LANES), shape(2, PER, LANES), shape(640, LANES),
            shape(PER * 4 * LANES, LANES), shape(3 * PER, LANES),
        ],
        in_specs=[VM] * 4,
        out_specs=[VM] * 6,
        scratch_shapes=[
            pltpu.VMEM((2, PER, LANES), F32),
            pltpu.VMEM((8, 8, LANES), F32),
            pltpu.VMEM((2, PER, LANES), F32),
            pltpu.VMEM((8, 8, LANES), F32),
            DMA((8,)),
            DMA((8,)),
        ],
        compiler_params=pltpu.CompilerParams(
            collective_id=1, has_side_effects=True, vmem_limit_bytes=16 << 20
        ),
        name="edges",
    )(weight_sums, pull_sums, data, notes)
    weight_sums, pull_sums = pl.pallas_call(
        second_kernel,
        out_shape=sums,
        in_specs=[VM] * 4 + [SM],
        out_specs=[VM] * 2,
        compiler_params=pltpu.CompilerParams(vmem_limit_bytes=16 << 20),
        name="smooth_two",
    )(cand, grid, fan, rates, list_two)
    betas, hats, residual = pl.pallas_call(
        return_kernel,
        out_shape=[shape(2, NTILE * LANES), shape(2, NTILE * LANES), shape(NTILE, LANES)],
        in_specs=[VM] * 12,
        out_specs=[VM] * 3,
        scratch_shapes=[
            pltpu.VMEM((9 * PER, LANES), F32),
            pltpu.VMEM((2, PER * CHUNK, LANES), F32),
            pltpu.VMEM((2, PER, LANES), F32),
            pltpu.VMEM((8, PER, LANES), F32),
            pltpu.VMEM((NTILE, PER, LANES), F32),
            pltpu.VMEM((8, PER, LANES), F32),
            pltpu.VMEM((8, PER, LANES), F32),
            DMA((NTILE,)),
            DMA((NTILE,)),
            DMA((8,)),
            DMA((8,)),
        ],
        compiler_params=pltpu.CompilerParams(collective_id=2, has_side_effects=True, vmem_limit_bytes=16 << 20),
        name="to_slots",
    )(beta_one, hat_one, weight_sums, pull_sums, data, notes, cells, home, cand, grid, fan, rates)
    betas, hats, residual = pl.pallas_call(
        store_kernel,
        out_shape=[shape(2, NTILE * LANES), shape(2, NTILE * LANES), shape(NTILE, LANES)],
        in_specs=[VM] * 3,
        out_specs=[HB] * 3,
        scratch_shapes=[DMA((3,))],
        compiler_params=pltpu.CompilerParams(vmem_limit_bytes=8 << 20),
        name="store",
    )(betas, hats, residual)
    return betas, hats, residual.reshape(-1)


def solution(mesh):
    split = ("region", "tile")
    in_specs = (
        P(None, split), P(None, split), P(split), P(split), P(split), P(None, split),
        P(None, split, None), P("region", "tile"),
    )
    out_specs = (P(None, split), P(None, split), P(split))
    return jax.shard_map(body, mesh=mesh, in_specs=in_specs, out_specs=out_specs, check_vma=False)
```

```python
import functools
import math

import jax
import jax.numpy as jnp
from jax import lax
from jax.experimental import pallas as pl
from jax.experimental.pallas import tpu as pltpu
from jax.sharding import PartitionSpec as P

TX = 4
LANES = 128
PER = 16
NPIECE = 13
CHUNK = 64
SHARE = (4, 1, 7, 3, 5, 0, 8, 2, 6)
NREGION = 8
NTILE = 32
F32 = jnp.float32
BF16 = jnp.bfloat16


def split3(x):
    hi = x.astype(BF16).astype(F32)
    rest = x - hi
    mid = rest.astype(BF16).astype(F32)
    low = (rest - mid).astype(BF16).astype(F32)
    return hi, mid, low


def wide_split(x):
    hi, mid, low = split3(x)
    return jnp.concatenate([hi.astype(BF16), mid.astype(BF16), low.astype(BF16)], axis=1)


def join3(x):
    return x[:, :LANES] + x[:, LANES : 2 * LANES] + x[:, 2 * LANES :]


def remote(src, dst, send, recv, region, tile):
    return pltpu.make_async_remote_copy(
        src_ref=src,
        dst_ref=dst,
        send_sem=send,
        recv_sem=recv,
        device_id=(region, tile),
        device_id_type=pl.DeviceIdType.MESH,
    )


def signal(sem, region, tile):
    pl.semaphore_signal(sem, inc=1, device_id=(region, tile), device_id_type=pl.DeviceIdType.MESH)


def links(k):
    away = (0, 1, 2, 1)
    return away[k // 2 % 4] + away[k // 8 % 4] + k % 2 / 2


FAR_FIRST = sorted(range(1, NTILE), key=lambda k: -links(k))


def each(low, high, step):
    def turn(index, carry):
        step(index)
        return carry

    lax.fori_loop(low, high, turn, 0)


def walk(tile):
    turned = (tile // 8) * 8 + 6 - lax.rem(tile, 8) + 2 * lax.rem(tile, 2)
    return jnp.where(lax.rem(tile // 8, 2) == 1, turned, tile)


def gather_kernel(
    offsets_in, design_in, target_in, prior_in, counts_in, width_in, reach_in, cells_in,
    data_out, width_out, list_one, list_two, cells_out, home_out,
    offs, design, target, prior, counts, widths, reach, cells, notes, rows_of,
    wanted, stage, rbuf, msg, recv, load, send1, recv1, send2, recv2,
):
    region = lax.axis_index("region")
    tile = lax.axis_index("tile")
    group = tile // 16
    piece = lax.rem(tile, 16)
    up = lax.rem(region + 1, NREGION)
    down = lax.rem(region + NREGION - 1, NREGION)

    barrier = pltpu.get_barrier_semaphore()
    for k in range(15, -1, -1):
        signal(barrier, up, jnp.bitwise_xor(tile, k))
        signal(barrier, down, jnp.bitwise_xor(tile, k))
    for k in FAR_FIRST:
        signal(barrier, region, jnp.bitwise_xor(tile, k))

    loads = [
        pltpu.make_async_copy(source, place, load.at[k])
        for k, (source, place) in enumerate(
            (
                (counts_in, counts), (width_in, widths), (reach_in, reach), (cells_in, cells),
                (offsets_in, offs), (design_in, design), (target_in, target), (prior_in, prior),
            )
        )
    ]
    for copy in loads:
        copy.start()
    notes[...] = jnp.zeros((32, LANES), F32)
    stage[12] = jnp.zeros((24, LANES), F32)
    rows_of[...] = jnp.zeros((48, LANES), F32)
    for copy in loads[:4]:
        copy.wait()
    notes[0:1, 0:PER] = counts[...].astype(F32)
    notes[1:3, 0:PER] = widths[...].astype(F32)
    for e in range(9):
        for w in range(2):
            at = 3 + 9 * w + e
            notes[at : at + 1, 0:PER] = reach[e, w : w + 1, :].astype(F32)
    turned = jnp.transpose(notes[...])[0:PER]
    stage[12, 0:PER, 0:32] = turned
    cell = cells[...]
    order = (lax.bitwise_and(cell, 127) * TX + lax.shift_right_logical(cell, 7)).astype(F32)
    for k in range(8):
        notes[24:25, PER * k : PER * k + PER] = order
    row_lane = lax.broadcasted_iota(jnp.int32, (8, LANES), 1)
    cell_row = jnp.where(
        lax.shift_right_logical(row_lane, 4) == lax.rem(tile, 8),
        jnp.broadcast_to(notes[24:25, :], (8, LANES)), 0.0,
    )
    for p in range(NPIECE):
        stage[p, PER : PER + 8, :] = cell_row
    for copy in loads[4:]:
        copy.wait()
    lane = lax.broadcasted_iota(jnp.int32, (PER, LANES), 1)
    count = turned[:, 0:1]
    for t in range(PER):
        for h in range(2):
            span = slice(LANES * (2 * t + h), LANES * (2 * t + h + 1))
            for f in range(2):
                stage[2 * f + h, t : t + 1, :] = offs[f : f + 1, span]
                stage[4 + 4 * f + h, t : t + 1, :] = design[f : f + 1, span]
    for h in range(2):
        present = ((lane + LANES * h).astype(F32) < count).astype(F32)
        cov_one = stage[4 + h, 0:PER, :] * present
        cov_two = stage[8 + h, 0:PER, :]
        seen = target[pl.ds(h, PER, stride=2), :]
        before = prior[pl.ds(h, PER, stride=2), :]
        stage[4 + h, 0:PER, :] = cov_one
        stage[6 + h, 0:PER, :] = seen - cov_two * before
        cov_two = cov_two * present
        stage[8 + h, 0:PER, :] = cov_two
        stage[10 + h, 0:PER, :] = seen
        home_out[h] = cov_one
        home_out[2 + h] = cov_two
        home_out[4 + h] = seen * present

    pl.semaphore_wait(barrier, NTILE - 1 + 32)

    def to_middle(o):
        other = jnp.bitwise_xor(tile, o)
        held = jnp.minimum(lax.rem(other, 16), NPIECE - 1)
        return remote(
            stage.at[held, pl.ds(0, PER + 1)], rbuf.at[tile, pl.ds(0, PER + 1)],
            send1.at[o], recv1.at[tile], region, other,
        )

    for k in FAR_FIRST:
        to_middle(k).start()
    rbuf[tile] = stage[jnp.minimum(piece, NPIECE - 1)]

    number = lax.broadcasted_iota(jnp.int32, (640, LANES), 0)
    owner = lax.shift_right_logical(number * 205, 13)
    q = number - owner * 40
    turned_owner = 14 - lax.bitwise_and(owner, 7) + 2 * lax.bitwise_and(owner, 1)
    first = (group * 16 + jnp.where(owner < 8, owner, turned_owner)) * 16
    side = jnp.where(q < 32, q - 24, q - 32)
    base = jnp.where(q < 24, q - 4, (side - 1) * 4 + jnp.where(q < 32, 3, 0))
    open_up = jnp.where(region < NREGION - 1, 1, 0)
    open_down = jnp.where(region > 0, 1, 0)
    beside = jnp.where(side < 6, jnp.where(q < 32, open_up, open_down), 0)
    allowed = jnp.where(q < 24, 1, beside)
    cell = first + base
    wanted[...] = jnp.where(allowed > 0, cell, -1).astype(F32)

    def from_source(o):
        other = jnp.bitwise_xor(tile, o)
        return remote(
            stage.at[0, pl.ds(0, PER + 1)], rbuf.at[other, pl.ds(0, PER + 1)],
            send1.at[o], recv1.at[other], region, other,
        )

    each(1, NTILE, lambda o: from_source(o).wait_recv())

    cell_rows = [
        jnp.sum(rbuf[8 * b : 8 * b + 8, PER, :], axis=0, keepdims=True) for b in range(4)
    ]
    for b in range(4):
        cells_out[b : b + 1, :] = cell_rows[b]
    cells_out[4:8, :] = jnp.zeros((4, LANES), F32)

    @pl.when(piece < NPIECE)
    def _():
        spread = wide_split(rbuf[:, 0:PER, :].reshape(NTILE * PER, LANES))
        hot = jnp.concatenate(
            [jnp.where(wanted[...] == cell_rows[b], 1.0, 0.0).astype(BF16) for b in range(4)], axis=1
        )
        moved = join3(jnp.dot(hot, spread, preferred_element_type=F32))
        msg[...] = moved.reshape(16, 40, LANES)

    def own_copy(o):
        i = jnp.bitwise_xor(piece, o)
        return remote(
            msg.at[i, pl.ds(0, 24)], recv.at[piece, pl.ds(0, 24)],
            send2.at[0, o], recv2.at[0, piece], region, group * 16 + i,
        )

    def up_copy(i):
        return remote(
            msg.at[i, pl.ds(24, 8)], recv.at[piece, pl.ds(24, 8)],
            send2.at[1, i], recv2.at[1, piece], up, group * 16 + i,
        )

    def down_copy(i):
        return remote(
            msg.at[i, pl.ds(32, 8)], recv.at[piece, pl.ds(32, 8)],
            send2.at[2, i], recv2.at[2, piece], down, group * 16 + i,
        )

    @pl.when(piece < NPIECE)
    def _():
        for k in sorted(range(16), key=lambda k: -links(k)):
            up_copy(jnp.bitwise_xor(piece, k)).start()
            down_copy(jnp.bitwise_xor(piece, k)).start()
        for k in FAR_FIRST:
            if k < 16:
                own_copy(k).start()
        recv[piece, 0:24, :] = msg[piece, 0:24, :]

    def wait_own(p):
        @pl.when(p != piece)
        def _():
            remote(
                msg.at[0, pl.ds(0, 24)], recv.at[p, pl.ds(0, 24)],
                send2.at[0, 0], recv2.at[0, p], region, group * 16 + p,
            ).wait_recv()

    def wait_sides(p):
        remote(
            msg.at[0, pl.ds(24, 8)], recv.at[p, pl.ds(24, 8)],
            send2.at[1, 0], recv2.at[1, p], down, group * 16 + p,
        ).wait_recv()
        remote(
            msg.at[0, pl.ds(32, 8)], recv.at[p, pl.ds(32, 8)],
            send2.at[2, 0], recv2.at[2, p], up, group * 16 + p,
        ).wait_recv()

    wait_own(12)
    wait_sides(12)
    width_out[...] = recv[12, 4:20, :]
    for r in range(6):
        rows_of[8 * r : 8 * r + 1, :] = recv[12, 24 + r : 25 + r, :]
        rows_of[8 * r + 1 : 8 * r + 5, :] = recv[12, 4 * r : 4 * r + 4, :]
        rows_of[8 * r + 5 : 8 * r + 6, :] = recv[12, 32 + r : 33 + r, :]

    def spread_lane(r, at):
        return jnp.broadcast_to(rows_of[8 * r : 8 * r + 8, at : at + 1], (8, LANES))

    lanes = lax.broadcasted_iota(jnp.int32, (8, LANES), 1)
    spots = lax.bitwise_and(lanes, 31)
    spots_f = spots.astype(F32)
    over = lax.broadcasted_iota(jnp.int32, (8, LANES), 0)
    filled = [spread_lane(r, 0) for r in range(6)]
    near = [
        [filled[r] if a == 1 else pltpu.roll(filled[r], (1 - a) % 8, 0) for a in range(3)]
        for r in range(6)
    ]
    for w, skipped, place in ((0, (), list_one.at[0]), (1, (), list_two.at[0]), (1, SHARE, list_two.at[1])):
        for r in range(1, 5):
            many = jnp.zeros((8, LANES), F32)
            todo = jnp.zeros((8, LANES), F32)
            for e in range(9):
                beside, beyond = e // 3, r + e % 3 - 1
                there = near[beyond][beside]
                keep = None if e == 4 else spread_lane(r, 3 + 9 * w + e)
                c = over + (beside - 1)
                t = jnp.where(c == 0, 24 + beyond, jnp.where(c == 5, 32 + beyond, beyond * 4 + c - 1))
                at = (8 * t).astype(F32)
                for h in range(1 if e in skipped else 0, 2):
                    flag = jnp.where(there > LANES * h, 1.0 if keep is None else keep, 0.0)
                    todo = todo + jnp.where(many == spots_f, flag * (at + 320.0 * h), 0.0)
                    many = many + flag
            chunks = lax.shift_right_logical(filled[r].astype(jnp.int32) + CHUNK - 1, CHUNK.bit_length() - 1)
            value = jnp.where(spots_f < many, todo, 240.0).astype(jnp.int32)
            groups = lax.shift_right_logical((many.astype(jnp.int32) + 2) * 11, 5)
            groups = jnp.maximum(groups, 1)
            value = jnp.where(spots == 24, groups, value)
            value = jnp.where(spots == 25, chunks, value)
            value = jnp.where(spots == 26, filled[r].astype(jnp.int32), value)
            band = value if r == 1 else jnp.where(lax.shift_right_logical(lanes, 5) == r - 1, value, band)
        place[...] = band
    each(0, NPIECE - 1, wait_own)
    each(0, NPIECE - 1, wait_sides)
    for p in range(12):
        data_out[p] = recv[p]

    each(1, NTILE, lambda o: to_middle(o).wait_send())

    @pl.when(piece < NPIECE)
    def _():
        each(1, 16, lambda o: own_copy(o).wait_send())
        each(0, 16, lambda i: up_copy(i).wait_send())
        each(0, 16, lambda i: down_copy(i).wait_send())


def rate_of(which, notes):
    width = notes[:, 1 + which : 2 + which]
    return jnp.broadcast_to((32.0 * math.log2(math.e)) / (width * width), (PER, LANES))


def prepare(which, data, notes, cand, fan, rates):
    rate = rate_of(which, notes)
    rates[0:PER, :] = -rate
    number = lax.broadcasted_iota(jnp.int32, (PER, LANES), 0)
    rates[PER : 2 * PER, :] = (lax.bitwise_and(number, 3) + 1).astype(F32)
    rates[2 * PER : 3 * PER, :] = (lax.shift_right_logical(number, 2) + 1).astype(F32)
    slot = lax.broadcasted_iota(jnp.int32, (40, LANES), 0)
    col = jnp.where(slot < 24, lax.rem(slot, 4) + 1, jnp.where(slot < 32, 0, 5)).astype(F32)
    row = jnp.where(
        slot < 24, slot // 4, jnp.where(slot < 32, slot - 24, slot - 32)
    ).astype(F32)
    columns = []
    for h in range(2):
        x = data[h] - 0.5
        y = data[2 + h] - 0.5
        cov = data[4 + 4 * which + h]
        for k, field in enumerate((x + col, y + row, cov * cov)):
            cand[pl.ds(320 * h + k, 40, stride=8), :] = field
        along, upward = [
            jnp.transpose(jnp.concatenate(split3(2.0 * rate * source), axis=0)).astype(BF16)
            for source in (x[4:20], y[4:20])
        ]
        for low in range(0, LANES, CHUNK):
            columns += [along[low : low + CHUNK], upward[low : low + CHUNK]]
    columns = jnp.concatenate(columns, axis=0)
    which_row = lax.bitwise_and(lax.broadcasted_iota(jnp.int32, (3 * PER, LANES), 0), PER - 1)
    for i in range(PER):
        pick = jnp.where(which_row == i, 1.0, 0.0).astype(BF16)
        fan[4 * LANES * i : 4 * LANES * (i + 1), :] = jnp.dot(
            columns, pick, preferred_element_type=F32
        )


def sums_of(which, cand, pull, fan, rates, lists, weight_sums, pull_sums):
    def listed(kind, i, at):
        band = lax.shift_right_logical(i, 2) * 32
        return lists[kind, lax.bitwise_and(i, 3) + 1, band + at]

    total = jnp.int32(0)
    for i in range(PER):
        r, at = i % 4 + 1, 32 * (i // 4) + 24
        if which == 0:
            total = total + lists[0, r, at] * lists[0, r, at + 1]
        else:
            total = total + lists[1, r, at] + lists[0, r, at] * (lists[0, r, at + 1] - 1)

    shape3 = (CHUNK // 8, 8, LANES)
    spare = PER * 2 * LANES

    def row(ref, at):
        return jnp.broadcast_to(ref[pl.ds(at, 1), :], (8, LANES))

    def rows(ref, at):
        return ref[pl.ds(pl.multiple_of(at, CHUNK), CHUNK), :].reshape(shape3)

    for ref in (weight_sums, pull_sums):
        ref[spare : spare + CHUNK, :] = jnp.zeros((CHUNK, LANES), F32)

    def item(n, carry):
        i, k, j, out, at, groups, chunks, old_from, old_out, old_at, fars, powers = carry
        x = [row(cand, base) - row(rates, PER + i) for base in at]
        y = [row(cand, base + 1) - row(rates, 2 * PER + i) for base in at]
        scale = row(rates, i)
        u = rows(fan, 2 * out)
        v = rows(fan, 2 * out + CHUNK)

        weight_sum = rows(weight_sums, old_from)
        pull_sum = rows(pull_sums, old_from)
        for base, far, power in zip(old_at, fars, powers):
            factor = jnp.exp2(far)
            weight = jnp.exp2(power)
            weight_sum = weight_sum + weight * (factor * row(cand, base + 2))
            pull_sum = pull_sum + weight * (factor * row(pull, lax.shift_right_logical(base, 3)))
        place = pl.ds(pl.multiple_of(old_out, CHUNK), CHUNK)
        weight_sums[place, :] = weight_sum.reshape(CHUNK, LANES)
        pull_sums[place, :] = pull_sum.reshape(CHUNK, LANES)

        fars = tuple((x[g] * x[g] + y[g] * y[g]) * scale for g in range(3))
        powers = tuple(u * x[g] + v * y[g] for g in range(3))
        last = j + 1 == groups
        end = last & (k + 1 == chunks)
        next_j = jnp.where(last, 0, j + 1)
        next_k = jnp.where(end, 0, jnp.where(last, k + 1, k))
        next_i = jnp.minimum(jnp.where(end, i + 1, i), PER - 1)
        next_out = next_i * (2 * LANES) + next_k * CHUNK
        kind = 0 if which == 0 else jnp.where(next_k == 0, 1, 0)
        return (
            next_i, next_k, next_j, next_out,
            tuple(listed(kind, next_i, 3 * next_j + g) for g in range(3)),
            listed(kind, next_i, 24), listed(kind, next_i, 25),
            jnp.where(j == 0, spare, out), out, at, fars, powers,
        )

    zero = rows(fan, 0) * 0.0
    none = row(rates, 0) * 0.0
    begin = jnp.int32(0)
    kind = which
    lax.fori_loop(
        0, total + 1, item,
        (
            begin, begin, begin, begin, tuple(lists[kind, 1, g] for g in range(3)),
            lists[kind, 1, 24], lists[kind, 1, 25],
            jnp.int32(spare), begin, (begin,) * 3, (none,) * 3, (zero,) * 3,
        ),
    )


def first_kernel(data, notes, lists, weight_sums, pull_sums, cand, pull, fan, rates):
    prepare(0, data, notes, cand, fan, rates)
    for h in range(2):
        pull[40 * h : 40 * h + 40, :] = data[4 + h] * data[6 + h]
    sums_of(0, cand, pull, fan, rates, lists, weight_sums, pull_sums)


def second_kernel(cand, pull, fan, rates, lists, weight_sums, pull_sums):
    sums_of(1, cand, pull, fan, rates, lists, weight_sums, pull_sums)


def finish(which, h, data, notes, weight_sums, pull_sums, totals, more=None):
    ones = jnp.ones((8, LANES), BF16)
    for k, ref in enumerate((weight_sums, pull_sums)):
        for i in range(PER):
            at = LANES * (2 * i + h)
            values = ref[at : at + LANES, :]
            if more is not None and h == 0:
                added = values[:CHUNK] + more[k, CHUNK * i : CHUNK * (i + 1), :]
                values = jnp.concatenate([added, values[CHUNK:]], axis=0)
            high = values.astype(BF16)
            low = (values - high.astype(F32)).astype(BF16)
            both = jnp.concatenate([high, low], axis=0)
            sums = lax.dot_general(
                ones, both, (((1,), (1,)), ((), ())), preferred_element_type=F32
            )
            totals[k, i : i + 1, :] = sums[0:1, :LANES] + sums[0:1, LANES:]
    x = data[h, 4:20, :] - 0.5
    y = data[2 + h, 4:20, :] - 0.5
    cov = data[4 + 4 * which + h, 4:20, :]
    fade = jnp.exp2(-rate_of(which, notes) * (x * x + y * y))
    lane = lax.broadcasted_iota(jnp.int32, (PER, LANES), 1)
    live = (lane + LANES * h).astype(F32) < notes[:, 0:1]
    total = 1.0 + fade * totals[0]
    beta = jnp.where(live, fade * totals[1] / total, 0.0)
    return beta, jnp.where(live, cov * cov / total, 0.0)


def edge_cells(a, b):
    cols = range(4) if a == 0 else (0 if a == -1 else 3,)
    rows = range(4) if b == 0 else (0 if b == -1 else 3,)
    return [4 * r + c for r in rows for c in cols]


def share(cand, pull, fan, rates, notes, keeps, more):
    shape3 = (CHUNK // 8, 8, LANES)

    def row(ref, at):
        return jnp.broadcast_to(ref[pl.ds(at, 1), :], (8, LANES))

    def rows(ref, at):
        return ref[pl.ds(pl.multiple_of(at, CHUNK), CHUNK), :].reshape(shape3)

    for e in SHARE:
        kept = jnp.ones((PER, LANES), F32)
        if e != 4:
            kept = jnp.broadcast_to(notes[:, 12 + e : 13 + e], (PER, LANES))
        keeps[PER * e : PER * (e + 1), :] = kept

    def band(r):
        for c in range(4):
            i = 4 * r + c
            u = rows(fan, 4 * LANES * i)
            v = rows(fan, 4 * LANES * i + CHUNK)
            scale = row(rates, i)
            north = row(rates, 2 * PER + i)
            weight_sum = jnp.zeros(shape3, F32)
            pull_sum = jnp.zeros(shape3, F32)
            for e in SHARE:
                col, line = c + e // 3, r + e % 3
                t = 24 + line if col == 0 else 32 + line if col == 5 else 4 * line + col - 1
                x = row(cand, 8 * t) - (c + 1.0)
                y = row(cand, 8 * t + 1) - north
                factor = jnp.exp2((x * x + y * y) * scale) * row(keeps, PER * e + i)
                weight = jnp.exp2(u * x + v * y)
                weight_sum = weight_sum + weight * (factor * row(cand, 8 * t + 2))
                pull_sum = pull_sum + weight * (factor * row(pull, t))
            place = pl.ds(pl.multiple_of(CHUNK * i, CHUNK), CHUNK)
            more[0, place, :] = weight_sum.reshape(CHUNK, LANES)
            more[1, place, :] = pull_sum.reshape(CHUNK, LANES)

    each(0, 4, band)


def halo_kernel(
    weight_sums, pull_sums, data, notes, grid_out, beta_out, hat_out, cand_out, fan_out, rates_out,
    own, edge, totals, recv, send, land,
):
    region = lax.axis_index("region")
    tile = lax.axis_index("tile")
    steps = [(a, b) for a in (-1, 0, 1) for b in (-1, 0, 1) if (a, b) != (0, 0)]

    owner = walk(tile)

    def place(a, b):
        return lax.rem(region + a + NREGION, NREGION), walk(lax.rem(owner + b + NTILE, NTILE))

    barrier = pltpu.get_barrier_semaphore()
    for a, b in steps:
        signal(barrier, *place(a, b))
    for h in range(2):
        beta, hat = finish(0, h, data, notes, weight_sums, pull_sums, totals)
        beta_out[h] = beta
        hat_out[h] = hat
        own[h] = data[8 + h, 4:20, :] * (data[10 + h, 4:20, :] - data[4 + h, 4:20, :] * beta)
    edge[...] = jnp.zeros((8, 8, LANES), F32)
    for k, (a, b) in enumerate(steps):
        for h in range(2):
            for n, i in enumerate(edge_cells(a, b)):
                edge[k, 4 * h + n : 4 * h + n + 1, :] = own[h, i : i + 1, :]
    pl.semaphore_wait(barrier, 8)
    copies = []
    for k, (a, b) in enumerate(steps):
        copies.append(remote(edge.at[k], recv.at[7 - k], send.at[k], land.at[7 - k], *place(a, b)))
    for copy in copies:
        copy.start()
    prepare(1, data, notes, cand_out, fan_out, rates_out)
    for copy in copies:
        copy.wait_recv()
    fits = {-1: region > 0, 0: None, 1: region < NREGION - 1}
    fits_row = {-1: owner > 0, 0: None, 1: owner < NTILE - 1}
    for h in range(2):
        to = 40 * h
        grid_out[to + 4 : to + 20, :] = own[h]
        for first in (to + 30, to + 38):
            grid_out[first : first + 2, :] = jnp.zeros((2, LANES), F32)
        for k, (a, b) in enumerate(steps):
            many = len(edge_cells(-a, -b))
            rows = recv[k, 4 * h : 4 * h + many, :]
            for fit in (fits[a], fits_row[b]):
                if fit is not None:
                    rows = jnp.where(fit, rows, 0.0)
            if a == 0:
                first = to + (0 if b == -1 else 20)
            else:
                first = to + (24 if a == -1 else 32) + (0, 1, 5)[b + 1]
            grid_out[first : first + many, :] = rows
    for copy in copies:
        copy.wait_send()


def return_kernel(
    beta_one, hat_one, weight_sums, pull_sums, data, notes, cells, home, cand, pull, fan, rates,
    betas, hats, residual, keeps, more, totals, stage, rbuf, msg, recv, send1, recv1, send2, recv2,
):
    region = lax.axis_index("region")
    tile = lax.axis_index("tile")
    group = tile // 8
    piece = lax.rem(tile, 8)
    barrier = pltpu.get_barrier_semaphore()
    for k in FAR_FIRST:
        signal(barrier, region, jnp.bitwise_xor(tile, k))
    share(cand, pull, fan, rates, notes, keeps, more)
    for h in range(2):
        stage[h] = beta_one[h]
        stage[2 + h] = hat_one[h]
        stage[4 + h], stage[6 + h] = finish(
            1, h, data, notes, weight_sums, pull_sums, totals, more
        )
    pl.semaphore_wait(barrier, NTILE - 1)

    def to_middle(o):
        other = jnp.bitwise_xor(tile, o)
        return remote(
            stage.at[lax.rem(other, 8)], rbuf.at[tile], send1.at[o], recv1.at[tile], region, other
        )

    for k in FAR_FIRST:
        to_middle(k).start()
    rbuf[tile] = stage[piece]

    row = cells[pl.ds(group, 1), :]
    column = jnp.transpose(jnp.broadcast_to(row, (LANES, LANES)))
    lane = lax.broadcasted_iota(jnp.int32, (LANES, LANES), 1)
    hots = []
    for b in range(4):
        of = lax.shift_right_logical(lane, 4)
        if b % 2 == 1:
            of = 6 - of + 2 * lax.bitwise_and(of, 1)
        here = LANES * b + of * PER + lax.bitwise_and(lane, PER - 1)
        hots.append(jnp.where(here.astype(F32) == column, 1.0, 0.0).astype(BF16))
    hot = jnp.concatenate(hots, axis=1)

    def from_source(o):
        other = jnp.bitwise_xor(tile, o)
        return remote(stage.at[0], rbuf.at[other], send1.at[o], recv1.at[other], region, other)

    each(1, NTILE, lambda o: from_source(o).wait_recv())
    spread = wide_split(rbuf[...].reshape(NTILE * PER, LANES))
    msg[...] = join3(jnp.dot(hot, spread, preferred_element_type=F32)).reshape(8, PER, LANES)

    def home_copy(o):
        i = jnp.bitwise_xor(piece, o)
        return remote(
            msg.at[i], recv.at[piece], send2.at[o], recv2.at[piece], region, group * 8 + i
        )

    for k in FAR_FIRST:
        if k < 8:
            home_copy(k).start()
    recv[piece] = msg[piece]

    def from_middle(o):
        p = jnp.bitwise_xor(piece, o)
        return remote(msg.at[0], recv.at[p], send2.at[o], recv2.at[p], region, group * 8 + p)

    each(1, 8, lambda o: from_middle(o).wait_recv())
    for h in range(2):
        left = home[4 + h] - home[h] * recv[h] - home[2 + h] * recv[4 + h]
        residual[pl.ds(h, PER, stride=2), :] = left
        for t in range(PER):
            span = slice(LANES * (2 * t + h), LANES * (2 * t + h + 1))
            for f in range(2):
                betas[f : f + 1, span] = recv[4 * f + h, t : t + 1, :]
                hats[f : f + 1, span] = recv[2 + 4 * f + h, t : t + 1, :]
    each(1, NTILE, lambda o: to_middle(o).wait_send())
    each(1, 8, lambda o: home_copy(o).wait_send())


def store_kernel(betas, hats, residual, betas_out, hats_out, residual_out, done):
    pairs = ((betas, betas_out), (hats, hats_out), (residual, residual_out))
    copies = [pltpu.make_async_copy(a, b, done.at[k]) for k, (a, b) in enumerate(pairs)]
    for copy in copies:
        copy.start()
    for copy in copies:
        copy.wait()


VM = pl.BlockSpec(memory_space=pltpu.VMEM)
SM = pl.BlockSpec(memory_space=pltpu.SMEM)
HB = pl.BlockSpec(memory_space=pltpu.HBM)
DMA = pltpu.SemaphoreType.DMA


def shape(*dims, dtype=F32):
    return jax.ShapeDtypeStruct(dims, dtype)


def body(offsets, design, target, beta_second, counts, kernel_width, reach, assignment):
    data, notes, list_one, list_two, cells, home = pl.pallas_call(
        gather_kernel,
        out_shape=[
            shape(12, 40, LANES), shape(PER, LANES), shape(1, 8, LANES, dtype=jnp.int32),
            shape(2, 8, LANES, dtype=jnp.int32), shape(8, LANES), shape(6, PER, LANES),
        ],
        in_specs=[HB] * 8,
        out_specs=[VM] * 6,
        scratch_shapes=[
            pltpu.VMEM((2, NTILE * LANES), F32),
            pltpu.VMEM((2, NTILE * LANES), F32),
            pltpu.VMEM((NTILE, LANES), F32),
            pltpu.VMEM((NTILE, LANES), F32),
            pltpu.VMEM((1, PER), jnp.int32),
            pltpu.VMEM((2, PER), jnp.int32),
            pltpu.VMEM((9, 2, PER), jnp.int32),
            pltpu.VMEM((1, PER), jnp.int32),
            pltpu.VMEM((32, LANES), F32),
            pltpu.VMEM((48, LANES), F32),
            pltpu.VMEM((640, LANES), F32),
            pltpu.VMEM((NPIECE, 24, LANES), F32),
            pltpu.VMEM((NTILE, 24, LANES), F32),
            pltpu.VMEM((16, 40, LANES), F32),
            pltpu.VMEM((NPIECE, 40, LANES), F32),
            DMA((8,)),
            DMA((NTILE,)),
            DMA((NTILE,)),
            DMA((3, 16)),
            DMA((3, 16)),
        ],
        compiler_params=pltpu.CompilerParams(collective_id=0, has_side_effects=True, vmem_limit_bytes=8 << 20),
        name="to_owners",
    )(
        *(
            pltpu.with_memory_space_constraint(value, pltpu.HBM)
            for value in (
                offsets, design, target.reshape(NTILE, LANES), beta_second.reshape(NTILE, LANES),
                counts.reshape(1, PER), kernel_width, reach.transpose(2, 0, 1), assignment,
            )
        )
    )
    sums = [shape((PER + 1) * 2 * LANES, LANES)] * 2
    tables = [(640, LANES), (80, LANES), (PER * 4 * LANES, LANES), (3 * PER, LANES)]
    weight_sums, pull_sums = pl.pallas_call(
        first_kernel,
        out_shape=sums,
        in_specs=[VM, VM, SM],
        out_specs=[VM] * 2,
        scratch_shapes=[pltpu.VMEM(dims, F32) for dims in tables],
        compiler_params=pltpu.CompilerParams(vmem_limit_bytes=16 << 20),
        name="smooth_one",
    )(data, notes, list_one)
    grid, beta_one, hat_one, cand, fan, rates = pl.pallas_call(
        halo_kernel,
        out_shape=[
            shape(80, LANES), shape(2, PER, LANES), shape(2, PER, LANES), shape(640, LANES),
            shape(PER * 4 * LANES, LANES), shape(3 * PER, LANES),
        ],
        in_specs=[VM] * 4,
        out_specs=[VM] * 6,
        scratch_shapes=[
            pltpu.VMEM((2, PER, LANES), F32),
            pltpu.VMEM((8, 8, LANES), F32),
            pltpu.VMEM((2, PER, LANES), F32),
            pltpu.VMEM((8, 8, LANES), F32),
            DMA((8,)),
            DMA((8,)),
        ],
        compiler_params=pltpu.CompilerParams(
            collective_id=1, has_side_effects=True, vmem_limit_bytes=16 << 20
        ),
        name="edges",
    )(weight_sums, pull_sums, data, notes)
    weight_sums, pull_sums = pl.pallas_call(
        second_kernel,
        out_shape=sums,
        in_specs=[VM] * 4 + [SM],
        out_specs=[VM] * 2,
        compiler_params=pltpu.CompilerParams(vmem_limit_bytes=16 << 20),
        name="smooth_two",
    )(cand, grid, fan, rates, list_two)
    betas, hats, residual = pl.pallas_call(
        return_kernel,
        out_shape=[shape(2, NTILE * LANES), shape(2, NTILE * LANES), shape(NTILE, LANES)],
        in_specs=[VM] * 12,
        out_specs=[VM] * 3,
        scratch_shapes=[
            pltpu.VMEM((9 * PER, LANES), F32),
            pltpu.VMEM((2, PER * CHUNK, LANES), F32),
            pltpu.VMEM((2, PER, LANES), F32),
            pltpu.VMEM((8, PER, LANES), F32),
            pltpu.VMEM((NTILE, PER, LANES), F32),
            pltpu.VMEM((8, PER, LANES), F32),
            pltpu.VMEM((8, PER, LANES), F32),
            DMA((NTILE,)),
            DMA((NTILE,)),
            DMA((8,)),
            DMA((8,)),
        ],
        compiler_params=pltpu.CompilerParams(collective_id=2, has_side_effects=True, vmem_limit_bytes=16 << 20),
        name="to_slots",
    )(beta_one, hat_one, weight_sums, pull_sums, data, notes, cells, home, cand, grid, fan, rates)
    betas, hats, residual = pl.pallas_call(
        store_kernel,
        out_shape=[shape(2, NTILE * LANES), shape(2, NTILE * LANES), shape(NTILE, LANES)],
        in_specs=[VM] * 3,
        out_specs=[HB] * 3,
        scratch_shapes=[DMA((3,))],
        compiler_params=pltpu.CompilerParams(vmem_limit_bytes=8 << 20),
        name="store",
    )(betas, hats, residual)
    return betas, hats, residual.reshape(-1)


def solution(mesh):
    split = ("region", "tile")
    in_specs = (
        P(None, split), P(None, split), P(split), P(split), P(split), P(None, split),
        P(None, split, None), P("region", "tile"),
    )
    out_specs = (P(None, split), P(None, split), P(split))
    return jax.shard_map(body, mesh=mesh, in_specs=in_specs, out_specs=out_specs, check_vma=False)
```
